32 devices in a mesh: dp: 4 (over z), ctx: 2 (over x), head: 4 (over y, core).
Axes of the slice: x: 2, y: 2, z: 4, core: 2. Of those that a mesh axis runs over, the one named last changes fastest.
Arguments:
- block_in: bfloat16 [4096, 640], P(('dp', 'ctx', 'head')), may hold values from -6 to 6
- cotangent: bfloat16 [4096, 640], P(('dp', 'ctx', 'head')), may hold values from -6 to 6
- positions: int32 [4096], P(('dp', 'ctx')), may hold values from 0 to 1023, as said below
- norm_gains: float32 [4, 640], replicated, may hold values from 0.5 to 1.5
- qk_gains: float32 [2, 256], replicated, may hold values from 0.5 to 1.5
- w_query: bfloat16 [640, 1024], P(None, ('dp', 'ctx', 'head')), may hold values from -0.25 to 0.25
- w_key: bfloat16 [640, 256], P(None, ('dp', 'ctx', 'head')), may hold values from -0.25 to 0.25
- w_value: bfloat16 [640, 256], P(None, ('dp', 'ctx', 'head')), may hold values from -0.25 to 0.25
- w_out: bfloat16 [1024, 640], P(('dp', 'ctx', 'head')), may hold values from -0.75 to 0.75
- w_gate: bfloat16 [640, 2048], P(None, ('dp', 'ctx', 'head')), may hold values from -0.25 to 0.25
- w_up: bfloat16 [640, 2048], P(None, ('dp', 'ctx', 'head')), may hold values from -0.25 to 0.25
- w_down: bfloat16 [2048, 640], P(('dp', 'ctx', 'head')), may hold values from -0.125 to 0.125
Outputs:
- block_out: bfloat16 [4096, 640], P(('dp', 'ctx', 'head'))
- d_block_in: bfloat16 [4096, 640], P(('dp', 'ctx', 'head'))
- grad_norm_gains: float32 [4, 640], replicated
- grad_qk_gains: float32 [2, 256], replicated
- grad_query: float32 [640, 1024], P(None, ('dp', 'ctx', 'head'))
- grad_key: float32 [640, 256], P(None, ('dp', 'ctx', 'head'))
- grad_value: float32 [640, 256], P(None, ('dp', 'ctx', 'head'))
- grad_out: float32 [1024, 640], P(('dp', 'ctx', 'head'))
- grad_gate: float32 [640, 2048], P(None, ('dp', 'ctx', 'head'))
- grad_up: float32 [640, 2048], P(None, ('dp', 'ctx', 'head'))
- grad_down: float32 [2048, 640], P(('dp', 'ctx', 'head'))
The draws below stay inside these ranges and needn't reach their ends.
Inputs may be any that keep to these rules, and one draw needn't show every extreme that they name: Each sequence of 1024 tokens holds one or two documents: positions count from 0 at the sequence's first token and restart from 0 at most once.
All inputs are finite; a program needn't handle non-finite values.
Results may differ from the reference program's by a relative error of at most 0.019.
Values may be sent and summed in bfloat16 or wider, within the bound.
A program may use at most 128 MiB of HBM per device.

```python
import math
import jax
import jax.numpy as jnp
from jax import lax

D = 640
HEADS = 4
HEAD_DIM = 256
FF = 2048
LENGTH = 1024
TOKENS = 4096
KEY_BLOCK = 512


def draw_positions(key, part):
    seq_count = TOKENS // LENGTH
    cut_points = jax.random.randint(key, (seq_count,), LENGTH // 4, 3 * LENGTH // 4 + 1)
    cut_points = jnp.where(jnp.arange(seq_count) == 0, LENGTH, cut_points).astype(jnp.int32)
    ladder = jnp.arange(LENGTH, dtype=jnp.int32)
    placed = jnp.where(ladder[None, :] < cut_points[:, None], ladder[None, :], ladder[None, :] - cut_points[:, None])
    return placed.reshape(TOKENS).astype(jnp.int32)


def levels(own_key, extent, shards, low, largest):
    factor_of = 1.0
    for axis_at, parts in shards:
        draws = jax.random.uniform(jax.random.fold_in(jax.random.fold_in(own_key, 6), axis_at), (parts,), jnp.float32, low / len(shards), largest / len(shards))
        factor_of = factor_of * jnp.repeat(jnp.exp(draws), extent[axis_at] // parts).reshape((-1,) + (1,) * (len(extent) - 1 - axis_at))
    return factor_of


def gaussian(stream_key, shape, scale, limit, cuts=(), held_as=jnp.bfloat16):
    result = scale * jax.random.normal(stream_key, shape, jnp.float32)
    if cuts:
        result = result * levels(stream_key, shape, cuts, -0.22, 0.18)
    return jnp.clip(result, -limit, limit).astype(held_as)


def setup_inputs(seed: int = 0) -> dict:
    keys = jax.random.split(jax.random.key(seed), 13)
    return {
        "block_in": gaussian(keys[0], (TOKENS, D), 1.0, 6.0, ((0, 32),)),
        "cotangent": gaussian(keys[1], (TOKENS, D), 1.0, 6.0, ((0, 32),)),
        "positions": draw_positions(jax.random.fold_in(keys[12], 71), 0),
        "norm_gains": jnp.clip(1.0 + 0.1 * jax.random.normal(keys[3], (4, D), jnp.float32), 0.5, 1.5),
        "qk_gains": jnp.clip(1.0 + 0.1 * jax.random.normal(keys[4], (2, HEAD_DIM), jnp.float32), 0.5, 1.5),
        "w_query": gaussian(keys[5], (D, HEADS * HEAD_DIM), D ** -0.5, 0.25, ((1, 32),)),
        "w_key": gaussian(keys[6], (D, HEAD_DIM), D ** -0.5, 0.25, ((1, 32),)),
        "w_value": gaussian(keys[7], (D, HEAD_DIM), D ** -0.5, 0.25, ((1, 32),)),
        "w_out": gaussian(keys[8], (HEADS * HEAD_DIM, D), (HEADS * HEAD_DIM // 16) ** -0.5, 0.75, ((0, 32),)),
        "w_gate": gaussian(keys[9], (D, FF), D ** -0.5, 0.25, ((1, 32),)),
        "w_up": gaussian(keys[10], (D, FF), D ** -0.5, 0.25, ((1, 32),)),
        "w_down": gaussian(keys[11], (FF, D), FF ** -0.5, 0.125, ((0, 32),)),
    }


epsilon = 1e-06
rope_base = 1000000.0
score_scale = 0.0625
negative_fill = -1e+30

def norm_rows(values, gain_vec):
    inverse = lax.rsqrt(lax.optimization_barrier(jnp.mean(values * values, axis=-1, keepdims=True)) + epsilon)
    return (values * inverse * gain_vec, inverse)

def norm_back(values, inverse, gain_vec, upstream):
    scaled = upstream * gain_vec
    inner_mean = lax.optimization_barrier(jnp.mean(scaled * values, axis=-1, keepdims=True))
    return (inverse * scaled - values * (inverse * inverse * inverse) * inner_mean, upstream * values * inverse)

def rope_angles(positions, full_width):
    ladder = jnp.arange(full_width // 2, dtype=jnp.float32)
    frequency = jnp.exp(ladder * (-2.0 / full_width) * math.log(rope_base))
    angles = positions.astype(jnp.float32)[:, None] * frequency[None, :]
    return (jnp.cos(angles), jnp.sin(angles))

def rotate(values, cosine, sine_part):
    middle = values.shape[-1] // 2
    first_half = values[..., :middle]
    second = values[..., middle:]
    return jnp.concatenate([first_half * cosine - second * sine_part, second * cosine + first_half * sine_part], axis=-1)

def gelu_product(gate_pre, up_pre):
    return jax.nn.gelu(gate_pre, approximate=True) * up_pre

def rounded(values):
    return lax.optimization_barrier(values.astype(jnp.bfloat16)).astype(jnp.float32)

def masked_scores(query_part, keys_wide, query_index, query_pos):
    scores = jnp.einsum('hqd,kd->hqk', query_part, keys_wide)
    key_index = jnp.arange(keys_wide.shape[0], dtype=jnp.int32)
    lowest_key = query_index - query_pos
    visible = (key_index[None, :] <= query_index[:, None]) & (key_index[None, :] >= lowest_key[:, None])
    return jnp.where(visible[None], scores, negative_fill)

def reference(block_in, cotangent, positions, norm_gains, qk_gains, w_query, w_key, w_value, w_out, w_gate, w_up, w_down):
    seq_count = TOKENS // LENGTH
    block_total = LENGTH // KEY_BLOCK

    def one_sequence(totals, seq_items):
        seq_in, seq_cot, seq_pos = seq_items
        input_wide = seq_in.astype(jnp.float32)
        attn_norm, inverse_in = norm_rows(input_wide, norm_gains[0])
        attn_in = attn_norm.astype(jnp.bfloat16)
        query_raw = jnp.dot(attn_in, w_query, preferred_element_type=jnp.float32).reshape(LENGTH, HEADS, HEAD_DIM)
        key_raw = jnp.dot(attn_in, w_key, preferred_element_type=jnp.float32)
        value_rows = jnp.dot(attn_in, w_value, preferred_element_type=jnp.float32).astype(jnp.bfloat16)
        query_normed, inverse_query = norm_rows(query_raw, qk_gains[0])
        key_normed, inverse_key = norm_rows(key_raw, qk_gains[1])
        cosine, sine_part = rope_angles(seq_pos, HEAD_DIM)
        rot_query = (rotate(query_normed, cosine[:, None], sine_part[:, None]) * score_scale).astype(jnp.bfloat16)
        rot_key = rotate(key_normed, cosine, sine_part).astype(jnp.bfloat16)
        head_query = jnp.transpose(rot_query, (1, 0, 2)).astype(jnp.float32)
        keys_wide = rot_key.astype(jnp.float32)
        values_wide = value_rows.astype(jnp.float32)
        all_index = jnp.arange(LENGTH, dtype=jnp.int32)
        total_blocks = []
        exact_blocks = []
        for block_index in range(block_total):
            row_start = block_index * KEY_BLOCK
            finish = row_start + KEY_BLOCK
            scores = masked_scores(head_query[:, row_start:finish], keys_wide[:finish], all_index[row_start:finish], seq_pos[row_start:finish])
            row_top = lax.optimization_barrier(jnp.max(scores, axis=-1, keepdims=True))
            log_total = row_top + jnp.log(lax.optimization_barrier(jnp.sum(jnp.exp(scores - row_top), axis=-1, keepdims=True)))
            prob_rows = rounded(jnp.exp(scores - log_total))
            total_blocks.append(log_total)
            exact_blocks.append(jnp.einsum('hqk,kd->hqd', prob_rows, values_wide[:finish]))
        attn_exact = jnp.concatenate(exact_blocks, axis=1)
        attn_out = jnp.transpose(attn_exact, (1, 0, 2)).astype(jnp.bfloat16).reshape(LENGTH, HEADS * HEAD_DIM)
        branch = jnp.dot(attn_out, w_out, preferred_element_type=jnp.float32)
        branch_normed, inverse_branch = norm_rows(branch, norm_gains[1])
        middle = input_wide + branch_normed
        mlp_norm, inverse_mid = norm_rows(middle, norm_gains[2])
        mlp_in = mlp_norm.astype(jnp.bfloat16)
        gate_pre = jnp.dot(mlp_in, w_gate, preferred_element_type=jnp.float32)
        up_pre = jnp.dot(mlp_in, w_up, preferred_element_type=jnp.float32)
        hidden = gelu_product(gate_pre, up_pre).astype(jnp.bfloat16)
        down_raw = jnp.dot(hidden, w_down, preferred_element_type=jnp.float32)
        down_normed, inverse_down = norm_rows(down_raw, norm_gains[3])
        block_out = (middle + down_normed).astype(jnp.bfloat16)
        cot_wide = seq_cot.astype(jnp.float32)
        grad_down_raw, gain_three = norm_back(down_raw, inverse_down, norm_gains[3], cot_wide)
        grad_down_in = grad_down_raw.astype(jnp.bfloat16)
        grad_down = jnp.dot(hidden.T, grad_down_in, preferred_element_type=jnp.float32)
        grad_hidden = jnp.dot(grad_down_in, w_down.T, preferred_element_type=jnp.float32)
        _, gelu_pull = jax.vjp(gelu_product, gate_pre, up_pre)
        grad_gate_raw, grad_up_raw = gelu_pull(grad_hidden)
        grad_gate_in = grad_gate_raw.astype(jnp.bfloat16)
        grad_up_in = grad_up_raw.astype(jnp.bfloat16)
        grad_gate = jnp.dot(mlp_in.T, grad_gate_in, preferred_element_type=jnp.float32)
        grad_up = jnp.dot(mlp_in.T, grad_up_in, preferred_element_type=jnp.float32)
        grad_mlp_in = jnp.dot(grad_gate_in, w_gate.T, preferred_element_type=jnp.float32) + jnp.dot(grad_up_in, w_up.T, preferred_element_type=jnp.float32)
        grad_mid_part, gain_two = norm_back(middle, inverse_mid, norm_gains[2], grad_mlp_in)
        grad_middle = cot_wide + grad_mid_part
        grad_branch_raw, gain_one = norm_back(branch, inverse_branch, norm_gains[1], grad_middle)
        grad_branch = grad_branch_raw.astype(jnp.bfloat16)
        grad_out = jnp.dot(attn_out.T, grad_branch, preferred_element_type=jnp.float32)
        grad_attn = jnp.dot(grad_branch, w_out.T, preferred_element_type=jnp.float32).astype(jnp.bfloat16)
        head_grad = jnp.transpose(grad_attn.reshape(LENGTH, HEADS, HEAD_DIM), (1, 0, 2)).astype(jnp.float32)
        key_sums = jnp.zeros((LENGTH, HEAD_DIM), jnp.float32)
        value_sums = jnp.zeros((LENGTH, HEAD_DIM), jnp.float32)
        query_blocks = []
        for block_index in range(block_total):
            row_start = block_index * KEY_BLOCK
            finish = row_start + KEY_BLOCK
            query_part = head_query[:, row_start:finish]
            scores = masked_scores(query_part, keys_wide[:finish], all_index[row_start:finish], seq_pos[row_start:finish])
            probs_wide = jnp.exp(scores - total_blocks[block_index])
            grad_part = head_grad[:, row_start:finish]
            row_delta = lax.optimization_barrier(jnp.sum(grad_part * exact_blocks[block_index], axis=-1, keepdims=True))
            value_sums = value_sums.at[:finish].add(jnp.einsum('hqk,hqd->kd', rounded(probs_wide), grad_part))
            grad_probs = jnp.einsum('hqd,kd->hqk', grad_part, values_wide[:finish])
            grad_scores = rounded(probs_wide * (grad_probs - row_delta))
            query_blocks.append(jnp.einsum('hqk,kd->hqd', grad_scores, keys_wide[:finish]))
            key_sums = key_sums.at[:finish].add(jnp.einsum('hqk,hqd->kd', grad_scores, query_part))
        grad_rot_query = jnp.transpose(jnp.concatenate(query_blocks, axis=1), (1, 0, 2))
        query_back = rotate(grad_rot_query * score_scale, cosine[:, None], -sine_part[:, None])
        grad_query_raw, gain_query = norm_back(query_raw, inverse_query, qk_gains[0], query_back)
        key_back = rotate(key_sums, cosine, -sine_part)
        grad_key_raw, gain_key = norm_back(key_raw, inverse_key, qk_gains[1], key_back)
        grad_query_in = grad_query_raw.reshape(LENGTH, HEADS * HEAD_DIM).astype(jnp.bfloat16)
        grad_key_in = grad_key_raw.astype(jnp.bfloat16)
        grad_value_in = value_sums.astype(jnp.bfloat16)
        grad_query = jnp.dot(attn_in.T, grad_query_in, preferred_element_type=jnp.float32)
        grad_key = jnp.dot(attn_in.T, grad_key_in, preferred_element_type=jnp.float32)
        grad_value = jnp.dot(attn_in.T, grad_value_in, preferred_element_type=jnp.float32)
        grad_attn_in = jnp.dot(grad_query_in, w_query.T, preferred_element_type=jnp.float32)
        grad_attn_in = grad_attn_in + jnp.dot(grad_key_in, w_key.T, preferred_element_type=jnp.float32)
        grad_attn_in = grad_attn_in + jnp.dot(grad_value_in, w_value.T, preferred_element_type=jnp.float32)
        grad_in_part, gain_zero = norm_back(input_wide, inverse_in, norm_gains[0], grad_attn_in)
        d_block_in = (grad_middle + grad_in_part).astype(jnp.bfloat16)
        gain_terms = jnp.stack([lax.optimization_barrier(jnp.sum(gain_zero, axis=0)), lax.optimization_barrier(jnp.sum(gain_one, axis=0)), lax.optimization_barrier(jnp.sum(gain_two, axis=0)), lax.optimization_barrier(jnp.sum(gain_three, axis=0))])
        qk_terms = jnp.stack([lax.optimization_barrier(jnp.sum(gain_query, axis=(0, 1))), lax.optimization_barrier(jnp.sum(gain_key, axis=0))])
        fresh = (gain_terms, qk_terms, grad_query, grad_key, grad_value, grad_out, grad_gate, grad_up, grad_down)
        return (jax.tree.map(lambda older, newer: older + newer, totals, fresh), (block_out, d_block_in))
    starting = (jnp.zeros((4, D), jnp.float32), jnp.zeros((2, HEAD_DIM), jnp.float32), jnp.zeros((D, HEADS * HEAD_DIM), jnp.float32), jnp.zeros((D, HEAD_DIM), jnp.float32), jnp.zeros((D, HEAD_DIM), jnp.float32), jnp.zeros((HEADS * HEAD_DIM, D), jnp.float32), jnp.zeros((D, FF), jnp.float32), jnp.zeros((D, FF), jnp.float32), jnp.zeros((FF, D), jnp.float32))
    totals, (outs_seq, grads_seq) = lax.scan(one_sequence, starting, (block_in.reshape(seq_count, LENGTH, D), cotangent.reshape(seq_count, LENGTH, D), positions.reshape(seq_count, LENGTH)))
    return (outs_seq.reshape(TOKENS, D), grads_seq.reshape(TOKENS, D), totals[0], totals[1], totals[2], totals[3], totals[4], totals[5], totals[6], totals[7], totals[8])
```

```python
import math
import types

import jax
import jax.numpy as jnp
from jax import lax
from jax.experimental import pallas as pl
from jax.experimental.pallas import tpu as pltpu
from jax.sharding import PartitionSpec as P

epsilon = 1e-06
rope_base = 1000000.0
score_scale = 0.0625
negative_fill = -1e30


def norm_rows(values, gain_vec):
    inverse = lax.rsqrt(jnp.mean(values * values, axis=-1, keepdims=True) + epsilon)
    return (values * inverse * gain_vec, inverse)


def norm_back(values, inverse, gain_vec, upstream):
    scaled = upstream * gain_vec
    inner_mean = jnp.mean(scaled * values, axis=-1, keepdims=True)
    return (
        inverse * scaled - values * (inverse * inverse * inverse) * inner_mean,
        upstream * values * inverse,
    )


def rope_angles(positions, full_width):
    ladder = jnp.arange(full_width // 2, dtype=jnp.float32)
    frequency = jnp.exp(ladder * (-2.0 / full_width) * math.log(rope_base))
    angles = positions.astype(jnp.float32)[:, None] * frequency[None, :]
    return (jnp.cos(angles), jnp.sin(angles))


def rotate(values, cosine, sine_part):
    middle = values.shape[-1] // 2
    first_half = values[..., :middle]
    second = values[..., middle:]
    return jnp.concatenate(
        [first_half * cosine - second * sine_part, second * cosine + first_half * sine_part],
        axis=-1,
    )


def gelu_product(gate_pre, up_pre):
    return jax.nn.gelu(gate_pre, approximate=True) * up_pre


every_axis = ("dp", "ctx", "head")
sequence_axes = ("ctx", "head")
weight_axes = ("dp", "ctx")


def place_in(axes):
    place = 0
    for name in axes:
        place = place * lax.axis_size(name) + lax.axis_index(name)
    return place


def coordinates(axes, place):
    found = {}
    for name in reversed(axes):
        size = lax.axis_size(name)
        found[name] = lax.rem(place, size)
        place = place // size
    return found


def each_peer(count, step):
    if count <= 8:
        for offset in range(1, count):
            step(offset)
    else:

        def looped(offset, carry):
            step(offset)
            return carry

        lax.fori_loop(1, count, looped, 0)


def exchange_kernel(kinds, greet, counts, *refs):
    total = len(kinds)
    sources, targets, sems = refs[:total], refs[total : 2 * total], refs[2 * total :]
    barrier = pltpu.get_barrier_semaphore()
    waits = 0
    for axes, count in greet:
        me = place_in(axes)

        def greet_peer(offset, axes=axes, count=count, me=me):
            pl.semaphore_signal(
                barrier,
                inc=1,
                device_id=coordinates(axes, lax.rem(me + offset, count)),
                device_id_type=pl.DeviceIdType.MESH,
            )

        each_peer(count, greet_peer)
        waits += count - 1
    locals_started = []
    for part, (kind, axes) in enumerate(kinds):
        me = place_in(axes)
        source = {"scatter": me, "relative": 0}.get(kind)
        source = sources[part] if source is None else sources[part].at[source]
        copy = pltpu.make_async_copy(source, targets[part].at[me], sems[3 * part + 2].at[0])
        copy.start()
        locals_started.append(copy)
    pl.semaphore_wait(barrier, waits)

    def descriptor(part, offset, backward):
        kind, axes = kinds[part]
        count = counts[part]
        me = place_in(axes)
        to = lax.rem(me + offset, count)
        origin = lax.rem(me + count - offset, count) if backward else me
        source = {"scatter": to, "relative": lax.rem(count - offset, count)}.get(kind)
        source = sources[part] if source is None else sources[part].at[source]
        return pltpu.make_async_remote_copy(
            src_ref=source,
            dst_ref=targets[part].at[origin],
            send_sem=sems[3 * part].at[offset],
            recv_sem=sems[3 * part + 1].at[origin],
            device_id=coordinates(axes, to),
            device_id_type=pl.DeviceIdType.MESH,
        )

    for part in range(total):
        each_peer(counts[part], lambda offset: descriptor(part, offset, False).start())
    for copy in locals_started:
        copy.wait()
    for part in range(total):
        each_peer(counts[part], lambda offset: descriptor(part, offset, True).wait_recv())
    for part in range(total):
        each_peer(counts[part], lambda offset: descriptor(part, offset, False).wait_send())


def exchange(call_id, name, parts, greet_axes=None):
    kinds = tuple((kind, axes) for kind, axes, _ in parts)
    arrays = [array for _, _, array in parts]
    counts = tuple(lax.axis_size(axes) for _, axes in kinds)
    if greet_axes is None:
        greet_axes = (kinds[0][1],)
    greet = tuple((axes, lax.axis_size(axes)) for axes in greet_axes)
    shapes = [
        jax.ShapeDtypeStruct(
            (count,) + array.shape if kind == "gather" else array.shape, array.dtype
        )
        for (kind, _, array), count in zip(parts, counts)
    ]
    scratch = []
    for count in counts:
        scratch += [
            pltpu.SemaphoreType.DMA((count,)),
            pltpu.SemaphoreType.DMA((count,)),
            pltpu.SemaphoreType.DMA((1,)),
        ]
    in_vmem = pl.BlockSpec(memory_space=pltpu.VMEM)
    return pl.pallas_call(
        lambda *refs: exchange_kernel(kinds, greet, counts, *refs),
        out_shape=shapes,
        in_specs=[in_vmem] * len(arrays),
        out_specs=[in_vmem] * len(arrays),
        scratch_shapes=scratch,
        compiler_params=pltpu.CompilerParams(collective_id=call_id, has_side_effects=True),
        name=name,
    )(*arrays)


def digit_place(digit):
    if digit == "head_slow":
        return lax.axis_index("head") // fast_size()
    if digit == "head_fast":
        return lax.rem(lax.axis_index("head"), fast_size())
    return lax.axis_index(digit)


def fast_size():
    return 2 if lax.axis_size("head") % 2 == 0 else 1


def digit_size(digit):
    if digit == "head_slow":
        return lax.axis_size("head") // fast_size()
    if digit == "head_fast":
        return fast_size()
    return lax.axis_size(digit)


def digit_device(digit, value):
    if digit == "head_slow":
        return {"head": value * fast_size() + digit_place("head_fast")}
    if digit == "head_fast":
        return {"head": digit_place("head_slow") * fast_size() + value}
    return {digit: value}


def staged_kernel(plans, greeted, *refs):
    total = len(plans)
    sources, targets, sems = refs[:total], refs[total : 2 * total], list(refs[2 * total :])
    barrier = pltpu.get_barrier_semaphore()
    waits = 0
    for digit in greeted:
        count, me = digit_size(digit), digit_place(digit)
        for offset in range(1, count):
            pl.semaphore_signal(
                barrier,
                inc=1,
                device_id=digit_device(digit, lax.rem(me + offset, count)),
                device_id_type=pl.DeviceIdType.MESH,
            )
            waits += 1
    local_sems = sems[:total]
    rest = sems[total:]
    pairs = []
    for plan in plans:
        pairs.append([(rest.pop(0), rest.pop(0)) for _ in plan])
    own = []
    for part, plan in enumerate(plans):
        here = tuple(digit_place(digit) for digit in reversed(plan))
        copy = pltpu.make_async_copy(sources[part], targets[part].at[here], local_sems[part].at[0])
        copy.start()
        own.append(copy)
    pl.semaphore_wait(barrier, waits)

    def descriptors(part, turn, backward):
        plan = plans[part]
        digit = plan[turn]
        count, me = digit_size(digit), digit_place(digit)
        outer = tuple(digit_place(name) for name in reversed(plan[turn + 1 :]))
        found = []
        for offset in range(1, count):
            to = lax.rem(me + offset, count)
            origin = lax.rem(me + count - offset, count) if backward else me
            source = sources[part] if turn == 0 else targets[part].at[outer + (me,)]
            found.append(
                pltpu.make_async_remote_copy(
                    src_ref=source,
                    dst_ref=targets[part].at[outer + (origin,)],
                    send_sem=pairs[part][turn][0].at[offset],
                    recv_sem=pairs[part][turn][1].at[origin],
                    device_id=digit_device(digit, to),
                    device_id_type=pl.DeviceIdType.MESH,
                )
            )
        return found

    most = max(len(plan) for plan in plans)
    for turn in range(most + 1):
        for part, plan in enumerate(plans):
            if 0 < turn <= len(plan):
                for copy in descriptors(part, turn - 1, True):
                    copy.wait_recv()
            if turn == 1:
                own[part].wait()
            if turn < len(plan):
                for copy in descriptors(part, turn, False):
                    copy.start()
    for part, plan in enumerate(plans):
        for turn in range(len(plan)):
            for copy in descriptors(part, turn, False):
                copy.wait_send()


def staged_gather(call_id, name, parts):
    plans = [plan for plan, _ in parts]
    arrays = [array for _, array in parts]
    greeted = []
    for plan in plans:
        greeted += [digit for digit in plan if digit not in greeted]
    shapes = [
        jax.ShapeDtypeStruct(
            tuple(digit_size(digit) for digit in reversed(plan)) + array.shape, array.dtype
        )
        for plan, array in parts
    ]
    scratch = [pltpu.SemaphoreType.DMA((1,)) for _ in parts]
    for plan in plans:
        for digit in plan:
            scratch += [pltpu.SemaphoreType.DMA((digit_size(digit),))] * 2
    in_vmem = pl.BlockSpec(memory_space=pltpu.VMEM)
    return pl.pallas_call(
        lambda *refs: staged_kernel(plans, greeted, *refs),
        out_shape=shapes,
        in_specs=[in_vmem] * len(arrays),
        out_specs=[in_vmem] * len(arrays),
        scratch_shapes=scratch,
        compiler_params=pltpu.CompilerParams(collective_id=call_id, has_side_effects=True),
        name=name,
    )(*arrays)


def gather_rows(call_id, name, rows):
    (blocks,) = exchange(call_id, name, [("gather", ("head",), rows)])
    return blocks.reshape(-1, rows.shape[1])


def shifted(array, axis, offset):
    count = lax.axis_size(axis)
    return lax.ppermute(array, axis, [(here, (here + offset) % count) for here in range(count)])


def gelu_parts(value):
    root = math.sqrt(2.0 / math.pi)
    square = value * value
    tanh_part = jnp.tanh(root * (value + 0.044715 * value * square))
    gelu = 0.5 * value * (1.0 + tanh_part)
    slope = 0.5 * (1.0 + tanh_part) + 0.5 * value * (1.0 - tanh_part * tanh_part) * root * (
        1.0 + 3.0 * 0.044715 * square
    )
    return gelu, slope


def mlp_forward_kernel(rows_ref, gate_ref, up_ref, down_ref, gate_pre_ref, up_pre_ref, hidden_ref, part_ref):
    rows = rows_ref[...]
    gate_pre = rows_dot(rows, gate_ref[...], 1, 1)
    up_pre = rows_dot(rows, up_ref[...], 1, 1)
    gate_pre_ref[...] = gate_pre
    up_pre_ref[...] = up_pre
    hidden = (gelu_parts(gate_pre)[0] * up_pre).astype(jnp.bfloat16)
    hidden_ref[...] = hidden
    part_ref[...] = rows_dot(hidden, down_ref[...], 1, 0).astype(jnp.bfloat16)


def mlp_backward_kernel(
    rows_ref, gate_ref, up_ref, down_ref, gate_pre_ref, up_pre_ref, grad_gate_ref, grad_up_ref, part_ref
):
    grad_hidden = rows_dot(rows_ref[...], down_ref[...], 1, 1)
    gelu, slope = gelu_parts(gate_pre_ref[...])
    grad_gate = (grad_hidden * up_pre_ref[...] * slope).astype(jnp.bfloat16)
    grad_up = (grad_hidden * gelu).astype(jnp.bfloat16)
    grad_gate_ref[...] = grad_gate
    grad_up_ref[...] = grad_up
    part_ref[...] = (
        rows_dot(grad_gate, gate_ref[...], 1, 0) + rows_dot(grad_up, up_ref[...], 1, 0)
    ).astype(jnp.bfloat16)


def rows_dot(left, right, left_dim, right_dim):
    return lax.dot_general(
        left, right, (((left_dim,), (right_dim,)), ((), ())), preferred_element_type=jnp.float32
    )


def add_up(blocks):
    return jnp.sum(blocks.astype(jnp.float32), axis=0)


def local(
    block_in,
    cotangent,
    positions,
    norm_gains,
    qk_gains,
    w_query,
    w_key,
    w_value,
    w_out,
    w_gate,
    w_up,
    w_down,
):
    tok_rows, model_width = block_in.shape
    head_count = lax.axis_size("head")
    head_width = qk_gains.shape[1]
    ctx_slot = lax.axis_index("ctx")
    query_rows = head_count * tok_rows
    group_count = lax.axis_size(weight_axes)
    every_count = lax.axis_size(every_axis)
    length_all = lax.axis_size(sequence_axes) * tok_rows
    query_cols = w_query.shape[1]
    key_cols = w_key.shape[1]
    ff_cols = w_gate.shape[1]
    narrow = jnp.bfloat16

    ff_rows = jnp.concatenate([w_gate.T, w_up.T, w_down], axis=0)
    dp_count, ctx_count = lax.axis_size("dp"), lax.axis_size("ctx")

    to_heads = [
        (head * group_count + index, index * head_count + head)
        for head in range(head_count)
        for index in range(group_count)
    ]
    to_owners = [(there, here) for here, there in to_heads]
    head_rows = lax.ppermute(
        jnp.concatenate([w_query.T, w_out], axis=0), every_axis, to_heads
    )
    key_value_rows = jnp.concatenate([w_key.T, w_value.T], axis=0)
    block_all, key_value_all, head_all, position_all = staged_gather(
        1,
        "first_gather",
        [
            (("ctx", "head_slow", "head_fast"), block_in),
            (("dp", "ctx", "head_slow", "head_fast"), key_value_rows),
            (("dp", "ctx"), head_rows),
            (("ctx",), positions.reshape(-1, 128)),
        ],
    )
    block_all, ff_rows = lax.optimization_barrier((block_all, ff_rows))
    near_blocks = [ff_rows] + [shifted(ff_rows, "dp", offset) for offset in range(1, dp_count)]
    ff_across = [shifted(ff_rows, "ctx", offset) for offset in range(1, ctx_count)]
    block_all = block_all.transpose(2, 1, 0, 3, 4)
    key_value_all = key_value_all.transpose(3, 2, 1, 0, 4, 5).reshape(
        every_count, 2 * key_cols, model_width
    )
    head_all = head_all.transpose(1, 0, 2, 3).reshape(group_count, 2 * query_cols, model_width)
    query_weight = head_all[:, :query_cols].reshape(head_width, model_width)
    out_weight = head_all[:, query_cols:].reshape(head_width, model_width)
    key_weight = key_value_all[:, :key_cols].reshape(head_width, model_width)
    value_weight = key_value_all[:, key_cols:].reshape(head_width, model_width)

    input_all = block_all.reshape(length_all, model_width).astype(jnp.float32)
    attn_in_all = norm_rows(input_all, norm_gains[0])[0].astype(narrow)
    first_query = ctx_slot * query_rows
    attn_in = lax.dynamic_slice_in_dim(attn_in_all, first_query, query_rows)
    query_raw = rows_dot(attn_in, query_weight, 1, 1)
    key_raw = rows_dot(attn_in_all, key_weight, 1, 1)
    all_values = rows_dot(attn_in_all, value_weight, 1, 1).astype(narrow)
    query_normed, inverse_query = norm_rows(query_raw, qk_gains[0])
    key_normed, inverse_key = norm_rows(key_raw, qk_gains[1])
    cosine, sine_part = rope_angles(position_all.reshape(length_all), head_width)
    cosine_own = lax.dynamic_slice_in_dim(cosine, first_query, query_rows)
    sine_own = lax.dynamic_slice_in_dim(sine_part, first_query, query_rows)
    head_query = (rotate(query_normed, cosine_own, sine_own) * score_scale).astype(narrow)
    all_keys = rotate(key_normed, cosine, sine_part).astype(narrow)

    query_index = first_query + jnp.arange(query_rows, dtype=jnp.int32)
    lowest_key = query_index - positions
    key_index = jnp.arange(length_all, dtype=jnp.int32)
    visible = (key_index[None, :] <= query_index[:, None]) & (
        key_index[None, :] >= lowest_key[:, None]
    )
    scores = jnp.where(visible, rows_dot(head_query, all_keys, 1, 1), negative_fill)
    top = jnp.max(scores, axis=1, keepdims=True)
    log_total = top + jnp.log(jnp.sum(jnp.exp(scores - top), axis=1, keepdims=True))
    probs_wide = jnp.exp(scores - log_total)
    prob_rows = probs_wide.astype(narrow)
    attn_exact = rows_dot(prob_rows, all_values, 1, 0)
    attn_out = attn_exact.astype(narrow)
    branch_part = rows_dot(attn_out, out_weight, 1, 0).astype(narrow)
    (branch_blocks,) = exchange(
        2,
        "branch_scatter",
        [("scatter", ("head",), branch_part.reshape(head_count, tok_rows, model_width))],
    )
    branch = add_up(branch_blocks)
    input_wide = block_in.astype(jnp.float32)
    inverse_in = norm_rows(input_wide, norm_gains[0])[1]
    branch_normed, inverse_branch = norm_rows(branch, norm_gains[1])
    middle = input_wide + branch_normed
    mlp_norm, inverse_mid = norm_rows(middle, norm_gains[2])
    mlp_norm, near_blocks, ff_across = lax.optimization_barrier((mlp_norm, near_blocks, ff_across))
    ff_slots = list(near_blocks)
    for offset in range(1, ctx_count):
        ff_slots += [ff_across[offset - 1]]
        ff_slots += [shifted(block, "ctx", offset) for block in near_blocks[1:]]
    mlp_in = gather_rows(3, "mlp_gather", mlp_norm.astype(narrow))

    ff_width = group_count * ff_cols
    gate_weight = jnp.concatenate([block[:ff_cols] for block in ff_slots], axis=0)
    up_weight = jnp.concatenate([block[ff_cols : 2 * ff_cols] for block in ff_slots], axis=0)
    down_weight = jnp.concatenate([block[2 * ff_cols :] for block in ff_slots], axis=0)
    wide_ff = jax.ShapeDtypeStruct((query_rows, ff_width), jnp.float32)
    narrow_ff = jax.ShapeDtypeStruct((query_rows, ff_width), narrow)
    narrow_rows = jax.ShapeDtypeStruct((query_rows, model_width), narrow)
    gate_pre, up_pre, hidden, down_part = pl.pallas_call(
        mlp_forward_kernel,
        out_shape=[wide_ff, wide_ff, narrow_ff, narrow_rows],
        name="mlp_forward",
    )(mlp_in, gate_weight, up_weight, down_weight)
    (down_blocks,) = exchange(
        4,
        "down_scatter",
        [("scatter", ("head",), down_part.reshape(head_count, tok_rows, model_width))],
    )
    down_raw = add_up(down_blocks)
    down_normed, inverse_down = norm_rows(down_raw, norm_gains[3])
    block_out = (middle + down_normed).astype(narrow)
    cot_wide = cotangent.astype(jnp.float32)
    grad_down_raw, gain_three = norm_back(down_raw, inverse_down, norm_gains[3], cot_wide)
    grad_down_in = gather_rows(5, "grad_down_gather", grad_down_raw.astype(narrow))
    grad_gate_in, grad_up_in, grad_mlp_part = pl.pallas_call(
        mlp_backward_kernel,
        out_shape=[narrow_ff, narrow_ff, narrow_rows],
        name="mlp_backward",
    )(grad_down_in, gate_weight, up_weight, down_weight, gate_pre, up_pre)
    slots = (ctx_count, dp_count, ff_cols, model_width)
    ff_terms = jnp.concatenate(
        [
            rows_dot(grad_gate_in, mlp_in, 0, 0).astype(narrow).reshape(slots),
            rows_dot(grad_up_in, mlp_in, 0, 0).astype(narrow).reshape(slots),
            rows_dot(hidden, grad_down_in, 0, 0).astype(narrow).reshape(slots),
        ],
        axis=2,
    )
    half = dp_count // 2
    grad_mlp_blocks, ff_early = exchange(
        6,
        "grad_mlp_scatter",
        [
            (
                "scatter",
                ("head",),
                grad_mlp_part.reshape(head_count, tok_rows, model_width),
            ),
            ("relative", ("ctx",), ff_terms[:, :half]),
        ],
        (("head",), ("ctx",)),
    )
    grad_mlp_in = add_up(grad_mlp_blocks)
    grad_mid_part, gain_two = norm_back(middle, inverse_mid, norm_gains[2], grad_mlp_in)
    grad_middle = cot_wide + grad_mid_part
    grad_branch_raw, gain_one = norm_back(branch, inverse_branch, norm_gains[1], grad_middle)
    grad_branch_blocks, ff_late = exchange(
        7,
        "grad_branch_gather",
        [
            ("gather", ("head",), grad_branch_raw.astype(narrow)),
            ("relative", ("ctx",), ff_terms[:, half:]),
        ],
        (("head",), ("ctx",)),
    )
    grad_branch = grad_branch_blocks.reshape(query_rows, model_width)
    ff_sums = jnp.concatenate([add_up(ff_early), add_up(ff_late)], axis=0).astype(narrow)
    head_grad = rows_dot(grad_branch, out_weight, 1, 1).astype(narrow)
    row_delta = jnp.sum(head_grad.astype(jnp.float32) * attn_exact, axis=1, keepdims=True)
    grad_probs = rows_dot(head_grad, all_values, 1, 1)
    grad_scores = (probs_wide * (grad_probs - row_delta)).astype(narrow)
    value_sums = rows_dot(prob_rows, head_grad, 0, 0)
    key_sums = rows_dot(grad_scores, head_query, 0, 0)
    grad_rot_query = rows_dot(grad_scores, all_keys, 1, 0)
    query_back = rotate(grad_rot_query * score_scale, cosine_own, -sine_own)
    grad_query_raw, gain_query = norm_back(query_raw, inverse_query, qk_gains[0], query_back)
    key_back = rotate(key_sums, cosine, -sine_part)
    grad_key_raw, gain_key = norm_back(key_raw, inverse_key, qk_gains[1], key_back)
    grad_query_in = grad_query_raw.astype(narrow)
    grad_key_in = grad_key_raw.astype(narrow)
    grad_value_in = value_sums.astype(narrow)
    grad_attn_part = rows_dot(grad_key_in, key_weight, 1, 0) + rows_dot(
        grad_value_in, value_weight, 1, 0
    )
    own_part = lax.dynamic_slice_in_dim(grad_attn_part, first_query, query_rows) + rows_dot(
        grad_query_in, query_weight, 1, 0
    )
    grad_attn_part = lax.dynamic_update_slice_in_dim(grad_attn_part, own_part, first_query, 0)
    head_terms = jnp.concatenate(
        [
            rows_dot(grad_query_in, attn_in, 0, 0).reshape(group_count, query_cols, model_width),
            rows_dot(attn_out, grad_branch, 0, 0).reshape(group_count, query_cols, model_width),
        ],
        axis=1,
    ).astype(narrow)
    planes = (dp_count, every_count // dp_count, key_cols, model_width)
    key_value_terms = jnp.concatenate(
        [
            rows_dot(grad_key_in, attn_in_all, 0, 0).reshape(planes),
            rows_dot(grad_value_in, attn_in_all, 0, 0).reshape(planes),
        ],
        axis=2,
    ).astype(narrow).transpose(1, 0, 2, 3)
    head_terms = head_terms.reshape(dp_count, ctx_count, 2 * query_cols, model_width)
    grad_attn_blocks, head_blocks, key_value_blocks, ff_blocks = exchange(
        8,
        "last_scatter",
        [
            (
                "scatter",
                sequence_axes,
                grad_attn_part.astype(narrow).reshape(-1, tok_rows, model_width),
            ),
            ("scatter", ("ctx",), head_terms.transpose(1, 0, 2, 3)),
            ("scatter", sequence_axes, key_value_terms),
            ("relative", ("dp",), ff_sums),
        ],
        (sequence_axes, ("dp",)),
    )
    ff_own = add_up(ff_blocks)
    grad_attn_in = add_up(grad_attn_blocks)
    grad_in_part, gain_zero = norm_back(input_wide, inverse_in, norm_gains[0], grad_attn_in)
    d_block_in = (grad_middle + grad_in_part).astype(narrow)

    pad = ((0, 0), (0, model_width - head_width))
    gain_terms = jnp.concatenate(
        [
            jnp.sum(gain_zero, axis=0, keepdims=True),
            jnp.sum(gain_one, axis=0, keepdims=True),
            jnp.sum(gain_two, axis=0, keepdims=True),
            jnp.sum(gain_three, axis=0, keepdims=True),
            jnp.pad(jnp.sum(gain_query, axis=0, keepdims=True), pad),
            jnp.pad(jnp.sum(gain_key, axis=0, keepdims=True), pad),
            jnp.zeros((2, model_width), jnp.float32),
        ],
        axis=0,
    )
    gain_blocks, head_blocks, key_value_blocks = exchange(
        9,
        "depth_exchange",
        [
            ("gather", ("dp",), gain_terms),
            ("scatter", ("dp",), add_up(head_blocks).astype(narrow)),
            ("scatter", ("dp",), add_up(key_value_blocks).astype(narrow)),
        ],
    )
    head_own = lax.ppermute(add_up(head_blocks).astype(narrow), every_axis, to_owners).astype(
        jnp.float32
    )
    (gain_blocks,) = exchange(10, "gain_gather", [("gather", sequence_axes, add_up(gain_blocks))])
    gains = add_up(gain_blocks)
    key_value_own = add_up(key_value_blocks)
    return (
        block_out,
        d_block_in,
        gains[:4],
        gains[4:6, :head_width],
        head_own[:query_cols].T,
        key_value_own[:key_cols].T,
        key_value_own[key_cols:].T,
        head_own[query_cols:],
        ff_own[:ff_cols].T,
        ff_own[ff_cols : 2 * ff_cols].T,
        ff_own[2 * ff_cols :],
    )


bits = (0, 1)


class Mail:
    def __init__(self, send_sems, recv_sems):
        self.send_sems, self.recv_sems = send_sems, recv_sems
        self.started = []

    def push(self, source, target, to):
        number = len(self.started)
        copy = pltpu.make_async_remote_copy(
            src_ref=source,
            dst_ref=target,
            send_sem=self.send_sems.at[number],
            recv_sem=self.recv_sems.at[number],
            device_id=to,
            device_id_type=pl.DeviceIdType.MESH,
        )
        copy.start()
        self.started.append(copy)
        return copy

    def settle(self):
        for copy in self.started:
            copy.wait_send()


copy_limit = 176


def fused_kernel(names, *refs):
    r = types.SimpleNamespace(**dict(zip(names, refs)))
    narrow, wide = jnp.bfloat16, jnp.float32
    d, x, h = lax.axis_index("dp"), lax.axis_index("ctx"), lax.axis_index("head")
    depth = lax.axis_size("dp")
    y, c = h // 2, lax.rem(h, 2)
    me = x * 4 + h
    mail = Mail(r.send_sems, r.recv_sems)
    rows, width = r.block_in.shape
    head_width = r.qk_gains.shape[1]
    half_width = head_width // 2
    heads, query_cols = r.q_raw.shape[1] // head_width, r.q_rows.shape[0]
    key_cols = r.kv_rows.shape[0] // 2
    ff_cols = r.ff_rows.shape[0] // 3
    all_rows = 8 * rows
    full = heads * head_width

    def deep(offset):
        return lax.rem(d + offset, depth)

    def z_peer(offset):
        return {"dp": deep(offset)}

    x_peer = {"ctx": 1 - x}
    y_peer = {"head": (1 - y) * 2 + c}
    c_peer = {"head": y * 2 + 1 - c}

    def flip(place, bit):
        return 1 - place if bit else place

    def plane_peer(dx, dy, dc):
        return {"ctx": flip(x, dx), "head": flip(y, dy) * 2 + flip(c, dc)}

    plane_steps = [(dx, dy, dc) for dx in bits for dy in bits for dc in bits][1:]
    chip_steps = [(0, 1), (1, 0), (1, 1)]

    barrier = pltpu.get_barrier_semaphore()
    greeted = [z_peer(offset) for offset in range(1, depth)] + [plane_peer(*s) for s in plane_steps]
    for peer in greeted:
        pl.semaphore_signal(barrier, inc=1, device_id=peer, device_id_type=pl.DeviceIdType.MESH)
    r.block_all[x, y, c] = r.block_in[...]
    r.kv_all[d, x, y, c] = r.kv_rows[...]
    r.q_all[d, x, y, c] = r.q_rows[...]
    r.o_all[d, x, y, c] = r.o_rows[...]
    r.ff_all[d, x] = r.ff_rows[...]
    pl.semaphore_wait(barrier, len(greeted))

    got_z, got_x, got_y, got_c = {}, {}, {}, {}

    def place(part):
        return (x, y, c) if part == "block" else (d, x, y, c)

    def source(part):
        return r.block_in if part == "block" else getattr(r, part + "_rows")

    def own_to_x(part):
        got_x[part, 0] = mail.push(source(part), getattr(r, part + "_all").at[place(part)], x_peer)

    def own_to_y(part):
        got_y[part, 0] = [
            mail.push(source(part), getattr(r, part + "_all").at[place(part)], y_peer)
        ]

    def own_to_z(part):
        for offset in range(1, depth):
            target = getattr(r, part + "_all").at[place(part)]
            got_z[part, offset] = mail.push(source(part), target, z_peer(offset))

    def to_x(part):
        for offset in range(1, depth):
            got_z[part, offset].wait_recv()
            slot = deep(depth - offset)
            block = getattr(r, part + "_all").at[(slot,) + place(part)[1:]]
            got_x[part, offset] = mail.push(block, block, x_peer)

    def near_to_y(part):
        got_x[part, 0].wait_recv()
        at = (1 - x, y, c) if part == "block" else (d, 1 - x, y, c)
        block = getattr(r, part + "_all").at[at]
        got_y[part, 0].append(mail.push(block, block, y_peer))

    def to_y(part):
        for offset in range(1, depth):
            got_x[part, offset].wait_recv()
            block = getattr(r, part + "_all").at[deep(depth - offset), :, y, c]
            got_y[part, offset] = [mail.push(block, block, y_peer)]

    def to_c(part):
        for offset in range(1 if part == "block" else depth):
            for copy in got_y[part, offset]:
                copy.wait_recv()
            block = getattr(r, part + "_all")
            block = block if part == "block" else block.at[deep(depth - offset)]
            block = block.at[:, :, c]
            got_c[part, offset] = mail.push(block, block, c_peer)

    def arrived(part):
        for offset in range(1 if part == "block" else depth):
            got_c[part, offset].wait_recv()

    def ff_piece(slot, piece):
        return r.ff_all.at[slot, x, pl.ds(piece * ff_cols, ff_cols)]

    def ff_to_z(piece):
        for offset in range(1, depth):
            block = ff_piece(d, piece)
            got_z["ff", piece, offset] = mail.push(block, block, z_peer(offset))

    def ff_own_to_x():
        block = r.ff_all.at[d, x]
        got_x["ff", 0, 0] = mail.push(block, block, x_peer)

    def ff_to_x(piece):
        for offset in range(1, depth):
            got_z["ff", piece, offset].wait_recv()
            block = ff_piece(deep(depth - offset), piece)
            got_x["ff", piece, offset] = mail.push(block, block, x_peer)

    position_copy = mail.push(r.pos, r.pos_far, x_peer)
    for part in ("kv", "block", "q", "o"):
        own_to_x(part)
        own_to_y(part)
        if part != "block":
            own_to_z(part)

    def rope_tables():
        position_copy.wait_recv()
        turned = (r.pos[...] + r.pos_far[...]).T
        ladder = lax.broadcasted_iota(jnp.int32, (1, half_width), 1).astype(wide)
        frequency = jnp.exp(ladder * (-2.0 / head_width) * math.log(rope_base))
        column = lax.broadcasted_iota(jnp.int32, turned.shape, 1)
        r.pos_own[...] = jnp.sum(jnp.where(column == me, turned, 0.0), axis=1, keepdims=True)
        for block in range(8):
            angle = turned[:, block : block + 1] * frequency
            r.cosine[block] = jnp.cos(angle)
            r.sine[block] = jnp.sin(angle)

    def shuffle():
        size = 2 * head_width
        there = lax.broadcasted_iota(jnp.int32, (size, size), 1).astype(wide)
        here = lax.broadcasted_iota(jnp.int32, (size, size), 0).astype(wide)

        def sorted_place(place):
            block = jnp.floor((place + 0.5) / (2 * key_cols))
            inside = place - block * (2 * key_cols)
            value = inside >= key_cols
            return block * key_cols + jnp.where(value, inside - key_cols + head_width, inside)

        r.unsort[...] = jnp.where(sorted_place(here) == there, 1.0, 0.0).astype(narrow)
        r.sort[...] = jnp.where(sorted_place(there) == here, 1.0, 0.0).astype(narrow)

    def attention_inputs():
        arrived("block")
        gain = r.norm_gains[0:1]
        for px in bits:
            for py in bits:
                for pc in bits:
                    values = r.block_all[px, py, pc].astype(wide)
                    r.attn_in[px * 4 + py * 2 + pc] = norm_rows(values, gain)[0].astype(narrow)

    def keys_and_values():
        arrived("kv")
        blocks = r.kv_all[...].reshape(2 * head_width, width)
        r.kv_sorted[...] = rows_dot(r.sort[...], blocks, 1, 0).astype(narrow)
        gain = r.qk_gains[1:2]
        for pair in range(4):
            two = pl.ds(2 * pair, 2)
            inputs = r.attn_in[two].reshape(2 * rows, width)
            raw = rows_dot(inputs, r.kv_sorted[...], 1, 1)
            key_raw = raw[:, :head_width]
            r.key_raw[two] = key_raw.reshape(2, rows, head_width)
            cosine = r.cosine[two].reshape(2 * rows, half_width)
            sine_part = r.sine[two].reshape(2 * rows, half_width)
            turned = rotate(norm_rows(key_raw, gain)[0], cosine, sine_part)
            r.keys[pl.ds(2 * pair * rows, 2 * rows)] = turned.astype(narrow)
            r.values[pl.ds(2 * pair * rows, 2 * rows)] = raw[:, head_width:].astype(narrow)

    shuffle()
    rope_tables()
    to_x("kv")
    near_to_y("kv")
    near_to_y("block")
    ff_to_z(0)
    to_x("q")
    near_to_y("q")
    to_y("kv")
    ff_to_z(1)
    ff_own_to_x()
    to_x("o")
    near_to_y("o")
    to_y("q")
    ff_to_z(2)
    to_c("block")
    attention_inputs()
    ff_to_x(0)
    to_c("kv")
    to_y("o")
    keys_and_values()
    ff_to_x(1)
    to_c("q")

    query_gain = r.qk_gains[0:1]
    arrived("q")
    weight = r.q_all[...].reshape(full, width)
    r.q_raw[...] = rows_dot(r.attn_in[me], weight, 1, 1)
    for head in range(heads):
        turned = rotate(
            norm_rows(r.q_raw[:, head * head_width : (head + 1) * head_width], query_gain)[0],
            r.cosine[me],
            r.sine[me],
        )
        r.q_rot[head] = (turned * score_scale).astype(narrow)
    to_c("o")
    ff_to_x(2)

    query_index = lax.broadcasted_iota(jnp.int32, (rows, all_rows), 0) + me * rows
    key_index = lax.broadcasted_iota(jnp.int32, (rows, all_rows), 1)
    lowest_key = query_index - r.pos_own[...].astype(jnp.int32)
    visible = (key_index <= query_index) & (key_index >= lowest_key)
    r.bias[...] = jnp.where(visible, 0.0, negative_fill)
    for head in range(heads):
        scores = rows_dot(r.q_rot[head], r.keys[...], 1, 1)
        scores = jnp.where(r.bias[...] < 0.0, negative_fill, scores)
        top = jnp.max(scores, axis=1, keepdims=True)
        raised = jnp.exp(scores - top)
        prob_rows = raised * (1.0 / jnp.sum(raised, axis=1, keepdims=True))
        r.probs[head] = prob_rows
        r.probs_narrow[head] = prob_rows.astype(narrow)
        exact = rows_dot(prob_rows.astype(narrow), r.values[...], 1, 0)
        r.exact[head] = exact
        r.attn_out[:, head * head_width : (head + 1) * head_width] = exact.astype(narrow)
    arrived("o")
    out_weight = r.o_all[...].reshape(full, width)
    r.branch[...] = rows_dot(r.attn_out[...], out_weight, 1, 0)
    def send_factor(name):
        copies = []
        for step in plane_steps:
            px, py, pc = (flip(place, bit) for place, bit in zip((x, y, c), step))
            copies.append(
                mail.push(getattr(r, name).at[:, px, py, pc], getattr(r, name + "_got").at[me], plane_peer(*step))
            )
        getattr(r, name + "_got")[me] = getattr(r, name)[:, x, y, c]
        return copies

    def turned_blocks(name, values, columns):
        getattr(r, name)[...] = values.astype(wide).T.astype(narrow).reshape(depth, 2, 2, 2, columns, rows)

    input_wide = r.block_in[...].astype(wide)
    branch_normed = norm_rows(r.branch[...], r.norm_gains[1:2])[0]
    r.middle[...] = input_wide + branch_normed
    mlp_rows = norm_rows(r.middle[...], r.norm_gains[2:3])[0].astype(narrow)

    def share_rows(name, values):
        getattr(r, name)[y, c] = values
        block = getattr(r, name).at[y, c]
        return mail.push(block, block, c_peer), mail.push(block, block, y_peer)

    def far_rows(name, from_y):
        from_y.wait_recv()
        block = getattr(r, name).at[1 - y, c]
        return mail.push(block, block, c_peer)

    def fetch_ff():
        got_x["ff", 0, 0].wait_recv()
        for piece in range(3):
            for offset in range(1, depth):
                got_x["ff", piece, offset].wait_recv()

    def ff_part(index):
        piece = r.ff_all[:, :, pl.ds(index * ff_cols, ff_cols)]
        return piece.reshape(2 * depth * ff_cols, width)

    def group_sum(name, half, own_rows, between):
        part, near, far = getattr(r, name), getattr(r, name + "_near"), getattr(r, name + "_far")
        from_c, from_y, forwarded = own_rows
        from_c.wait_recv()
        half(y)
        near_own = mail.push(part.at[y, 1 - c], near.at[0], c_peer)
        if forwarded is None:
            forwarded = from_y()
        forwarded.wait_recv()
        half(1 - y)
        near_far = mail.push(part.at[1 - y, 1 - c], near.at[1], c_peer)
        near_far.wait_recv()
        summed = part[1 - y, c].astype(wide) + near[1].astype(wide)
        getattr(r, name + "_sum")[...] = summed.astype(narrow)
        far_copy = mail.push(getattr(r, name + "_sum"), far, y_peer)
        between()
        near_own.wait_recv()
        own = part[y, c].astype(wide) + near[0].astype(wide)
        far_copy.wait_recv()
        return own + far[...].astype(wide)

    def forward_half(side):
        inputs = r.mlp_in[side].reshape(2 * rows, width)
        gate_pre = rows_dot(inputs, ff_part(0), 1, 1)
        up_pre = rows_dot(inputs, ff_part(1), 1, 1)
        r.gate_pre[side] = gate_pre
        r.up_pre[side] = up_pre
        hidden = (gelu_parts(gate_pre)[0] * up_pre).astype(narrow)
        r.hidden[side] = hidden
        part = rows_dot(hidden, ff_part(2), 1, 0).astype(narrow)
        r.down[side] = part.reshape(2, rows, width)

    near_copy, y_copy = share_rows("mlp_in", mlp_rows)
    turned_blocks("out_turned", r.attn_out[...], query_cols)
    out_copies = send_factor("out_turned")
    fetch_ff()
    r.down_raw[...] = group_sum(
        "down", forward_half, (near_copy, lambda: far_rows("mlp_in", y_copy), None), lambda: None
    )
    down_raw = r.down_raw[...]
    down_normed, inverse_down = norm_rows(down_raw, r.norm_gains[3:4])
    r.block_out[...] = (r.middle[...] + down_normed).astype(narrow)
    cot_wide = r.cotangent[...].astype(wide)
    grad_down_raw, gain_three = norm_back(down_raw, inverse_down, r.norm_gains[3:4], cot_wide)
    r.gains[...] = jnp.zeros_like(r.gains)
    r.gains[3:4] = jnp.sum(gain_three, axis=0, keepdims=True)

    def backward_half(side):
        grad_hidden = rows_dot(r.grad_down[side].reshape(2 * rows, width), ff_part(2), 1, 1)
        gelu, slope = gelu_parts(r.gate_pre[side])
        grad_gate = (grad_hidden * r.up_pre[side] * slope).astype(narrow)
        grad_up = (grad_hidden * gelu).astype(narrow)
        r.grad_gate[side] = grad_gate
        r.grad_up[side] = grad_up
        part = rows_dot(grad_gate, ff_part(0), 1, 0) + rows_dot(grad_up, ff_part(1), 1, 0)
        r.mlp_back[side] = part.astype(narrow).reshape(2, rows, width)

    ff_width = 2 * depth * ff_cols

    def ff_terms(index, left, right):
        terms = rows_dot(getattr(r, left)[...].reshape(4 * rows, ff_width), getattr(r, right)[...].reshape(4 * rows, width), 0, 0)
        r.ff_terms[:, :, pl.ds(index * ff_cols, ff_cols)] = terms.astype(narrow).reshape(
            depth, 2, ff_cols, width
        )

    ff_across = []

    def ff_terms_to_x(offset):
        ff_across.append(mail.push(r.ff_terms.at[deep(offset), 1 - x], r.ff_near.at[offset], x_peer))

    def all_ff_terms():
        ff_terms(2, "hidden", "grad_down")
        ff_terms(0, "grad_gate", "mlp_in")
        ff_terms(1, "grad_up", "mlp_in")
        for offset in range(1, depth):
            ff_terms_to_x(offset)

    near_copy, y_copy = share_rows("grad_down", grad_down_raw.astype(narrow))
    grad_mlp_in = group_sum(
        "mlp_back",
        backward_half,
        (near_copy, lambda: far_rows("grad_down", y_copy), None),
        all_ff_terms,
    )
    middle = r.middle[...]
    inverse_mid = norm_rows(middle, r.norm_gains[2:3])[1]
    grad_mid_part, gain_two = norm_back(middle, inverse_mid, r.norm_gains[2:3], grad_mlp_in)
    r.gains[2:3] = jnp.sum(gain_two, axis=0, keepdims=True)
    grad_middle = r.cotangent[...].astype(wide) + grad_mid_part
    r.grad_middle[...] = grad_middle
    branch = r.branch[...]
    inverse_branch = norm_rows(branch, r.norm_gains[1:2])[1]
    grad_branch_raw, gain_one = norm_back(branch, inverse_branch, r.norm_gains[1:2], grad_middle)
    r.gains[1:2] = jnp.sum(gain_one, axis=0, keepdims=True)
    grad_branch = grad_branch_raw.astype(narrow)
    branch_all = r.branch_all
    branch_all[x, y, c] = grad_branch
    block = branch_all.at[x, y, c]
    branch_x = mail.push(block, block, x_peer)
    branch_y = [mail.push(block, block, y_peer)]

    head_grad = rows_dot(grad_branch, out_weight, 1, 1).astype(narrow)
    for head in range(heads):
        r.head_grad[head] = head_grad[:, head * head_width : (head + 1) * head_width]

    ff_deep = []

    def ff_step(number):
        ff_across[number].wait_recv()
        offset = number + 1 if number < depth - 1 else 0
        summed = r.ff_terms[deep(offset), x].astype(wide) + r.ff_near[offset].astype(wide)
        if offset:
            r.ff_sum[offset] = summed.astype(narrow)
            ff_deep.append(
                mail.push(r.ff_sum.at[offset], r.ff_got.at[offset], z_peer(offset))
            )
        else:
            r.ff_own[...] = summed

    for head in range(heads):
        grad_rows = r.head_grad[head]
        delta = jnp.sum(grad_rows.astype(wide) * r.exact[head], axis=1, keepdims=True)
        grad_probs = rows_dot(grad_rows, r.values[...], 1, 1)
        r.grad_scores[head] = (r.probs[head] * (grad_probs - delta)).astype(narrow)
    ff_step(0)
    all_grads = r.head_grad[...].reshape(heads * rows, head_width)
    all_queries = r.q_rot[...].reshape(heads * rows, head_width)
    for pair in range(4):
        here = slice(2 * pair * rows, 2 * (pair + 1) * rows)
        px, py = pair // 2, pair % 2
        key_part = rows_dot(
            r.grad_scores[:, :, here].reshape(heads * rows, 2 * rows), all_queries, 0, 0
        )
        value_part = rows_dot(
            r.probs_narrow[:, :, here].reshape(heads * rows, 2 * rows), all_grads, 0, 0
        )
        r.kv_terms[px, py, :, :, :head_width] = key_part.astype(narrow).reshape(2, rows, head_width)
        r.kv_terms[px, py, :, :, head_width:] = value_part.astype(narrow).reshape(2, rows, head_width)
    kv_near = mail.push(r.kv_terms.at[:, :, 1 - c], r.kv_near, c_peer)

    cosine, sine_part = r.cosine[me], r.sine[me]
    gain_query = jnp.zeros((1, head_width), wide)
    for head in range(heads):
        here = slice(head * head_width, (head + 1) * head_width)
        turned = rows_dot(r.grad_scores[head], r.keys[...], 1, 0) * score_scale
        upstream = rotate(turned, cosine, -sine_part)
        query_raw = r.q_raw[:, here]
        inverse = norm_rows(query_raw, query_gain)[1]
        grad_raw, gain_rows = norm_back(query_raw, inverse, query_gain, upstream)
        gain_query += jnp.sum(gain_rows, axis=0, keepdims=True)
        r.grad_query[:, here] = grad_raw.astype(narrow)
    r.gains[4:5, :head_width] = gain_query

    kv_near.wait_recv()
    for px in bits:
        for py in bits:
            summed = r.kv_terms[px, py, c].astype(wide) + r.kv_near[px, py].astype(wide)
            r.kv_sums[px, py] = summed.astype(narrow)
    kv_copies = []
    for number, (dx, dy) in enumerate(chip_steps):
        kv_copies.append(
            mail.push(
                r.kv_sums.at[flip(x, dx), flip(y, dy)], r.kv_far.at[number], plane_peer(dx, dy, 0)
            )
        )
    turned_blocks("query_turned", r.grad_query[...], query_cols)
    query_copies = send_factor("query_turned")
    ff_terms_to_x(0)
    ff_step(1)
    branch_x.wait_recv()
    block = branch_all.at[1 - x, y, c]
    branch_y.append(mail.push(block, block, y_peer))
    query_part = rows_dot(r.grad_query[...], r.q_all[...].reshape(full, width), 1, 0)
    r.query_part[...] = query_part

    def weight_terms(name, copies, source, columns):
        for copy in copies:
            copy.wait_recv()
        terms = jnp.zeros((depth * columns, width), wide)
        for block in range(8):
            left = getattr(r, name + "_got")[block].reshape(depth * columns, rows)
            right = source(block)
            terms += rows_dot(left, right, 1, 0)
        getattr(r, name + "_wide")[...] = terms.reshape(depth, columns, width)
        getattr(r, name + "_terms")[...] = terms.astype(narrow).reshape(depth, columns, width)
        return [
            mail.push(getattr(r, name + "_terms").at[deep(offset)], getattr(r, name + "_far").at[offset], z_peer(offset))
            for offset in range(1, depth)
        ]

    ff_step(2)
    for copy in kv_copies:
        copy.wait_recv()
    kv_sum = r.kv_sums[x, y].astype(wide)
    for number in range(len(chip_steps)):
        kv_sum += r.kv_far[number].astype(wide)
    key_gain = r.qk_gains[1:2]
    key_raw = r.key_raw[me]
    key_back = rotate(kv_sum[:, :head_width], cosine, -sine_part)
    inverse_key = norm_rows(key_raw, key_gain)[1]
    grad_key_raw, gain_key = norm_back(key_raw, inverse_key, key_gain, key_back)
    r.gains[5:6, :head_width] = jnp.sum(gain_key, axis=0, keepdims=True)
    r.grad_kv[:, :head_width] = grad_key_raw.astype(narrow)
    r.grad_kv[:, head_width:] = kv_sum[:, head_width:].astype(narrow)
    kv_turned = rows_dot(r.unsort[...], r.grad_kv[...], 1, 1).astype(narrow)
    r.kv_turned[...] = kv_turned.reshape(depth, 2, 2, 2, 2 * key_cols, rows)
    kv_factor_copies = send_factor("kv_turned")

    grad_attn_in = r.query_part[...] + rows_dot(r.grad_kv[...], r.kv_sorted[...], 1, 0)
    input_wide = r.block_in[...].astype(wide)
    inverse_in = norm_rows(input_wide, r.norm_gains[0:1])[1]
    grad_in_part, gain_zero = norm_back(input_wide, inverse_in, r.norm_gains[0:1], grad_attn_in)
    r.d_block_in[...] = (r.grad_middle[...] + grad_in_part).astype(narrow)
    r.gains[0:1] = jnp.sum(gain_zero, axis=0, keepdims=True)
    gain_copies = [
        mail.push(r.gains, r.gains_got.at[number], plane_peer(*step))
        for number, step in enumerate(plane_steps)
    ]

    for copy in branch_y:
        copy.wait_recv()
    block = branch_all.at[:, :, c]
    branch_c = mail.push(block, block, c_peer)
    query_deep = weight_terms("query_turned", query_copies, lambda block: r.attn_in[block], query_cols)
    kv_deep = weight_terms("kv_turned", kv_factor_copies, lambda block: r.attn_in[block], 2 * key_cols)
    gain_sum = r.gains[...]
    for number, copy in enumerate(gain_copies):
        copy.wait_recv()
        gain_sum += r.gains_got[number]
    r.gains_sum[...] = gain_sum
    gain_deep = [
        mail.push(r.gains_sum, r.gains_deep.at[offset], z_peer(offset)) for offset in range(1, depth)
    ]
    branch_c.wait_recv()
    out_deep = weight_terms(
        "out_turned",
        out_copies,
        lambda block: branch_all[block // 4, block // 2 % 2, block % 2],
        query_cols,
    )
    for number in range(3, depth):
        ff_step(number)

    def deep_sum(own, far, copies):
        for number, copy in enumerate(copies):
            copy.wait_recv()
            own += far[number + 1].astype(wide)
        return own

    r.grad_q_rows[...] = deep_sum(r.query_turned_wide[d], r.query_turned_far, query_deep)
    r.grad_o_rows[...] = deep_sum(r.out_turned_wide[d], r.out_turned_far, out_deep)
    r.grad_ff_rows[...] = deep_sum(r.ff_own[...], r.ff_got, ff_deep)
    r.grad_kv_rows[...] = deep_sum(r.kv_turned_wide[d], r.kv_turned_far, kv_deep)
    r.gains_out[...] = deep_sum(r.gains_sum[...], r.gains_deep, gain_deep)
    mail.settle()


def fused_local(
    block_in,
    cotangent,
    positions,
    norm_gains,
    qk_gains,
    w_query,
    w_key,
    w_value,
    w_out,
    w_gate,
    w_up,
    w_down,
):
    narrow, wide = jnp.bfloat16, jnp.float32
    rows, width = block_in.shape
    head_width = qk_gains.shape[1]
    depth = lax.axis_size("dp")
    query_cols, key_cols, ff_cols = w_query.shape[1], w_key.shape[1], w_gate.shape[1]
    full = query_cols * lax.axis_size(every_axis)
    heads = full // head_width
    plane = lax.axis_size(sequence_axes)
    length = plane * rows
    ff_width = 2 * depth * ff_cols
    own_positions = positions.reshape(-1, rows).astype(wide)
    pos = lax.dynamic_update_slice(
        jnp.zeros((plane, rows), wide), own_positions, (lax.axis_index("ctx") * own_positions.shape[0], 0)
    )
    operands = dict(
        block_in=block_in,
        cotangent=cotangent,
        pos=pos,
        norm_gains=norm_gains,
        qk_gains=qk_gains,
        q_rows=w_query.T,
        o_rows=w_out,
        kv_rows=jnp.concatenate([w_key.T, w_value.T], axis=0),
        ff_rows=jnp.concatenate([w_gate.T, w_up.T, w_down], axis=0),
    )
    results = dict(
        block_out=((rows, width), narrow),
        d_block_in=((rows, width), narrow),
        gains_out=((8, width), wide),
        grad_q_rows=((query_cols, width), wide),
        grad_o_rows=((query_cols, width), wide),
        grad_kv_rows=((2 * key_cols, width), wide),
        grad_ff_rows=((3 * ff_cols, width), wide),
    )
    cube = (depth, 2, 2, 2)
    scratch = dict(
        block_all=((2, 2, 2, rows, width), narrow),
        kv_all=(cube + (2 * key_cols, width), narrow),
        q_all=(cube + (query_cols, width), narrow),
        o_all=(cube + (query_cols, width), narrow),
        ff_all=((depth, 2, 3 * ff_cols, width), narrow),
        pos_far=((plane, rows), wide),
        pos_own=((rows, 1), wide),
        cosine=((plane, rows, head_width // 2), wide),
        sine=((plane, rows, head_width // 2), wide),
        sort=((2 * head_width, 2 * head_width), narrow),
        unsort=((2 * head_width, 2 * head_width), narrow),
        attn_in=((plane, rows, width), narrow),
        kv_sorted=((2 * head_width, width), narrow),
        key_raw=((plane, rows, head_width), wide),
        keys=((length, head_width), narrow),
        values=((length, head_width), narrow),
        q_raw=((rows, full), wide),
        q_rot=((heads, rows, head_width), narrow),
        bias=((rows, length), wide),
        probs=((heads, rows, length), wide),
        probs_narrow=((heads, rows, length), narrow),
        exact=((heads, rows, head_width), wide),
        attn_out=((rows, full), narrow),
        branch=((rows, width), wide),
        middle=((rows, width), wide),
        mlp_in=((2, 2, rows, width), narrow),
        gate_pre=((2, 2 * rows, ff_width), wide),
        up_pre=((2, 2 * rows, ff_width), wide),
        hidden=((2, 2 * rows, ff_width), narrow),
        down_raw=((rows, width), wide),
        grad_down=((2, 2, rows, width), narrow),
        grad_gate=((2, 2 * rows, ff_width), narrow),
        grad_up=((2, 2 * rows, ff_width), narrow),
        grad_middle=((rows, width), wide),
        branch_all=((2, 2, 2, rows, width), narrow),
        head_grad=((heads, rows, head_width), narrow),
        grad_scores=((heads, rows, length), narrow),
        grad_query=((rows, full), narrow),
        query_part=((rows, width), wide),
        grad_kv=((rows, 2 * head_width), narrow),
        kv_terms=((2, 2, 2, rows, 2 * head_width), narrow),
        kv_near=((2, 2, rows, 2 * head_width), narrow),
        kv_sums=((2, 2, rows, 2 * head_width), narrow),
        kv_far=((3, rows, 2 * head_width), narrow),
        ff_terms=((depth, 2, 3 * ff_cols, width), narrow),
        ff_near=((depth, 3 * ff_cols, width), narrow),
        ff_sum=((depth, 3 * ff_cols, width), narrow),
        ff_got=((depth, 3 * ff_cols, width), narrow),
        ff_own=((3 * ff_cols, width), wide),
        gains=((8, width), wide),
        gains_got=((plane - 1, 8, width), wide),
        gains_sum=((8, width), wide),
        gains_deep=((depth, 8, width), wide),
    )
    for name in ("down", "mlp_back"):
        scratch[name] = ((2, 2, rows, width), narrow)
        scratch[name + "_near"] = ((2, rows, width), narrow)
        scratch[name + "_sum"] = ((rows, width), narrow)
        scratch[name + "_far"] = ((rows, width), narrow)
    for name, columns in (("out_turned", query_cols), ("query_turned", query_cols), ("kv_turned", 2 * key_cols)):
        scratch[name] = (cube + (columns, rows), narrow)
        scratch[name + "_got"] = ((plane, depth, columns, rows), narrow)
        scratch[name + "_wide"] = ((depth, columns, width), wide)
        scratch[name + "_terms"] = ((depth, columns, width), narrow)
        scratch[name + "_far"] = ((depth, columns, width), narrow)
    names = list(operands) + list(results) + list(scratch) + ["send_sems", "recv_sems"]
    in_vmem = pl.BlockSpec(memory_space=pltpu.VMEM)
    outs = pl.pallas_call(
        lambda *refs: fused_kernel(names, *refs),
        out_shape=[jax.ShapeDtypeStruct(*result) for result in results.values()],
        in_specs=[in_vmem] * len(operands),
        out_specs=[in_vmem] * len(results),
        scratch_shapes=[pltpu.VMEM(*one) for one in scratch.values()]
        + [pltpu.SemaphoreType.DMA((copy_limit,))] * 2,
        compiler_params=pltpu.CompilerParams(
            collective_id=11, has_side_effects=True, vmem_limit_bytes=56 * 1024 * 1024
        ),
        name="layer",
    )(*operands.values())
    block_out, d_block_in, gains, query_rows, out_rows, kv_rows, ff_rows = outs
    return (
        block_out,
        d_block_in,
        gains[:4],
        gains[4:6, :head_width],
        query_rows.T,
        kv_rows[:key_cols].T,
        kv_rows[key_cols:].T,
        out_rows,
        ff_rows[:ff_cols].T,
        ff_rows[ff_cols : 2 * ff_cols].T,
        ff_rows[2 * ff_cols :],
    )


def fits_fused(block_in, w_query, w_key, w_gate):
    tiles = (w_query.shape[1], 2 * w_key.shape[1], w_gate.shape[1])
    return (
        lax.axis_size("ctx") == 2
        and lax.axis_size("head") == 4
        and block_in.shape[0] % 128 == 0
        and all(columns % 16 == 0 for columns in tiles)
    )


def either_local(*args):
    if fits_fused(args[0], args[5], args[6], args[9]):
        return fused_local(*args)
    return local(*args)


def solution(mesh):
    in_specs = (
        P(every_axis, None),
        P(every_axis, None),
        P(weight_axes),
        P(),
        P(),
        P(None, every_axis),
        P(None, every_axis),
        P(None, every_axis),
        P(every_axis, None),
        P(None, every_axis),
        P(None, every_axis),
        P(every_axis, None),
    )
    out_specs = (
        P(every_axis, None),
        P(every_axis, None),
        P(),
        P(),
        P(None, every_axis),
        P(None, every_axis),
        P(None, every_axis),
        P(every_axis, None),
        P(None, every_axis),
        P(None, every_axis),
        P(every_axis, None),
    )
    return jax.shard_map(either_local, mesh=mesh, in_specs=in_specs, out_specs=out_specs, check_vma=False)
```

```python
import math
import types

import jax
import jax.numpy as jnp
from jax import lax
from jax.experimental import pallas as pl
from jax.experimental.pallas import tpu as pltpu
from jax.sharding import PartitionSpec as P

epsilon = 1e-06
rope_base = 1000000.0
score_scale = 0.0625
negative_fill = -1e30


def norm_rows(values, gain_vec):
    inverse = lax.rsqrt(jnp.mean(values * values, axis=-1, keepdims=True) + epsilon)
    return (values * inverse * gain_vec, inverse)


def norm_back(values, inverse, gain_vec, upstream):
    scaled = upstream * gain_vec
    inner_mean = jnp.mean(scaled * values, axis=-1, keepdims=True)
    return (
        inverse * scaled - values * (inverse * inverse * inverse) * inner_mean,
        upstream * values * inverse,
    )


def rope_angles(positions, full_width):
    ladder = jnp.arange(full_width // 2, dtype=jnp.float32)
    frequency = jnp.exp(ladder * (-2.0 / full_width) * math.log(rope_base))
    angles = positions.astype(jnp.float32)[:, None] * frequency[None, :]
    return (jnp.cos(angles), jnp.sin(angles))


def rotate(values, cosine, sine_part):
    middle = values.shape[-1] // 2
    first_half = values[..., :middle]
    second = values[..., middle:]
    return jnp.concatenate(
        [first_half * cosine - second * sine_part, second * cosine + first_half * sine_part],
        axis=-1,
    )


def gelu_product(gate_pre, up_pre):
    return jax.nn.gelu(gate_pre, approximate=True) * up_pre


every_axis = ("dp", "ctx", "head")
sequence_axes = ("ctx", "head")
weight_axes = ("dp", "ctx")


def place_in(axes):
    place = 0
    for name in axes:
        place = place * lax.axis_size(name) + lax.axis_index(name)
    return place


def coordinates(axes, place):
    found = {}
    for name in reversed(axes):
        size = lax.axis_size(name)
        found[name] = lax.rem(place, size)
        place = place // size
    return found


def each_peer(count, step):
    if count <= 8:
        for offset in range(1, count):
            step(offset)
    else:

        def looped(offset, carry):
            step(offset)
            return carry

        lax.fori_loop(1, count, looped, 0)


def exchange_kernel(kinds, greet, counts, *refs):
    total = len(kinds)
    sources, targets, sems = refs[:total], refs[total : 2 * total], refs[2 * total :]
    barrier = pltpu.get_barrier_semaphore()
    waits = 0
    for axes, count in greet:
        me = place_in(axes)

        def greet_peer(offset, axes=axes, count=count, me=me):
            pl.semaphore_signal(
                barrier,
                inc=1,
                device_id=coordinates(axes, lax.rem(me + offset, count)),
                device_id_type=pl.DeviceIdType.MESH,
            )

        each_peer(count, greet_peer)
        waits += count - 1
    locals_started = []
    for part, (kind, axes) in enumerate(kinds):
        me = place_in(axes)
        source = {"scatter": me, "relative": 0}.get(kind)
        source = sources[part] if source is None else sources[part].at[source]
        copy = pltpu.make_async_copy(source, targets[part].at[me], sems[3 * part + 2].at[0])
        copy.start()
        locals_started.append(copy)
    pl.semaphore_wait(barrier, waits)

    def descriptor(part, offset, backward):
        kind, axes = kinds[part]
        count = counts[part]
        me = place_in(axes)
        to = lax.rem(me + offset, count)
        origin = lax.rem(me + count - offset, count) if backward else me
        source = {"scatter": to, "relative": lax.rem(count - offset, count)}.get(kind)
        source = sources[part] if source is None else sources[part].at[source]
        return pltpu.make_async_remote_copy(
            src_ref=source,
            dst_ref=targets[part].at[origin],
            send_sem=sems[3 * part].at[offset],
            recv_sem=sems[3 * part + 1].at[origin],
            device_id=coordinates(axes, to),
            device_id_type=pl.DeviceIdType.MESH,
        )

    for part in range(total):
        each_peer(counts[part], lambda offset: descriptor(part, offset, False).start())
    for copy in locals_started:
        copy.wait()
    for part in range(total):
        each_peer(counts[part], lambda offset: descriptor(part, offset, True).wait_recv())
    for part in range(total):
        each_peer(counts[part], lambda offset: descriptor(part, offset, False).wait_send())


def exchange(call_id, name, parts, greet_axes=None):
    kinds = tuple((kind, axes) for kind, axes, _ in parts)
    arrays = [array for _, _, array in parts]
    counts = tuple(lax.axis_size(axes) for _, axes in kinds)
    if greet_axes is None:
        greet_axes = (kinds[0][1],)
    greet = tuple((axes, lax.axis_size(axes)) for axes in greet_axes)
    shapes = [
        jax.ShapeDtypeStruct(
            (count,) + array.shape if kind == "gather" else array.shape, array.dtype
        )
        for (kind, _, array), count in zip(parts, counts)
    ]
    scratch = []
    for count in counts:
        scratch += [
            pltpu.SemaphoreType.DMA((count,)),
            pltpu.SemaphoreType.DMA((count,)),
            pltpu.SemaphoreType.DMA((1,)),
        ]
    in_vmem = pl.BlockSpec(memory_space=pltpu.VMEM)
    return pl.pallas_call(
        lambda *refs: exchange_kernel(kinds, greet, counts, *refs),
        out_shape=shapes,
        in_specs=[in_vmem] * len(arrays),
        out_specs=[in_vmem] * len(arrays),
        scratch_shapes=scratch,
        compiler_params=pltpu.CompilerParams(collective_id=call_id, has_side_effects=True),
        name=name,
    )(*arrays)


def digit_place(digit):
    if digit == "head_slow":
        return lax.axis_index("head") // fast_size()
    if digit == "head_fast":
        return lax.rem(lax.axis_index("head"), fast_size())
    return lax.axis_index(digit)


def fast_size():
    return 2 if lax.axis_size("head") % 2 == 0 else 1


def digit_size(digit):
    if digit == "head_slow":
        return lax.axis_size("head") // fast_size()
    if digit == "head_fast":
        return fast_size()
    return lax.axis_size(digit)


def digit_device(digit, value):
    if digit == "head_slow":
        return {"head": value * fast_size() + digit_place("head_fast")}
    if digit == "head_fast":
        return {"head": digit_place("head_slow") * fast_size() + value}
    return {digit: value}


def staged_kernel(plans, greeted, *refs):
    total = len(plans)
    sources, targets, sems = refs[:total], refs[total : 2 * total], list(refs[2 * total :])
    barrier = pltpu.get_barrier_semaphore()
    waits = 0
    for digit in greeted:
        count, me = digit_size(digit), digit_place(digit)
        for offset in range(1, count):
            pl.semaphore_signal(
                barrier,
                inc=1,
                device_id=digit_device(digit, lax.rem(me + offset, count)),
                device_id_type=pl.DeviceIdType.MESH,
            )
            waits += 1
    local_sems = sems[:total]
    rest = sems[total:]
    pairs = []
    for plan in plans:
        pairs.append([(rest.pop(0), rest.pop(0)) for _ in plan])
    own = []
    for part, plan in enumerate(plans):
        here = tuple(digit_place(digit) for digit in reversed(plan))
        copy = pltpu.make_async_copy(sources[part], targets[part].at[here], local_sems[part].at[0])
        copy.start()
        own.append(copy)
    pl.semaphore_wait(barrier, waits)

    def descriptors(part, turn, backward):
        plan = plans[part]
        digit = plan[turn]
        count, me = digit_size(digit), digit_place(digit)
        outer = tuple(digit_place(name) for name in reversed(plan[turn + 1 :]))
        found = []
        for offset in range(1, count):
            to = lax.rem(me + offset, count)
            origin = lax.rem(me + count - offset, count) if backward else me
            source = sources[part] if turn == 0 else targets[part].at[outer + (me,)]
            found.append(
                pltpu.make_async_remote_copy(
                    src_ref=source,
                    dst_ref=targets[part].at[outer + (origin,)],
                    send_sem=pairs[part][turn][0].at[offset],
                    recv_sem=pairs[part][turn][1].at[origin],
                    device_id=digit_device(digit, to),
                    device_id_type=pl.DeviceIdType.MESH,
                )
            )
        return found

    most = max(len(plan) for plan in plans)
    for turn in range(most + 1):
        for part, plan in enumerate(plans):
            if 0 < turn <= len(plan):
                for copy in descriptors(part, turn - 1, True):
                    copy.wait_recv()
            if turn == 1:
                own[part].wait()
            if turn < len(plan):
                for copy in descriptors(part, turn, False):
                    copy.start()
    for part, plan in enumerate(plans):
        for turn in range(len(plan)):
            for copy in descriptors(part, turn, False):
                copy.wait_send()


def staged_gather(call_id, name, parts):
    plans = [plan for plan, _ in parts]
    arrays = [array for _, array in parts]
    greeted = []
    for plan in plans:
        greeted += [digit for digit in plan if digit not in greeted]
    shapes = [
        jax.ShapeDtypeStruct(
            tuple(digit_size(digit) for digit in reversed(plan)) + array.shape, array.dtype
        )
        for plan, array in parts
    ]
    scratch = [pltpu.SemaphoreType.DMA((1,)) for _ in parts]
    for plan in plans:
        for digit in plan:
            scratch += [pltpu.SemaphoreType.DMA((digit_size(digit),))] * 2
    in_vmem = pl.BlockSpec(memory_space=pltpu.VMEM)
    return pl.pallas_call(
        lambda *refs: staged_kernel(plans, greeted, *refs),
        out_shape=shapes,
        in_specs=[in_vmem] * len(arrays),
        out_specs=[in_vmem] * len(arrays),
        scratch_shapes=scratch,
        compiler_params=pltpu.CompilerParams(collective_id=call_id, has_side_effects=True),
        name=name,
    )(*arrays)


def gather_rows(call_id, name, rows):
    (blocks,) = exchange(call_id, name, [("gather", ("head",), rows)])
    return blocks.reshape(-1, rows.shape[1])


def shifted(array, axis, offset):
    count = lax.axis_size(axis)
    return lax.ppermute(array, axis, [(here, (here + offset) % count) for here in range(count)])


def gelu_parts(value):
    root = math.sqrt(2.0 / math.pi)
    square = value * value
    tanh_part = jnp.tanh(root * (value + 0.044715 * value * square))
    gelu = 0.5 * value * (1.0 + tanh_part)
    slope = 0.5 * (1.0 + tanh_part) + 0.5 * value * (1.0 - tanh_part * tanh_part) * root * (
        1.0 + 3.0 * 0.044715 * square
    )
    return gelu, slope


def mlp_forward_kernel(rows_ref, gate_ref, up_ref, down_ref, gate_pre_ref, up_pre_ref, hidden_ref, part_ref):
    rows = rows_ref[...]
    gate_pre = rows_dot(rows, gate_ref[...], 1, 1)
    up_pre = rows_dot(rows, up_ref[...], 1, 1)
    gate_pre_ref[...] = gate_pre
    up_pre_ref[...] = up_pre
    hidden = (gelu_parts(gate_pre)[0] * up_pre).astype(jnp.bfloat16)
    hidden_ref[...] = hidden
    part_ref[...] = rows_dot(hidden, down_ref[...], 1, 0).astype(jnp.bfloat16)


def mlp_backward_kernel(
    rows_ref, gate_ref, up_ref, down_ref, gate_pre_ref, up_pre_ref, grad_gate_ref, grad_up_ref, part_ref
):
    grad_hidden = rows_dot(rows_ref[...], down_ref[...], 1, 1)
    gelu, slope = gelu_parts(gate_pre_ref[...])
    grad_gate = (grad_hidden * up_pre_ref[...] * slope).astype(jnp.bfloat16)
    grad_up = (grad_hidden * gelu).astype(jnp.bfloat16)
    grad_gate_ref[...] = grad_gate
    grad_up_ref[...] = grad_up
    part_ref[...] = (
        rows_dot(grad_gate, gate_ref[...], 1, 0) + rows_dot(grad_up, up_ref[...], 1, 0)
    ).astype(jnp.bfloat16)


def rows_dot(left, right, left_dim, right_dim):
    return lax.dot_general(
        left, right, (((left_dim,), (right_dim,)), ((), ())), preferred_element_type=jnp.float32
    )


def add_up(blocks):
    return jnp.sum(blocks.astype(jnp.float32), axis=0)


def local(
    block_in,
    cotangent,
    positions,
    norm_gains,
    qk_gains,
    w_query,
    w_key,
    w_value,
    w_out,
    w_gate,
    w_up,
    w_down,
):
    tok_rows, model_width = block_in.shape
    head_count = lax.axis_size("head")
    head_width = qk_gains.shape[1]
    ctx_slot = lax.axis_index("ctx")
    query_rows = head_count * tok_rows
    group_count = lax.axis_size(weight_axes)
    every_count = lax.axis_size(every_axis)
    length_all = lax.axis_size(sequence_axes) * tok_rows
    query_cols = w_query.shape[1]
    key_cols = w_key.shape[1]
    ff_cols = w_gate.shape[1]
    narrow = jnp.bfloat16

    ff_rows = jnp.concatenate([w_gate.T, w_up.T, w_down], axis=0)
    dp_count, ctx_count = lax.axis_size("dp"), lax.axis_size("ctx")

    to_heads = [
        (head * group_count + index, index * head_count + head)
        for head in range(head_count)
        for index in range(group_count)
    ]
    to_owners = [(there, here) for here, there in to_heads]
    head_rows = lax.ppermute(
        jnp.concatenate([w_query.T, w_out], axis=0), every_axis, to_heads
    )
    key_value_rows = jnp.concatenate([w_key.T, w_value.T], axis=0)
    block_all, key_value_all, head_all, position_all = staged_gather(
        1,
        "first_gather",
        [
            (("ctx", "head_slow", "head_fast"), block_in),
            (("dp", "ctx", "head_slow", "head_fast"), key_value_rows),
            (("dp", "ctx"), head_rows),
            (("ctx",), positions.reshape(-1, 128)),
        ],
    )
    block_all, ff_rows = lax.optimization_barrier((block_all, ff_rows))
    near_blocks = [ff_rows] + [shifted(ff_rows, "dp", offset) for offset in range(1, dp_count)]
    ff_across = [shifted(ff_rows, "ctx", offset) for offset in range(1, ctx_count)]
    block_all = block_all.transpose(2, 1, 0, 3, 4)
    key_value_all = key_value_all.transpose(3, 2, 1, 0, 4, 5).reshape(
        every_count, 2 * key_cols, model_width
    )
    head_all = head_all.transpose(1, 0, 2, 3).reshape(group_count, 2 * query_cols, model_width)
    query_weight = head_all[:, :query_cols].reshape(head_width, model_width)
    out_weight = head_all[:, query_cols:].reshape(head_width, model_width)
    key_weight = key_value_all[:, :key_cols].reshape(head_width, model_width)
    value_weight = key_value_all[:, key_cols:].reshape(head_width, model_width)

    input_all = block_all.reshape(length_all, model_width).astype(jnp.float32)
    attn_in_all = norm_rows(input_all, norm_gains[0])[0].astype(narrow)
    first_query = ctx_slot * query_rows
    attn_in = lax.dynamic_slice_in_dim(attn_in_all, first_query, query_rows)
    query_raw = rows_dot(attn_in, query_weight, 1, 1)
    key_raw = rows_dot(attn_in_all, key_weight, 1, 1)
    all_values = rows_dot(attn_in_all, value_weight, 1, 1).astype(narrow)
    query_normed, inverse_query = norm_rows(query_raw, qk_gains[0])
    key_normed, inverse_key = norm_rows(key_raw, qk_gains[1])
    cosine, sine_part = rope_angles(position_all.reshape(length_all), head_width)
    cosine_own = lax.dynamic_slice_in_dim(cosine, first_query, query_rows)
    sine_own = lax.dynamic_slice_in_dim(sine_part, first_query, query_rows)
    head_query = (rotate(query_normed, cosine_own, sine_own) * score_scale).astype(narrow)
    all_keys = rotate(key_normed, cosine, sine_part).astype(narrow)

    query_index = first_query + jnp.arange(query_rows, dtype=jnp.int32)
    lowest_key = query_index - positions
    key_index = jnp.arange(length_all, dtype=jnp.int32)
    visible = (key_index[None, :] <= query_index[:, None]) & (
        key_index[None, :] >= lowest_key[:, None]
    )
    scores = jnp.where(visible, rows_dot(head_query, all_keys, 1, 1), negative_fill)
    top = jnp.max(scores, axis=1, keepdims=True)
    log_total = top + jnp.log(jnp.sum(jnp.exp(scores - top), axis=1, keepdims=True))
    probs_wide = jnp.exp(scores - log_total)
    prob_rows = probs_wide.astype(narrow)
    attn_exact = rows_dot(prob_rows, all_values, 1, 0)
    attn_out = attn_exact.astype(narrow)
    branch_part = rows_dot(attn_out, out_weight, 1, 0).astype(narrow)
    (branch_blocks,) = exchange(
        2,
        "branch_scatter",
        [("scatter", ("head",), branch_part.reshape(head_count, tok_rows, model_width))],
    )
    branch = add_up(branch_blocks)
    input_wide = block_in.astype(jnp.float32)
    inverse_in = norm_rows(input_wide, norm_gains[0])[1]
    branch_normed, inverse_branch = norm_rows(branch, norm_gains[1])
    middle = input_wide + branch_normed
    mlp_norm, inverse_mid = norm_rows(middle, norm_gains[2])
    mlp_norm, near_blocks, ff_across = lax.optimization_barrier((mlp_norm, near_blocks, ff_across))
    ff_slots = list(near_blocks)
    for offset in range(1, ctx_count):
        ff_slots += [ff_across[offset - 1]]
        ff_slots += [shifted(block, "ctx", offset) for block in near_blocks[1:]]
    mlp_in = gather_rows(3, "mlp_gather", mlp_norm.astype(narrow))

    ff_width = group_count * ff_cols
    gate_weight = jnp.concatenate([block[:ff_cols] for block in ff_slots], axis=0)
    up_weight = jnp.concatenate([block[ff_cols : 2 * ff_cols] for block in ff_slots], axis=0)
    down_weight = jnp.concatenate([block[2 * ff_cols :] for block in ff_slots], axis=0)
    wide_ff = jax.ShapeDtypeStruct((query_rows, ff_width), jnp.float32)
    narrow_ff = jax.ShapeDtypeStruct((query_rows, ff_width), narrow)
    narrow_rows = jax.ShapeDtypeStruct((query_rows, model_width), narrow)
    gate_pre, up_pre, hidden, down_part = pl.pallas_call(
        mlp_forward_kernel,
        out_shape=[wide_ff, wide_ff, narrow_ff, narrow_rows],
        name="mlp_forward",
    )(mlp_in, gate_weight, up_weight, down_weight)
    (down_blocks,) = exchange(
        4,
        "down_scatter",
        [("scatter", ("head",), down_part.reshape(head_count, tok_rows, model_width))],
    )
    down_raw = add_up(down_blocks)
    down_normed, inverse_down = norm_rows(down_raw, norm_gains[3])
    block_out = (middle + down_normed).astype(narrow)
    cot_wide = cotangent.astype(jnp.float32)
    grad_down_raw, gain_three = norm_back(down_raw, inverse_down, norm_gains[3], cot_wide)
    grad_down_in = gather_rows(5, "grad_down_gather", grad_down_raw.astype(narrow))
    grad_gate_in, grad_up_in, grad_mlp_part = pl.pallas_call(
        mlp_backward_kernel,
        out_shape=[narrow_ff, narrow_ff, narrow_rows],
        name="mlp_backward",
    )(grad_down_in, gate_weight, up_weight, down_weight, gate_pre, up_pre)
    slots = (ctx_count, dp_count, ff_cols, model_width)
    ff_terms = jnp.concatenate(
        [
            rows_dot(grad_gate_in, mlp_in, 0, 0).astype(narrow).reshape(slots),
            rows_dot(grad_up_in, mlp_in, 0, 0).astype(narrow).reshape(slots),
            rows_dot(hidden, grad_down_in, 0, 0).astype(narrow).reshape(slots),
        ],
        axis=2,
    )
    half = dp_count // 2
    grad_mlp_blocks, ff_early = exchange(
        6,
        "grad_mlp_scatter",
        [
            (
                "scatter",
                ("head",),
                grad_mlp_part.reshape(head_count, tok_rows, model_width),
            ),
            ("relative", ("ctx",), ff_terms[:, :half]),
        ],
        (("head",), ("ctx",)),
    )
    grad_mlp_in = add_up(grad_mlp_blocks)
    grad_mid_part, gain_two = norm_back(middle, inverse_mid, norm_gains[2], grad_mlp_in)
    grad_middle = cot_wide + grad_mid_part
    grad_branch_raw, gain_one = norm_back(branch, inverse_branch, norm_gains[1], grad_middle)
    grad_branch_blocks, ff_late = exchange(
        7,
        "grad_branch_gather",
        [
            ("gather", ("head",), grad_branch_raw.astype(narrow)),
            ("relative", ("ctx",), ff_terms[:, half:]),
        ],
        (("head",), ("ctx",)),
    )
    grad_branch = grad_branch_blocks.reshape(query_rows, model_width)
    ff_sums = jnp.concatenate([add_up(ff_early), add_up(ff_late)], axis=0).astype(narrow)
    head_grad = rows_dot(grad_branch, out_weight, 1, 1).astype(narrow)
    row_delta = jnp.sum(head_grad.astype(jnp.float32) * attn_exact, axis=1, keepdims=True)
    grad_probs = rows_dot(head_grad, all_values, 1, 1)
    grad_scores = (probs_wide * (grad_probs - row_delta)).astype(narrow)
    value_sums = rows_dot(prob_rows, head_grad, 0, 0)
    key_sums = rows_dot(grad_scores, head_query, 0, 0)
    grad_rot_query = rows_dot(grad_scores, all_keys, 1, 0)
    query_back = rotate(grad_rot_query * score_scale, cosine_own, -sine_own)
    grad_query_raw, gain_query = norm_back(query_raw, inverse_query, qk_gains[0], query_back)
    key_back = rotate(key_sums, cosine, -sine_part)
    grad_key_raw, gain_key = norm_back(key_raw, inverse_key, qk_gains[1], key_back)
    grad_query_in = grad_query_raw.astype(narrow)
    grad_key_in = grad_key_raw.astype(narrow)
    grad_value_in = value_sums.astype(narrow)
    grad_attn_part = rows_dot(grad_key_in, key_weight, 1, 0) + rows_dot(
        grad_value_in, value_weight, 1, 0
    )
    own_part = lax.dynamic_slice_in_dim(grad_attn_part, first_query, query_rows) + rows_dot(
        grad_query_in, query_weight, 1, 0
    )
    grad_attn_part = lax.dynamic_update_slice_in_dim(grad_attn_part, own_part, first_query, 0)
    head_terms = jnp.concatenate(
        [
            rows_dot(grad_query_in, attn_in, 0, 0).reshape(group_count, query_cols, model_width),
            rows_dot(attn_out, grad_branch, 0, 0).reshape(group_count, query_cols, model_width),
        ],
        axis=1,
    ).astype(narrow)
    planes = (dp_count, every_count // dp_count, key_cols, model_width)
    key_value_terms = jnp.concatenate(
        [
            rows_dot(grad_key_in, attn_in_all, 0, 0).reshape(planes),
            rows_dot(grad_value_in, attn_in_all, 0, 0).reshape(planes),
        ],
        axis=2,
    ).astype(narrow).transpose(1, 0, 2, 3)
    head_terms = head_terms.reshape(dp_count, ctx_count, 2 * query_cols, model_width)
    grad_attn_blocks, head_blocks, key_value_blocks, ff_blocks = exchange(
        8,
        "last_scatter",
        [
            (
                "scatter",
                sequence_axes,
                grad_attn_part.astype(narrow).reshape(-1, tok_rows, model_width),
            ),
            ("scatter", ("ctx",), head_terms.transpose(1, 0, 2, 3)),
            ("scatter", sequence_axes, key_value_terms),
            ("relative", ("dp",), ff_sums),
        ],
        (sequence_axes, ("dp",)),
    )
    ff_own = add_up(ff_blocks)
    grad_attn_in = add_up(grad_attn_blocks)
    grad_in_part, gain_zero = norm_back(input_wide, inverse_in, norm_gains[0], grad_attn_in)
    d_block_in = (grad_middle + grad_in_part).astype(narrow)

    pad = ((0, 0), (0, model_width - head_width))
    gain_terms = jnp.concatenate(
        [
            jnp.sum(gain_zero, axis=0, keepdims=True),
            jnp.sum(gain_one, axis=0, keepdims=True),
            jnp.sum(gain_two, axis=0, keepdims=True),
            jnp.sum(gain_three, axis=0, keepdims=True),
            jnp.pad(jnp.sum(gain_query, axis=0, keepdims=True), pad),
            jnp.pad(jnp.sum(gain_key, axis=0, keepdims=True), pad),
            jnp.zeros((2, model_width), jnp.float32),
        ],
        axis=0,
    )
    gain_blocks, head_blocks, key_value_blocks = exchange(
        9,
        "depth_exchange",
        [
            ("gather", ("dp",), gain_terms),
            ("scatter", ("dp",), add_up(head_blocks).astype(narrow)),
            ("scatter", ("dp",), add_up(key_value_blocks).astype(narrow)),
        ],
    )
    head_own = lax.ppermute(add_up(head_blocks).astype(narrow), every_axis, to_owners).astype(
        jnp.float32
    )
    (gain_blocks,) = exchange(10, "gain_gather", [("gather", sequence_axes, add_up(gain_blocks))])
    gains = add_up(gain_blocks)
    key_value_own = add_up(key_value_blocks)
    return (
        block_out,
        d_block_in,
        gains[:4],
        gains[4:6, :head_width],
        head_own[:query_cols].T,
        key_value_own[:key_cols].T,
        key_value_own[key_cols:].T,
        head_own[query_cols:],
        ff_own[:ff_cols].T,
        ff_own[ff_cols : 2 * ff_cols].T,
        ff_own[2 * ff_cols :],
    )


bits = (0, 1)


class Mail:
    def __init__(self, send_sems, recv_sems):
        self.send_sems, self.recv_sems = send_sems, recv_sems
        self.started = []

    def push(self, source, target, to, when=None, arrives_as=None):
        number = len(self.started)
        copy = pltpu.make_async_remote_copy(
            src_ref=source,
            dst_ref=target,
            send_sem=self.send_sems.at[number],
            recv_sem=self.recv_sems.at[number if arrives_as is None else arrives_as],
            device_id=to,
            device_id_type=pl.DeviceIdType.MESH,
        )
        if when is None:
            copy.start()
        else:
            pl.when(when)(copy.start)
        self.started.append((copy, when))
        return copy

    def settle(self):
        for copy, when in self.started:
            if when is None:
                copy.wait_send()
            else:
                pl.when(when)(copy.wait_send)


copy_limit = 176


def fused_kernel(names, *refs):
    r = types.SimpleNamespace(**dict(zip(names, refs)))
    narrow, wide = jnp.bfloat16, jnp.float32
    d, x, h = lax.axis_index("dp"), lax.axis_index("ctx"), lax.axis_index("head")
    depth = lax.axis_size("dp")
    y, c = h // 2, lax.rem(h, 2)
    me = x * 4 + h
    mail = Mail(r.send_sems, r.recv_sems)
    rows, width = r.block_in.shape
    head_width = r.qk_gains.shape[1]
    half_width = head_width // 2
    heads, query_cols = r.q_raw.shape[1] // head_width, r.q_rows.shape[0]
    key_cols = r.key_rows.shape[0]
    ff_cols = r.gate_rows.shape[0]
    all_rows = 8 * rows
    full = heads * head_width

    def deep(offset):
        return lax.rem(d + offset, depth)

    def z_peer(offset):
        return {"dp": deep(offset)}

    x_peer = {"ctx": 1 - x}
    y_peer = {"head": (1 - y) * 2 + c}
    c_peer = {"head": y * 2 + 1 - c}

    def flip(place, bit):
        return 1 - place if bit else place

    def plane_peer(dx, dy, dc):
        return {"ctx": flip(x, dx), "head": flip(y, dy) * 2 + flip(c, dc)}

    plane_steps = [(dx, dy, dc) for dx in bits for dy in bits for dc in bits][1:]
    chip_steps = [(0, 1), (1, 0), (1, 1)]

    barrier = pltpu.get_barrier_semaphore()
    greeted = [z_peer(offset) for offset in range(1, depth)] + [plane_peer(*s) for s in plane_steps]
    for peer in greeted:
        pl.semaphore_signal(barrier, inc=1, device_id=peer, device_id_type=pl.DeviceIdType.MESH)
    r.block_all[x, y, c] = r.block_in[...]
    key_value = [r.key_rows[...].astype(wide), r.value_rows[...].astype(wide)]
    r.kv_all[d, x, y, c] = jnp.concatenate(key_value, axis=0).astype(narrow)
    r.q_all[d, x, y, c] = r.q_rows[...]
    r.o_all[d, x, y, c] = r.o_rows[...]
    for piece, own in enumerate((r.gate_rows, r.up_rows, r.down_rows)):
        r.ff_all[d, x, pl.ds(piece * ff_cols, ff_cols)] = own[...]
    r.pos_pair[x] = r.positions[...].astype(wide)
    pl.semaphore_wait(barrier, len(greeted))

    got_z, got_x, got_y, got_c = {}, {}, {}, {}

    def place(part):
        return (x, y, c) if part == "block" else (d, x, y, c)

    def source(part):
        return getattr(r, part + "_all").at[place(part)]

    def own_to_x(part):
        got_x[part, 0] = mail.push(source(part), getattr(r, part + "_all").at[place(part)], x_peer)

    def own_to_y(part):
        got_y[part, 0] = [
            mail.push(source(part), getattr(r, part + "_all").at[place(part)], y_peer)
        ]

    relayed = depth >= 4
    relays = ((depth - 1, 2, 0), (1, depth - 3, depth - 1)) if relayed else ()
    z_order = sorted(range(1, depth), key=lambda offset: offset != 2)

    def blocks_to_z(key, block_of):
        for offset in range(1, depth):
            when = None
            if relayed and offset == 1:
                when = d < depth - 1
            if relayed and offset == depth - 1:
                when = d > 0
            number = len(mail.started)
            copy = mail.push(block_of(d), block_of(d), z_peer(offset), when)
            got_z[key, offset] = copy, number

    def blocks_to_x(key, block_of):
        for offset in z_order:
            got_z[key, offset][0].wait_recv()
            block = block_of(deep(depth - offset))
            if offset == 2:
                for other, relay, _ in relays:
                    to = {"dp": lax.rem(d + depth - 2 + other, depth)}
                    mail.push(block, block, to, d == relay, got_z[key, other][1])
            got_x[key, offset] = mail.push(block, block, x_peer)

    def block_of(part):
        return lambda slot: getattr(r, part + "_all").at[(slot,) + place(part)[1:]]

    def own_to_z(part):
        blocks_to_z(part, block_of(part))

    def to_x(part):
        blocks_to_x(part, block_of(part))

    def near_to_y(part):
        got_x[part, 0].wait_recv()
        at = (1 - x, y, c) if part == "block" else (d, 1 - x, y, c)
        block = getattr(r, part + "_all").at[at]
        got_y[part, 0].append(mail.push(block, block, y_peer))

    def to_y(part):
        for offset in range(1, depth):
            got_x[part, offset].wait_recv()
            block = getattr(r, part + "_all").at[deep(depth - offset), :, y, c]
            got_y[part, offset] = [mail.push(block, block, y_peer)]

    def to_c(part):
        for offset in range(1 if part == "block" else depth):
            for copy in got_y[part, offset]:
                copy.wait_recv()
            block = getattr(r, part + "_all")
            block = block if part == "block" else block.at[deep(depth - offset)]
            block = block.at[:, :, c]
            got_c[part, offset] = mail.push(block, block, c_peer)

    def arrived(part):
        for offset in range(1 if part == "block" else depth):
            got_c[part, offset].wait_recv()

    def ff_piece(slot, piece):
        return r.ff_all.at[slot, x, pl.ds(piece * ff_cols, ff_cols)]

    def ff_to_z(piece):
        blocks_to_z(("ff", piece), lambda slot: ff_piece(slot, piece))

    def ff_own_to_x():
        block = r.ff_all.at[d, x]
        got_x["ff", 0] = mail.push(block, block, x_peer)

    def ff_to_x(piece):
        blocks_to_x(("ff", piece), lambda slot: ff_piece(slot, piece))

    position_copy = mail.push(r.pos_pair.at[x], r.pos_pair.at[x], x_peer)
    for part in ("kv", "block", "q", "o"):
        own_to_x(part)
        own_to_y(part)
        if part != "block":
            own_to_z(part)

    def rope_tables():
        position_copy.wait_recv()
        for half in bits:
            r.pos_all[half * 4 : half * 4 + 4] = r.pos_pair[half]
        turned = r.pos_all[...].T
        ladder = lax.broadcasted_iota(jnp.int32, (1, half_width), 1).astype(wide)
        frequency = jnp.exp(ladder * (-2.0 / head_width) * math.log(rope_base))
        column = lax.broadcasted_iota(jnp.int32, turned.shape, 1)
        r.pos_own[...] = jnp.sum(jnp.where(column == me, turned, 0.0), axis=1, keepdims=True)
        for block in range(8):
            angle = turned[:, block : block + 1] * frequency
            r.cosine[block] = jnp.cos(angle)
            r.sine[block] = jnp.sin(angle)

    def shuffle():
        size = 2 * head_width
        there = lax.broadcasted_iota(jnp.int32, (size, size), 1).astype(wide)
        here = lax.broadcasted_iota(jnp.int32, (size, size), 0).astype(wide)

        def sorted_place(place):
            block = jnp.floor((place + 0.5) / (2 * key_cols))
            inside = place - block * (2 * key_cols)
            value = inside >= key_cols
            return block * key_cols + jnp.where(value, inside - key_cols + head_width, inside)

        r.unsort[...] = jnp.where(sorted_place(here) == there, 1.0, 0.0).astype(narrow)
        r.sort[...] = jnp.where(sorted_place(there) == here, 1.0, 0.0).astype(narrow)

    def attention_inputs():
        arrived("block")
        gain = r.norm_gains[0:1]
        for px in bits:
            for py in bits:
                for pc in bits:
                    values = r.block_all[px, py, pc].astype(wide)
                    r.attn_in[px * 4 + py * 2 + pc] = norm_rows(values, gain)[0].astype(narrow)

    def keys_and_values():
        arrived("kv")
        blocks = r.kv_all[...].reshape(2 * head_width, width)
        r.kv_sorted[...] = rows_dot(r.sort[...], blocks, 1, 0).astype(narrow)
        gain = r.qk_gains[1:2]
        for pair in range(4):
            two = pl.ds(2 * pair, 2)
            inputs = r.attn_in[two].reshape(2 * rows, width)
            raw = rows_dot(inputs, r.kv_sorted[...], 1, 1)
            key_raw = raw[:, :head_width]
            r.key_raw[two] = key_raw.reshape(2, rows, head_width)
            cosine = r.cosine[two].reshape(2 * rows, half_width)
            sine_part = r.sine[two].reshape(2 * rows, half_width)
            turned = rotate(norm_rows(key_raw, gain)[0], cosine, sine_part)
            r.keys[pl.ds(2 * pair * rows, 2 * rows)] = turned.astype(narrow)
            r.values[pl.ds(2 * pair * rows, 2 * rows)] = raw[:, head_width:].astype(narrow)

    shuffle()
    rope_tables()
    to_x("kv")
    near_to_y("kv")
    near_to_y("block")
    ff_to_z(0)
    to_x("q")
    near_to_y("q")
    to_y("kv")
    ff_to_z(1)
    ff_own_to_x()
    to_x("o")
    near_to_y("o")
    to_y("q")
    ff_to_z(2)
    to_c("block")
    attention_inputs()
    ff_to_x(0)
    to_c("kv")
    to_y("o")
    keys_and_values()
    ff_to_x(1)
    to_c("q")

    query_gain = r.qk_gains[0:1]
    arrived("q")
    weight = r.q_all[...].reshape(full, width)
    r.q_raw[...] = rows_dot(r.attn_in[me], weight, 1, 1)
    for head in range(heads):
        turned = rotate(
            norm_rows(r.q_raw[:, head * head_width : (head + 1) * head_width], query_gain)[0],
            r.cosine[me],
            r.sine[me],
        )
        r.q_rot[head] = (turned * score_scale).astype(narrow)
    to_c("o")
    ff_to_x(2)

    query_index = lax.broadcasted_iota(jnp.int32, (rows, all_rows), 0) + me * rows
    key_index = lax.broadcasted_iota(jnp.int32, (rows, all_rows), 1)
    lowest_key = query_index - r.pos_own[...].astype(jnp.int32)
    visible = (key_index <= query_index) & (key_index >= lowest_key)
    r.bias[...] = jnp.where(visible, 0.0, negative_fill)
    for head in range(heads):
        scores = rows_dot(r.q_rot[head], r.keys[...], 1, 1)
        scores = jnp.where(r.bias[...] < 0.0, negative_fill, scores)
        top = jnp.max(scores, axis=1, keepdims=True)
        raised = jnp.exp(scores - top)
        prob_rows = raised * (1.0 / jnp.sum(raised, axis=1, keepdims=True))
        r.probs[head] = prob_rows
        r.probs_narrow[head] = prob_rows.astype(narrow)
        exact = rows_dot(prob_rows.astype(narrow), r.values[...], 1, 0)
        r.exact[head] = exact
        r.attn_out[:, head * head_width : (head + 1) * head_width] = exact.astype(narrow)
    arrived("o")
    out_weight = r.o_all[...].reshape(full, width)
    r.branch[...] = rows_dot(r.attn_out[...], out_weight, 1, 0)
    def send_factor(name):
        copies = []
        for step in plane_steps:
            px, py, pc = (flip(place, bit) for place, bit in zip((x, y, c), step))
            copies.append(
                mail.push(getattr(r, name).at[:, px, py, pc], getattr(r, name + "_got").at[me], plane_peer(*step))
            )
        getattr(r, name + "_got")[me] = getattr(r, name)[:, x, y, c]
        return copies

    def turned_blocks(name, values, columns):
        getattr(r, name)[...] = values.astype(wide).T.astype(narrow).reshape(depth, 2, 2, 2, columns, rows)

    input_wide = r.block_in[...].astype(wide)
    branch_normed = norm_rows(r.branch[...], r.norm_gains[1:2])[0]
    r.middle[...] = input_wide + branch_normed
    mlp_rows = norm_rows(r.middle[...], r.norm_gains[2:3])[0].astype(narrow)

    def share_rows(name, values):
        getattr(r, name)[y, c] = values
        block = getattr(r, name).at[y, c]
        return mail.push(block, block, c_peer), mail.push(block, block, y_peer)

    def far_rows(name, from_y):
        from_y.wait_recv()
        block = getattr(r, name).at[1 - y, c]
        return mail.push(block, block, c_peer)

    def fetch_ff():
        got_x["ff", 0].wait_recv()
        for piece in range(3):
            for offset in range(1, depth):
                got_x[("ff", piece), offset].wait_recv()

    def ff_part(index):
        piece = r.ff_all[:, :, pl.ds(index * ff_cols, ff_cols)]
        return piece.reshape(2 * depth * ff_cols, width)

    def group_sum(name, half, own_rows, between):
        part, near, far = getattr(r, name), getattr(r, name + "_near"), getattr(r, name + "_far")
        from_c, from_y, forwarded = own_rows
        from_c.wait_recv()
        half(y)
        near_own = mail.push(part.at[y, 1 - c], near.at[0], c_peer)
        if forwarded is None:
            forwarded = from_y()
        forwarded.wait_recv()
        half(1 - y)
        near_far = mail.push(part.at[1 - y, 1 - c], near.at[1], c_peer)
        near_far.wait_recv()
        summed = part[1 - y, c].astype(wide) + near[1].astype(wide)
        getattr(r, name + "_sum")[...] = summed.astype(narrow)
        far_copy = mail.push(getattr(r, name + "_sum"), far, y_peer)
        between()
        near_own.wait_recv()
        own = part[y, c].astype(wide) + near[0].astype(wide)
        far_copy.wait_recv()
        return own + far[...].astype(wide)

    def forward_half(side):
        inputs = r.mlp_in[side].reshape(2 * rows, width)
        gate_pre = rows_dot(inputs, ff_part(0), 1, 1)
        up_pre = rows_dot(inputs, ff_part(1), 1, 1)
        r.gate_pre[side] = gate_pre
        r.up_pre[side] = up_pre
        hidden = (gelu_parts(gate_pre)[0] * up_pre).astype(narrow)
        r.hidden[side] = hidden
        part = rows_dot(hidden, ff_part(2), 1, 0).astype(narrow)
        r.down[side] = part.reshape(2, rows, width)

    near_copy, y_copy = share_rows("mlp_in", mlp_rows)
    turned_blocks("out_turned", r.attn_out[...], query_cols)
    out_copies = send_factor("out_turned")
    fetch_ff()
    r.down_raw[...] = group_sum(
        "down", forward_half, (near_copy, lambda: far_rows("mlp_in", y_copy), None), lambda: None
    )
    down_raw = r.down_raw[...]
    down_normed, inverse_down = norm_rows(down_raw, r.norm_gains[3:4])
    r.block_out[...] = (r.middle[...] + down_normed).astype(narrow)
    cot_wide = r.cotangent[...].astype(wide)
    grad_down_raw, gain_three = norm_back(down_raw, inverse_down, r.norm_gains[3:4], cot_wide)
    r.gains[...] = jnp.zeros_like(r.gains)
    r.gains[3:4] = jnp.sum(gain_three, axis=0, keepdims=True)

    def backward_half(side):
        grad_hidden = rows_dot(r.grad_down[side].reshape(2 * rows, width), ff_part(2), 1, 1)
        gelu, slope = gelu_parts(r.gate_pre[side])
        grad_gate = (grad_hidden * r.up_pre[side] * slope).astype(narrow)
        grad_up = (grad_hidden * gelu).astype(narrow)
        r.grad_gate[side] = grad_gate
        r.grad_up[side] = grad_up
        part = rows_dot(grad_gate, ff_part(0), 1, 0) + rows_dot(grad_up, ff_part(1), 1, 0)
        r.mlp_back[side] = part.astype(narrow).reshape(2, rows, width)

    ff_width = 2 * depth * ff_cols

    def ff_terms(index, left, right):
        terms = rows_dot(getattr(r, left)[...].reshape(4 * rows, ff_width), getattr(r, right)[...].reshape(4 * rows, width), 0, 0)
        r.ff_terms[:, :, pl.ds(index * ff_cols, ff_cols)] = terms.astype(narrow).reshape(
            depth, 2, ff_cols, width
        )

    ff_across = []

    def ff_terms_to_x(offset):
        ff_across.append(mail.push(r.ff_terms.at[deep(offset), 1 - x], r.ff_near.at[offset], x_peer))

    def all_ff_terms():
        ff_terms(2, "hidden", "grad_down")
        ff_terms(0, "grad_gate", "mlp_in")
        ff_terms(1, "grad_up", "mlp_in")
        for offset in range(1, depth):
            ff_terms_to_x(offset)

    near_copy, y_copy = share_rows("grad_down", grad_down_raw.astype(narrow))
    grad_mlp_in = group_sum(
        "mlp_back",
        backward_half,
        (near_copy, lambda: far_rows("grad_down", y_copy), None),
        all_ff_terms,
    )
    middle = r.middle[...]
    inverse_mid = norm_rows(middle, r.norm_gains[2:3])[1]
    grad_mid_part, gain_two = norm_back(middle, inverse_mid, r.norm_gains[2:3], grad_mlp_in)
    r.gains[2:3] = jnp.sum(gain_two, axis=0, keepdims=True)
    grad_middle = r.cotangent[...].astype(wide) + grad_mid_part
    r.grad_middle[...] = grad_middle
    branch = r.branch[...]
    inverse_branch = norm_rows(branch, r.norm_gains[1:2])[1]
    grad_branch_raw, gain_one = norm_back(branch, inverse_branch, r.norm_gains[1:2], grad_middle)
    r.gains[1:2] = jnp.sum(gain_one, axis=0, keepdims=True)
    grad_branch = grad_branch_raw.astype(narrow)
    branch_all = r.branch_all
    branch_all[x, y, c] = grad_branch
    block = branch_all.at[x, y, c]
    branch_x = mail.push(block, block, x_peer)
    branch_y = [mail.push(block, block, y_peer)]

    head_grad = rows_dot(grad_branch, out_weight, 1, 1).astype(narrow)
    for head in range(heads):
        r.head_grad[head] = head_grad[:, head * head_width : (head + 1) * head_width]

    ff_deep = []

    def ff_step(number):
        ff_across[number].wait_recv()
        offset = number + 1 if number < depth - 1 else 0
        summed = r.ff_terms[deep(offset), x].astype(wide) + r.ff_near[offset].astype(wide)
        if offset:
            r.ff_sum[offset] = summed.astype(narrow)
            ff_deep.append(
                mail.push(r.ff_sum.at[offset], r.ff_got.at[offset], z_peer(offset))
            )
        else:
            r.ff_own[...] = summed

    for head in range(heads):
        grad_rows = r.head_grad[head]
        delta = jnp.sum(grad_rows.astype(wide) * r.exact[head], axis=1, keepdims=True)
        grad_probs = rows_dot(grad_rows, r.values[...], 1, 1)
        r.grad_scores[head] = (r.probs[head] * (grad_probs - delta)).astype(narrow)
    ff_step(0)
    all_grads = r.head_grad[...].reshape(heads * rows, head_width)
    all_queries = r.q_rot[...].reshape(heads * rows, head_width)
    for pair in range(4):
        here = slice(2 * pair * rows, 2 * (pair + 1) * rows)
        px, py = pair // 2, pair % 2
        key_part = rows_dot(
            r.grad_scores[:, :, here].reshape(heads * rows, 2 * rows), all_queries, 0, 0
        )
        value_part = rows_dot(
            r.probs_narrow[:, :, here].reshape(heads * rows, 2 * rows), all_grads, 0, 0
        )
        r.kv_terms[px, py, :, :, :head_width] = key_part.astype(narrow).reshape(2, rows, head_width)
        r.kv_terms[px, py, :, :, head_width:] = value_part.astype(narrow).reshape(2, rows, head_width)
    kv_near = mail.push(r.kv_terms.at[:, :, 1 - c], r.kv_near, c_peer)

    cosine, sine_part = r.cosine[me], r.sine[me]
    gain_query = jnp.zeros((1, head_width), wide)
    for head in range(heads):
        here = slice(head * head_width, (head + 1) * head_width)
        turned = rows_dot(r.grad_scores[head], r.keys[...], 1, 0) * score_scale
        upstream = rotate(turned, cosine, -sine_part)
        query_raw = r.q_raw[:, here]
        inverse = norm_rows(query_raw, query_gain)[1]
        grad_raw, gain_rows = norm_back(query_raw, inverse, query_gain, upstream)
        gain_query += jnp.sum(gain_rows, axis=0, keepdims=True)
        r.grad_query[:, here] = grad_raw.astype(narrow)
    r.gains[4:5, :head_width] = gain_query

    kv_near.wait_recv()
    for px in bits:
        for py in bits:
            summed = r.kv_terms[px, py, c].astype(wide) + r.kv_near[px, py].astype(wide)
            r.kv_sums[px, py] = summed.astype(narrow)
    kv_copies = []
    for number, (dx, dy) in enumerate(chip_steps):
        kv_copies.append(
            mail.push(
                r.kv_sums.at[flip(x, dx), flip(y, dy)], r.kv_far.at[number], plane_peer(dx, dy, 0)
            )
        )
    turned_blocks("query_turned", r.grad_query[...], query_cols)
    query_copies = send_factor("query_turned")
    ff_terms_to_x(0)
    ff_step(1)
    branch_x.wait_recv()
    block = branch_all.at[1 - x, y, c]
    branch_y.append(mail.push(block, block, y_peer))
    query_part = rows_dot(r.grad_query[...], r.q_all[...].reshape(full, width), 1, 0)
    r.query_part[...] = query_part

    def weight_terms(name, copies, source, columns):
        for copy in copies:
            copy.wait_recv()
        terms = jnp.zeros((depth * columns, width), wide)
        for block in range(8):
            left = getattr(r, name + "_got")[block].reshape(depth * columns, rows)
            right = source(block)
            terms += rows_dot(left, right, 1, 0)
        getattr(r, name + "_wide")[...] = terms.reshape(depth, columns, width)
        getattr(r, name + "_terms")[...] = terms.astype(narrow).reshape(depth, columns, width)
        return [
            mail.push(getattr(r, name + "_terms").at[deep(offset)], getattr(r, name + "_far").at[offset], z_peer(offset))
            for offset in range(1, depth)
        ]

    ff_step(2)
    for copy in kv_copies:
        copy.wait_recv()
    kv_sum = r.kv_sums[x, y].astype(wide)
    for number in range(len(chip_steps)):
        kv_sum += r.kv_far[number].astype(wide)
    key_gain = r.qk_gains[1:2]
    key_raw = r.key_raw[me]
    key_back = rotate(kv_sum[:, :head_width], cosine, -sine_part)
    inverse_key = norm_rows(key_raw, key_gain)[1]
    grad_key_raw, gain_key = norm_back(key_raw, inverse_key, key_gain, key_back)
    r.gains[5:6, :head_width] = jnp.sum(gain_key, axis=0, keepdims=True)
    r.grad_kv[:, :head_width] = grad_key_raw.astype(narrow)
    r.grad_kv[:, head_width:] = kv_sum[:, head_width:].astype(narrow)
    kv_turned = rows_dot(r.unsort[...], r.grad_kv[...], 1, 1).astype(narrow)
    r.kv_turned[...] = kv_turned.reshape(depth, 2, 2, 2, 2 * key_cols, rows)
    kv_factor_copies = send_factor("kv_turned")

    grad_attn_in = r.query_part[...] + rows_dot(r.grad_kv[...], r.kv_sorted[...], 1, 0)
    input_wide = r.block_in[...].astype(wide)
    inverse_in = norm_rows(input_wide, r.norm_gains[0:1])[1]
    grad_in_part, gain_zero = norm_back(input_wide, inverse_in, r.norm_gains[0:1], grad_attn_in)
    r.d_block_in[...] = (r.grad_middle[...] + grad_in_part).astype(narrow)
    r.gains[0:1] = jnp.sum(gain_zero, axis=0, keepdims=True)
    gain_copies = [
        mail.push(r.gains, r.gains_got.at[number], plane_peer(*step))
        for number, step in enumerate(plane_steps)
    ]

    for copy in branch_y:
        copy.wait_recv()
    block = branch_all.at[:, :, c]
    branch_c = mail.push(block, block, c_peer)
    query_deep = weight_terms("query_turned", query_copies, lambda block: r.attn_in[block], query_cols)
    kv_deep = weight_terms("kv_turned", kv_factor_copies, lambda block: r.attn_in[block], 2 * key_cols)
    gain_sum = r.gains[...]
    for number, copy in enumerate(gain_copies):
        copy.wait_recv()
        gain_sum += r.gains_got[number]
    r.gains_sum[...] = gain_sum
    gain_deep = [
        mail.push(r.gains_sum, r.gains_deep.at[offset], z_peer(offset)) for offset in range(1, depth)
    ]
    branch_c.wait_recv()
    out_deep = weight_terms(
        "out_turned",
        out_copies,
        lambda block: branch_all[block // 4, block // 2 % 2, block % 2],
        query_cols,
    )
    for number in range(3, depth):
        ff_step(number)

    def deep_sum(own, far, copies):
        for number, copy in enumerate(copies):
            copy.wait_recv()
            own += far[number + 1].astype(wide)
        return own

    r.grad_q_rows[...] = deep_sum(r.query_turned_wide[d], r.query_turned_far, query_deep)
    r.grad_o_rows[...] = deep_sum(r.out_turned_wide[d], r.out_turned_far, out_deep)
    r.grad_ff_rows[...] = deep_sum(r.ff_own[...], r.ff_got, ff_deep)
    r.grad_kv_rows[...] = deep_sum(r.kv_turned_wide[d], r.kv_turned_far, kv_deep)
    r.gains_out[...] = deep_sum(r.gains_sum[...], r.gains_deep, gain_deep)
    mail.settle()


def split_kernel(block_ref, back_ref, gains_ref, q_ref, o_ref, kv_ref, ff_ref, *outs):
    key_cols, ff_cols = outs[5].shape[0], outs[8].shape[0]
    outs[0][...] = block_ref[...]
    outs[1][...] = back_ref[...]
    norm_count = outs[2].shape[0]
    outs[2][...] = gains_ref[:norm_count]
    outs[3][...] = gains_ref[norm_count : norm_count + outs[3].shape[0], : outs[3].shape[1]]
    outs[4][...] = q_ref[...]
    outs[5][...] = kv_ref[:key_cols]
    outs[6][...] = kv_ref[key_cols:]
    outs[7][...] = o_ref[...]
    for piece in range(3):
        outs[8 + piece][...] = ff_ref[piece * ff_cols : (piece + 1) * ff_cols]


def fused_local(
    block_in,
    cotangent,
    positions,
    norm_gains,
    qk_gains,
    w_query,
    w_key,
    w_value,
    w_out,
    w_gate,
    w_up,
    w_down,
):
    narrow, wide = jnp.bfloat16, jnp.float32
    rows, width = block_in.shape
    head_width = qk_gains.shape[1]
    depth = lax.axis_size("dp")
    query_cols, key_cols, ff_cols = w_query.shape[1], w_key.shape[1], w_gate.shape[1]
    full = query_cols * lax.axis_size(every_axis)
    heads = full // head_width
    plane = lax.axis_size(sequence_axes)
    length = plane * rows
    ff_width = 2 * depth * ff_cols
    operands = dict(
        block_in=block_in,
        cotangent=cotangent,
        positions=positions.reshape(-1, rows),
        norm_gains=norm_gains,
        qk_gains=qk_gains,
        q_rows=w_query.T,
        o_rows=w_out,
        key_rows=w_key.T,
        value_rows=w_value.T,
        gate_rows=w_gate.T,
        up_rows=w_up.T,
        down_rows=w_down,
    )
    results = dict(
        block_out=((rows, width), narrow),
        d_block_in=((rows, width), narrow),
        gains_out=((8, width), wide),
        grad_q_rows=((query_cols, width), wide),
        grad_o_rows=((query_cols, width), wide),
        grad_kv_rows=((2 * key_cols, width), wide),
        grad_ff_rows=((3 * ff_cols, width), wide),
    )
    cube = (depth, 2, 2, 2)
    scratch = dict(
        block_all=((2, 2, 2, rows, width), narrow),
        kv_all=(cube + (2 * key_cols, width), narrow),
        q_all=(cube + (query_cols, width), narrow),
        o_all=(cube + (query_cols, width), narrow),
        ff_all=((depth, 2, 3 * ff_cols, width), narrow),
        pos_pair=((2, plane // 2, rows), wide),
        pos_all=((plane, rows), wide),
        pos_own=((rows, 1), wide),
        cosine=((plane, rows, head_width // 2), wide),
        sine=((plane, rows, head_width // 2), wide),
        sort=((2 * head_width, 2 * head_width), narrow),
        unsort=((2 * head_width, 2 * head_width), narrow),
        attn_in=((plane, rows, width), narrow),
        kv_sorted=((2 * head_width, width), narrow),
        key_raw=((plane, rows, head_width), wide),
        keys=((length, head_width), narrow),
        values=((length, head_width), narrow),
        q_raw=((rows, full), wide),
        q_rot=((heads, rows, head_width), narrow),
        bias=((rows, length), wide),
        probs=((heads, rows, length), wide),
        probs_narrow=((heads, rows, length), narrow),
        exact=((heads, rows, head_width), wide),
        attn_out=((rows, full), narrow),
        branch=((rows, width), wide),
        middle=((rows, width), wide),
        mlp_in=((2, 2, rows, width), narrow),
        gate_pre=((2, 2 * rows, ff_width), wide),
        up_pre=((2, 2 * rows, ff_width), wide),
        hidden=((2, 2 * rows, ff_width), narrow),
        down_raw=((rows, width), wide),
        grad_down=((2, 2, rows, width), narrow),
        grad_gate=((2, 2 * rows, ff_width), narrow),
        grad_up=((2, 2 * rows, ff_width), narrow),
        grad_middle=((rows, width), wide),
        branch_all=((2, 2, 2, rows, width), narrow),
        head_grad=((heads, rows, head_width), narrow),
        grad_scores=((heads, rows, length), narrow),
        grad_query=((rows, full), narrow),
        query_part=((rows, width), wide),
        grad_kv=((rows, 2 * head_width), narrow),
        kv_terms=((2, 2, 2, rows, 2 * head_width), narrow),
        kv_near=((2, 2, rows, 2 * head_width), narrow),
        kv_sums=((2, 2, rows, 2 * head_width), narrow),
        kv_far=((3, rows, 2 * head_width), narrow),
        ff_terms=((depth, 2, 3 * ff_cols, width), narrow),
        ff_near=((depth, 3 * ff_cols, width), narrow),
        ff_sum=((depth, 3 * ff_cols, width), narrow),
        ff_got=((depth, 3 * ff_cols, width), narrow),
        ff_own=((3 * ff_cols, width), wide),
        gains=((8, width), wide),
        gains_got=((plane - 1, 8, width), wide),
        gains_sum=((8, width), wide),
        gains_deep=((depth, 8, width), wide),
    )
    for name in ("down", "mlp_back"):
        scratch[name] = ((2, 2, rows, width), narrow)
        scratch[name + "_near"] = ((2, rows, width), narrow)
        scratch[name + "_sum"] = ((rows, width), narrow)
        scratch[name + "_far"] = ((rows, width), narrow)
    for name, columns in (("out_turned", query_cols), ("query_turned", query_cols), ("kv_turned", 2 * key_cols)):
        scratch[name] = (cube + (columns, rows), narrow)
        scratch[name + "_got"] = ((plane, depth, columns, rows), narrow)
        scratch[name + "_wide"] = ((depth, columns, width), wide)
        scratch[name + "_terms"] = ((depth, columns, width), narrow)
        scratch[name + "_far"] = ((depth, columns, width), narrow)
    names = list(operands) + list(results) + list(scratch) + ["send_sems", "recv_sems"]
    in_vmem = pl.BlockSpec(memory_space=pltpu.VMEM)
    outs = pl.pallas_call(
        lambda *refs: fused_kernel(names, *refs),
        out_shape=[jax.ShapeDtypeStruct(*result) for result in results.values()],
        in_specs=[in_vmem] * len(operands),
        out_specs=[in_vmem] * len(results),
        scratch_shapes=[pltpu.VMEM(*one) for one in scratch.values()]
        + [pltpu.SemaphoreType.DMA((copy_limit,))] * 2,
        compiler_params=pltpu.CompilerParams(
            collective_id=11, has_side_effects=True, vmem_limit_bytes=56 * 1024 * 1024
        ),
        name="layer",
    )(*operands.values())
    parts = [
        ((rows, width), narrow),
        ((rows, width), narrow),
        (norm_gains.shape, wide),
        (qk_gains.shape, wide),
        ((query_cols, width), wide),
        ((key_cols, width), wide),
        ((key_cols, width), wide),
        ((query_cols, width), wide),
        ((ff_cols, width), wide),
        ((ff_cols, width), wide),
        ((ff_cols, width), wide),
    ]
    parts = pl.pallas_call(
        split_kernel,
        out_shape=[jax.ShapeDtypeStruct(*part) for part in parts],
        in_specs=[in_vmem] * len(results),
        out_specs=[in_vmem] * len(parts),
        name="split",
    )(*outs)
    turned = (4, 5, 6, 8, 9)
    return tuple(part.T if index in turned else part for index, part in enumerate(parts))


def fits_fused(block_in, w_query, w_key, w_gate):
    tiles = (w_query.shape[1], 2 * w_key.shape[1], w_gate.shape[1])
    return (
        lax.axis_size("ctx") == 2
        and lax.axis_size("head") == 4
        and block_in.shape[0] % 128 == 0
        and all(columns % 16 == 0 for columns in tiles)
    )


def either_local(*args):
    if fits_fused(args[0], args[5], args[6], args[9]):
        return fused_local(*args)
    return local(*args)


def solution(mesh):
    in_specs = (
        P(every_axis, None),
        P(every_axis, None),
        P(weight_axes),
        P(),
        P(),
        P(None, every_axis),
        P(None, every_axis),
        P(None, every_axis),
        P(every_axis, None),
        P(None, every_axis),
        P(None, every_axis),
        P(every_axis, None),
    )
    out_specs = (
        P(every_axis, None),
        P(every_axis, None),
        P(),
        P(),
        P(None, every_axis),
        P(None, every_axis),
        P(None, every_axis),
        P(every_axis, None),
        P(None, every_axis),
        P(None, every_axis),
        P(every_axis, None),
    )
    return jax.shard_map(either_local, mesh=mesh, in_specs=in_specs, out_specs=out_specs, check_vma=False)
```

```python
import math
import types

import jax
import jax.numpy as jnp
from jax import lax
from jax.experimental import pallas as pl
from jax.experimental.pallas import tpu as pltpu
from jax.sharding import PartitionSpec as P

epsilon = 1e-06
rope_base = 1000000.0
score_scale = 0.0625
negative_fill = -1e30


def norm_rows(values, gain_vec):
    inverse = lax.rsqrt(jnp.mean(values * values, axis=-1, keepdims=True) + epsilon)
    return (values * inverse * gain_vec, inverse)


def norm_back(values, inverse, gain_vec, upstream):
    scaled = upstream * gain_vec
    inner_mean = jnp.mean(scaled * values, axis=-1, keepdims=True)
    return (
        inverse * scaled - values * (inverse * inverse * inverse) * inner_mean,
        upstream * values * inverse,
    )


def rope_angles(positions, full_width):
    ladder = jnp.arange(full_width // 2, dtype=jnp.float32)
    frequency = jnp.exp(ladder * (-2.0 / full_width) * math.log(rope_base))
    angles = positions.astype(jnp.float32)[:, None] * frequency[None, :]
    return (jnp.cos(angles), jnp.sin(angles))


def rotate(values, cosine, sine_part):
    middle = values.shape[-1] // 2
    first_half = values[..., :middle]
    second = values[..., middle:]
    return jnp.concatenate(
        [first_half * cosine - second * sine_part, second * cosine + first_half * sine_part],
        axis=-1,
    )


def gelu_product(gate_pre, up_pre):
    return jax.nn.gelu(gate_pre, approximate=True) * up_pre


every_axis = ("dp", "ctx", "head")
sequence_axes = ("ctx", "head")
weight_axes = ("dp", "ctx")


def place_in(axes):
    place = 0
    for name in axes:
        place = place * lax.axis_size(name) + lax.axis_index(name)
    return place


def coordinates(axes, place):
    found = {}
    for name in reversed(axes):
        size = lax.axis_size(name)
        found[name] = lax.rem(place, size)
        place = place // size
    return found


def each_peer(count, step):
    if count <= 8:
        for offset in range(1, count):
            step(offset)
    else:

        def looped(offset, carry):
            step(offset)
            return carry

        lax.fori_loop(1, count, looped, 0)


def exchange_kernel(kinds, greet, counts, *refs):
    total = len(kinds)
    sources, targets, sems = refs[:total], refs[total : 2 * total], refs[2 * total :]
    barrier = pltpu.get_barrier_semaphore()
    waits = 0
    for axes, count in greet:
        me = place_in(axes)

        def greet_peer(offset, axes=axes, count=count, me=me):
            pl.semaphore_signal(
                barrier,
                inc=1,
                device_id=coordinates(axes, lax.rem(me + offset, count)),
                device_id_type=pl.DeviceIdType.MESH,
            )

        each_peer(count, greet_peer)
        waits += count - 1
    locals_started = []
    for part, (kind, axes) in enumerate(kinds):
        me = place_in(axes)
        source = {"scatter": me, "relative": 0}.get(kind)
        source = sources[part] if source is None else sources[part].at[source]
        copy = pltpu.make_async_copy(source, targets[part].at[me], sems[3 * part + 2].at[0])
        copy.start()
        locals_started.append(copy)
    pl.semaphore_wait(barrier, waits)

    def descriptor(part, offset, backward):
        kind, axes = kinds[part]
        count = counts[part]
        me = place_in(axes)
        to = lax.rem(me + offset, count)
        origin = lax.rem(me + count - offset, count) if backward else me
        source = {"scatter": to, "relative": lax.rem(count - offset, count)}.get(kind)
        source = sources[part] if source is None else sources[part].at[source]
        return pltpu.make_async_remote_copy(
            src_ref=source,
            dst_ref=targets[part].at[origin],
            send_sem=sems[3 * part].at[offset],
            recv_sem=sems[3 * part + 1].at[origin],
            device_id=coordinates(axes, to),
            device_id_type=pl.DeviceIdType.MESH,
        )

    for part in range(total):
        each_peer(counts[part], lambda offset: descriptor(part, offset, False).start())
    for copy in locals_started:
        copy.wait()
    for part in range(total):
        each_peer(counts[part], lambda offset: descriptor(part, offset, True).wait_recv())
    for part in range(total):
        each_peer(counts[part], lambda offset: descriptor(part, offset, False).wait_send())


def exchange(call_id, name, parts, greet_axes=None):
    kinds = tuple((kind, axes) for kind, axes, _ in parts)
    arrays = [array for _, _, array in parts]
    counts = tuple(lax.axis_size(axes) for _, axes in kinds)
    if greet_axes is None:
        greet_axes = (kinds[0][1],)
    greet = tuple((axes, lax.axis_size(axes)) for axes in greet_axes)
    shapes = [
        jax.ShapeDtypeStruct(
            (count,) + array.shape if kind == "gather" else array.shape, array.dtype
        )
        for (kind, _, array), count in zip(parts, counts)
    ]
    scratch = []
    for count in counts:
        scratch += [
            pltpu.SemaphoreType.DMA((count,)),
            pltpu.SemaphoreType.DMA((count,)),
            pltpu.SemaphoreType.DMA((1,)),
        ]
    in_vmem = pl.BlockSpec(memory_space=pltpu.VMEM)
    return pl.pallas_call(
        lambda *refs: exchange_kernel(kinds, greet, counts, *refs),
        out_shape=shapes,
        in_specs=[in_vmem] * len(arrays),
        out_specs=[in_vmem] * len(arrays),
        scratch_shapes=scratch,
        compiler_params=pltpu.CompilerParams(collective_id=call_id, has_side_effects=True),
        name=name,
    )(*arrays)


def digit_place(digit):
    if digit == "head_slow":
        return lax.axis_index("head") // fast_size()
    if digit == "head_fast":
        return lax.rem(lax.axis_index("head"), fast_size())
    return lax.axis_index(digit)


def fast_size():
    return 2 if lax.axis_size("head") % 2 == 0 else 1


def digit_size(digit):
    if digit == "head_slow":
        return lax.axis_size("head") // fast_size()
    if digit == "head_fast":
        return fast_size()
    return lax.axis_size(digit)


def digit_device(digit, value):
    if digit == "head_slow":
        return {"head": value * fast_size() + digit_place("head_fast")}
    if digit == "head_fast":
        return {"head": digit_place("head_slow") * fast_size() + value}
    return {digit: value}


def staged_kernel(plans, greeted, *refs):
    total = len(plans)
    sources, targets, sems = refs[:total], refs[total : 2 * total], list(refs[2 * total :])
    barrier = pltpu.get_barrier_semaphore()
    waits = 0
    for digit in greeted:
        count, me = digit_size(digit), digit_place(digit)
        for offset in range(1, count):
            pl.semaphore_signal(
                barrier,
                inc=1,
                device_id=digit_device(digit, lax.rem(me + offset, count)),
                device_id_type=pl.DeviceIdType.MESH,
            )
            waits += 1
    local_sems = sems[:total]
    rest = sems[total:]
    pairs = []
    for plan in plans:
        pairs.append([(rest.pop(0), rest.pop(0)) for _ in plan])
    own = []
    for part, plan in enumerate(plans):
        here = tuple(digit_place(digit) for digit in reversed(plan))
        copy = pltpu.make_async_copy(sources[part], targets[part].at[here], local_sems[part].at[0])
        copy.start()
        own.append(copy)
    pl.semaphore_wait(barrier, waits)

    def descriptors(part, turn, backward):
        plan = plans[part]
        digit = plan[turn]
        count, me = digit_size(digit), digit_place(digit)
        outer = tuple(digit_place(name) for name in reversed(plan[turn + 1 :]))
        found = []
        for offset in range(1, count):
            to = lax.rem(me + offset, count)
            origin = lax.rem(me + count - offset, count) if backward else me
            source = sources[part] if turn == 0 else targets[part].at[outer + (me,)]
            found.append(
                pltpu.make_async_remote_copy(
                    src_ref=source,
                    dst_ref=targets[part].at[outer + (origin,)],
                    send_sem=pairs[part][turn][0].at[offset],
                    recv_sem=pairs[part][turn][1].at[origin],
                    device_id=digit_device(digit, to),
                    device_id_type=pl.DeviceIdType.MESH,
                )
            )
        return found

    most = max(len(plan) for plan in plans)
    for turn in range(most + 1):
        for part, plan in enumerate(plans):
            if 0 < turn <= len(plan):
                for copy in descriptors(part, turn - 1, True):
                    copy.wait_recv()
            if turn == 1:
                own[part].wait()
            if turn < len(plan):
                for copy in descriptors(part, turn, False):
                    copy.start()
    for part, plan in enumerate(plans):
        for turn in range(len(plan)):
            for copy in descriptors(part, turn, False):
                copy.wait_send()


def staged_gather(call_id, name, parts):
    plans = [plan for plan, _ in parts]
    arrays = [array for _, array in parts]
    greeted = []
    for plan in plans:
        greeted += [digit for digit in plan if digit not in greeted]
    shapes = [
        jax.ShapeDtypeStruct(
            tuple(digit_size(digit) for digit in reversed(plan)) + array.shape, array.dtype
        )
        for plan, array in parts
    ]
    scratch = [pltpu.SemaphoreType.DMA((1,)) for _ in parts]
    for plan in plans:
        for digit in plan:
            scratch += [pltpu.SemaphoreType.DMA((digit_size(digit),))] * 2
    in_vmem = pl.BlockSpec(memory_space=pltpu.VMEM)
    return pl.pallas_call(
        lambda *refs: staged_kernel(plans, greeted, *refs),
        out_shape=shapes,
        in_specs=[in_vmem] * len(arrays),
        out_specs=[in_vmem] * len(arrays),
        scratch_shapes=scratch,
        compiler_params=pltpu.CompilerParams(collective_id=call_id, has_side_effects=True),
        name=name,
    )(*arrays)


def gather_rows(call_id, name, rows):
    (blocks,) = exchange(call_id, name, [("gather", ("head",), rows)])
    return blocks.reshape(-1, rows.shape[1])


def shifted(array, axis, offset):
    count = lax.axis_size(axis)
    return lax.ppermute(array, axis, [(here, (here + offset) % count) for here in range(count)])


def gelu_parts(value):
    root = math.sqrt(2.0 / math.pi)
    square = value * value
    tanh_part = jnp.tanh(root * (value + 0.044715 * value * square))
    gelu = 0.5 * value * (1.0 + tanh_part)
    slope = 0.5 * (1.0 + tanh_part) + 0.5 * value * (1.0 - tanh_part * tanh_part) * root * (
        1.0 + 3.0 * 0.044715 * square
    )
    return gelu, slope


def mlp_forward_kernel(rows_ref, gate_ref, up_ref, down_ref, gate_pre_ref, up_pre_ref, hidden_ref, part_ref):
    rows = rows_ref[...]
    gate_pre = rows_dot(rows, gate_ref[...], 1, 1)
    up_pre = rows_dot(rows, up_ref[...], 1, 1)
    gate_pre_ref[...] = gate_pre
    up_pre_ref[...] = up_pre
    hidden = (gelu_parts(gate_pre)[0] * up_pre).astype(jnp.bfloat16)
    hidden_ref[...] = hidden
    part_ref[...] = rows_dot(hidden, down_ref[...], 1, 0).astype(jnp.bfloat16)


def mlp_backward_kernel(
    rows_ref, gate_ref, up_ref, down_ref, gate_pre_ref, up_pre_ref, grad_gate_ref, grad_up_ref, part_ref
):
    grad_hidden = rows_dot(rows_ref[...], down_ref[...], 1, 1)
    gelu, slope = gelu_parts(gate_pre_ref[...])
    grad_gate = (grad_hidden * up_pre_ref[...] * slope).astype(jnp.bfloat16)
    grad_up = (grad_hidden * gelu).astype(jnp.bfloat16)
    grad_gate_ref[...] = grad_gate
    grad_up_ref[...] = grad_up
    part_ref[...] = (
        rows_dot(grad_gate, gate_ref[...], 1, 0) + rows_dot(grad_up, up_ref[...], 1, 0)
    ).astype(jnp.bfloat16)


def rows_dot(left, right, left_dim, right_dim):
    return lax.dot_general(
        left, right, (((left_dim,), (right_dim,)), ((), ())), preferred_element_type=jnp.float32
    )


def add_up(blocks):
    return jnp.sum(blocks.astype(jnp.float32), axis=0)


def local(
    block_in,
    cotangent,
    positions,
    norm_gains,
    qk_gains,
    w_query,
    w_key,
    w_value,
    w_out,
    w_gate,
    w_up,
    w_down,
):
    tok_rows, model_width = block_in.shape
    head_count = lax.axis_size("head")
    head_width = qk_gains.shape[1]
    ctx_slot = lax.axis_index("ctx")
    query_rows = head_count * tok_rows
    group_count = lax.axis_size(weight_axes)
    every_count = lax.axis_size(every_axis)
    length_all = lax.axis_size(sequence_axes) * tok_rows
    query_cols = w_query.shape[1]
    key_cols = w_key.shape[1]
    ff_cols = w_gate.shape[1]
    narrow = jnp.bfloat16

    ff_rows = jnp.concatenate([w_gate.T, w_up.T, w_down], axis=0)
    dp_count, ctx_count = lax.axis_size("dp"), lax.axis_size("ctx")

    to_heads = [
        (head * group_count + index, index * head_count + head)
        for head in range(head_count)
        for index in range(group_count)
    ]
    to_owners = [(there, here) for here, there in to_heads]
    head_rows = lax.ppermute(
        jnp.concatenate([w_query.T, w_out], axis=0), every_axis, to_heads
    )
    key_value_rows = jnp.concatenate([w_key.T, w_value.T], axis=0)
    block_all, key_value_all, head_all, position_all = staged_gather(
        1,
        "first_gather",
        [
            (("ctx", "head_slow", "head_fast"), block_in),
            (("dp", "ctx", "head_slow", "head_fast"), key_value_rows),
            (("dp", "ctx"), head_rows),
            (("ctx",), positions.reshape(-1, 128)),
        ],
    )
    block_all, ff_rows = lax.optimization_barrier((block_all, ff_rows))
    near_blocks = [ff_rows] + [shifted(ff_rows, "dp", offset) for offset in range(1, dp_count)]
    ff_across = [shifted(ff_rows, "ctx", offset) for offset in range(1, ctx_count)]
    block_all = block_all.transpose(2, 1, 0, 3, 4)
    key_value_all = key_value_all.transpose(3, 2, 1, 0, 4, 5).reshape(
        every_count, 2 * key_cols, model_width
    )
    head_all = head_all.transpose(1, 0, 2, 3).reshape(group_count, 2 * query_cols, model_width)
    query_weight = head_all[:, :query_cols].reshape(head_width, model_width)
    out_weight = head_all[:, query_cols:].reshape(head_width, model_width)
    key_weight = key_value_all[:, :key_cols].reshape(head_width, model_width)
    value_weight = key_value_all[:, key_cols:].reshape(head_width, model_width)

    input_all = block_all.reshape(length_all, model_width).astype(jnp.float32)
    attn_in_all = norm_rows(input_all, norm_gains[0])[0].astype(narrow)
    first_query = ctx_slot * query_rows
    attn_in = lax.dynamic_slice_in_dim(attn_in_all, first_query, query_rows)
    query_raw = rows_dot(attn_in, query_weight, 1, 1)
    key_raw = rows_dot(attn_in_all, key_weight, 1, 1)
    all_values = rows_dot(attn_in_all, value_weight, 1, 1).astype(narrow)
    query_normed, inverse_query = norm_rows(query_raw, qk_gains[0])
    key_normed, inverse_key = norm_rows(key_raw, qk_gains[1])
    cosine, sine_part = rope_angles(position_all.reshape(length_all), head_width)
    cosine_own = lax.dynamic_slice_in_dim(cosine, first_query, query_rows)
    sine_own = lax.dynamic_slice_in_dim(sine_part, first_query, query_rows)
    head_query = (rotate(query_normed, cosine_own, sine_own) * score_scale).astype(narrow)
    all_keys = rotate(key_normed, cosine, sine_part).astype(narrow)

    query_index = first_query + jnp.arange(query_rows, dtype=jnp.int32)
    lowest_key = query_index - positions
    key_index = jnp.arange(length_all, dtype=jnp.int32)
    visible = (key_index[None, :] <= query_index[:, None]) & (
        key_index[None, :] >= lowest_key[:, None]
    )
    scores = jnp.where(visible, rows_dot(head_query, all_keys, 1, 1), negative_fill)
    top = jnp.max(scores, axis=1, keepdims=True)
    log_total = top + jnp.log(jnp.sum(jnp.exp(scores - top), axis=1, keepdims=True))
    probs_wide = jnp.exp(scores - log_total)
    prob_rows = probs_wide.astype(narrow)
    attn_exact = rows_dot(prob_rows, all_values, 1, 0)
    attn_out = attn_exact.astype(narrow)
    branch_part = rows_dot(attn_out, out_weight, 1, 0).astype(narrow)
    (branch_blocks,) = exchange(
        2,
        "branch_scatter",
        [("scatter", ("head",), branch_part.reshape(head_count, tok_rows, model_width))],
    )
    branch = add_up(branch_blocks)
    input_wide = block_in.astype(jnp.float32)
    inverse_in = norm_rows(input_wide, norm_gains[0])[1]
    branch_normed, inverse_branch = norm_rows(branch, norm_gains[1])
    middle = input_wide + branch_normed
    mlp_norm, inverse_mid = norm_rows(middle, norm_gains[2])
    mlp_norm, near_blocks, ff_across = lax.optimization_barrier((mlp_norm, near_blocks, ff_across))
    ff_slots = list(near_blocks)
    for offset in range(1, ctx_count):
        ff_slots += [ff_across[offset - 1]]
        ff_slots += [shifted(block, "ctx", offset) for block in near_blocks[1:]]
    mlp_in = gather_rows(3, "mlp_gather", mlp_norm.astype(narrow))

    ff_width = group_count * ff_cols
    gate_weight = jnp.concatenate([block[:ff_cols] for block in ff_slots], axis=0)
    up_weight = jnp.concatenate([block[ff_cols : 2 * ff_cols] for block in ff_slots], axis=0)
    down_weight = jnp.concatenate([block[2 * ff_cols :] for block in ff_slots], axis=0)
    wide_ff = jax.ShapeDtypeStruct((query_rows, ff_width), jnp.float32)
    narrow_ff = jax.ShapeDtypeStruct((query_rows, ff_width), narrow)
    narrow_rows = jax.ShapeDtypeStruct((query_rows, model_width), narrow)
    gate_pre, up_pre, hidden, down_part = pl.pallas_call(
        mlp_forward_kernel,
        out_shape=[wide_ff, wide_ff, narrow_ff, narrow_rows],
        name="mlp_forward",
    )(mlp_in, gate_weight, up_weight, down_weight)
    (down_blocks,) = exchange(
        4,
        "down_scatter",
        [("scatter", ("head",), down_part.reshape(head_count, tok_rows, model_width))],
    )
    down_raw = add_up(down_blocks)
    down_normed, inverse_down = norm_rows(down_raw, norm_gains[3])
    block_out = (middle + down_normed).astype(narrow)
    cot_wide = cotangent.astype(jnp.float32)
    grad_down_raw, gain_three = norm_back(down_raw, inverse_down, norm_gains[3], cot_wide)
    grad_down_in = gather_rows(5, "grad_down_gather", grad_down_raw.astype(narrow))
    grad_gate_in, grad_up_in, grad_mlp_part = pl.pallas_call(
        mlp_backward_kernel,
        out_shape=[narrow_ff, narrow_ff, narrow_rows],
        name="mlp_backward",
    )(grad_down_in, gate_weight, up_weight, down_weight, gate_pre, up_pre)
    slots = (ctx_count, dp_count, ff_cols, model_width)
    ff_terms = jnp.concatenate(
        [
            rows_dot(grad_gate_in, mlp_in, 0, 0).astype(narrow).reshape(slots),
            rows_dot(grad_up_in, mlp_in, 0, 0).astype(narrow).reshape(slots),
            rows_dot(hidden, grad_down_in, 0, 0).astype(narrow).reshape(slots),
        ],
        axis=2,
    )
    half = dp_count // 2
    grad_mlp_blocks, ff_early = exchange(
        6,
        "grad_mlp_scatter",
        [
            (
                "scatter",
                ("head",),
                grad_mlp_part.reshape(head_count, tok_rows, model_width),
            ),
            ("relative", ("ctx",), ff_terms[:, :half]),
        ],
        (("head",), ("ctx",)),
    )
    grad_mlp_in = add_up(grad_mlp_blocks)
    grad_mid_part, gain_two = norm_back(middle, inverse_mid, norm_gains[2], grad_mlp_in)
    grad_middle = cot_wide + grad_mid_part
    grad_branch_raw, gain_one = norm_back(branch, inverse_branch, norm_gains[1], grad_middle)
    grad_branch_blocks, ff_late = exchange(
        7,
        "grad_branch_gather",
        [
            ("gather", ("head",), grad_branch_raw.astype(narrow)),
            ("relative", ("ctx",), ff_terms[:, half:]),
        ],
        (("head",), ("ctx",)),
    )
    grad_branch = grad_branch_blocks.reshape(query_rows, model_width)
    ff_sums = jnp.concatenate([add_up(ff_early), add_up(ff_late)], axis=0).astype(narrow)
    head_grad = rows_dot(grad_branch, out_weight, 1, 1).astype(narrow)
    row_delta = jnp.sum(head_grad.astype(jnp.float32) * attn_exact, axis=1, keepdims=True)
    grad_probs = rows_dot(head_grad, all_values, 1, 1)
    grad_scores = (probs_wide * (grad_probs - row_delta)).astype(narrow)
    value_sums = rows_dot(prob_rows, head_grad, 0, 0)
    key_sums = rows_dot(grad_scores, head_query, 0, 0)
    grad_rot_query = rows_dot(grad_scores, all_keys, 1, 0)
    query_back = rotate(grad_rot_query * score_scale, cosine_own, -sine_own)
    grad_query_raw, gain_query = norm_back(query_raw, inverse_query, qk_gains[0], query_back)
    key_back = rotate(key_sums, cosine, -sine_part)
    grad_key_raw, gain_key = norm_back(key_raw, inverse_key, qk_gains[1], key_back)
    grad_query_in = grad_query_raw.astype(narrow)
    grad_key_in = grad_key_raw.astype(narrow)
    grad_value_in = value_sums.astype(narrow)
    grad_attn_part = rows_dot(grad_key_in, key_weight, 1, 0) + rows_dot(
        grad_value_in, value_weight, 1, 0
    )
    own_part = lax.dynamic_slice_in_dim(grad_attn_part, first_query, query_rows) + rows_dot(
        grad_query_in, query_weight, 1, 0
    )
    grad_attn_part = lax.dynamic_update_slice_in_dim(grad_attn_part, own_part, first_query, 0)
    head_terms = jnp.concatenate(
        [
            rows_dot(grad_query_in, attn_in, 0, 0).reshape(group_count, query_cols, model_width),
            rows_dot(attn_out, grad_branch, 0, 0).reshape(group_count, query_cols, model_width),
        ],
        axis=1,
    ).astype(narrow)
    planes = (dp_count, every_count // dp_count, key_cols, model_width)
    key_value_terms = jnp.concatenate(
        [
            rows_dot(grad_key_in, attn_in_all, 0, 0).reshape(planes),
            rows_dot(grad_value_in, attn_in_all, 0, 0).reshape(planes),
        ],
        axis=2,
    ).astype(narrow).transpose(1, 0, 2, 3)
    head_terms = head_terms.reshape(dp_count, ctx_count, 2 * query_cols, model_width)
    grad_attn_blocks, head_blocks, key_value_blocks, ff_blocks = exchange(
        8,
        "last_scatter",
        [
            (
                "scatter",
                sequence_axes,
                grad_attn_part.astype(narrow).reshape(-1, tok_rows, model_width),
            ),
            ("scatter", ("ctx",), head_terms.transpose(1, 0, 2, 3)),
            ("scatter", sequence_axes, key_value_terms),
            ("relative", ("dp",), ff_sums),
        ],
        (sequence_axes, ("dp",)),
    )
    ff_own = add_up(ff_blocks)
    grad_attn_in = add_up(grad_attn_blocks)
    grad_in_part, gain_zero = norm_back(input_wide, inverse_in, norm_gains[0], grad_attn_in)
    d_block_in = (grad_middle + grad_in_part).astype(narrow)

    pad = ((0, 0), (0, model_width - head_width))
    gain_terms = jnp.concatenate(
        [
            jnp.sum(gain_zero, axis=0, keepdims=True),
            jnp.sum(gain_one, axis=0, keepdims=True),
            jnp.sum(gain_two, axis=0, keepdims=True),
            jnp.sum(gain_three, axis=0, keepdims=True),
            jnp.pad(jnp.sum(gain_query, axis=0, keepdims=True), pad),
            jnp.pad(jnp.sum(gain_key, axis=0, keepdims=True), pad),
            jnp.zeros((2, model_width), jnp.float32),
        ],
        axis=0,
    )
    gain_blocks, head_blocks, key_value_blocks = exchange(
        9,
        "depth_exchange",
        [
            ("gather", ("dp",), gain_terms),
            ("scatter", ("dp",), add_up(head_blocks).astype(narrow)),
            ("scatter", ("dp",), add_up(key_value_blocks).astype(narrow)),
        ],
    )
    head_own = lax.ppermute(add_up(head_blocks).astype(narrow), every_axis, to_owners).astype(
        jnp.float32
    )
    (gain_blocks,) = exchange(10, "gain_gather", [("gather", sequence_axes, add_up(gain_blocks))])
    gains = add_up(gain_blocks)
    key_value_own = add_up(key_value_blocks)
    return (
        block_out,
        d_block_in,
        gains[:4],
        gains[4:6, :head_width],
        head_own[:query_cols].T,
        key_value_own[:key_cols].T,
        key_value_own[key_cols:].T,
        head_own[query_cols:],
        ff_own[:ff_cols].T,
        ff_own[ff_cols : 2 * ff_cols].T,
        ff_own[2 * ff_cols :],
    )


bits = (0, 1)


class Mail:
    def __init__(self, send_sems, recv_sems):
        self.send_sems, self.recv_sems = send_sems, recv_sems
        self.started = []

    def push(self, source, target, to, when=None, arrives_as=None):
        number = len(self.started)
        copy = pltpu.make_async_remote_copy(
            src_ref=source,
            dst_ref=target,
            send_sem=self.send_sems.at[number],
            recv_sem=self.recv_sems.at[number if arrives_as is None else arrives_as],
            device_id=to,
            device_id_type=pl.DeviceIdType.MESH,
        )
        if when is None:
            copy.start()
        else:
            pl.when(when)(copy.start)
        self.started.append((copy, when))
        return copy

    def settle(self):
        for copy, when in self.started:
            if when is None:
                copy.wait_send()
            else:
                pl.when(when)(copy.wait_send)


copy_limit = 176


def fused_kernel(names, *refs):
    r = types.SimpleNamespace(**dict(zip(names, refs)))
    narrow, wide = jnp.bfloat16, jnp.float32
    d, x, h = lax.axis_index("dp"), lax.axis_index("ctx"), lax.axis_index("head")
    depth = lax.axis_size("dp")
    y, c = h // 2, lax.rem(h, 2)
    me = x * 4 + h
    mail = Mail(r.send_sems, r.recv_sems)
    rows, width = r.block_in.shape
    head_width = r.qk_gains.shape[1]
    half_width = head_width // 2
    heads, query_cols = r.q_raw.shape[1] // head_width, r.q_rows.shape[0]
    key_cols = r.key_rows.shape[0]
    ff_cols = r.gate_rows.shape[0]
    all_rows = 8 * rows
    full = heads * head_width

    def deep(offset):
        return lax.rem(d + offset, depth)

    def z_peer(offset):
        return {"dp": deep(offset)}

    x_peer = {"ctx": 1 - x}
    y_peer = {"head": (1 - y) * 2 + c}
    c_peer = {"head": y * 2 + 1 - c}

    def flip(place, bit):
        return 1 - place if bit else place

    def plane_peer(dx, dy, dc):
        return {"ctx": flip(x, dx), "head": flip(y, dy) * 2 + flip(c, dc)}

    plane_steps = [(dx, dy, dc) for dx in bits for dy in bits for dc in bits][1:]
    chip_steps = [(0, 1), (1, 0), (1, 1)]

    barrier = pltpu.get_barrier_semaphore()
    greeted = [z_peer(offset) for offset in range(1, depth)] + [plane_peer(*s) for s in plane_steps]
    for peer in greeted:
        pl.semaphore_signal(barrier, inc=1, device_id=peer, device_id_type=pl.DeviceIdType.MESH)
    r.block_all[x, y, c] = r.block_in[...]
    key_value = [r.key_rows[...].astype(wide), r.value_rows[...].astype(wide)]
    r.kv_all[d, x, y, c] = jnp.concatenate(key_value, axis=0).astype(narrow)
    r.q_all[d, x, y, c] = r.q_rows[...]
    r.o_all[d, x, y, c] = r.o_rows[...]
    for piece, own in enumerate((r.gate_rows, r.up_rows, r.down_rows)):
        r.ff_all[d, x, pl.ds(piece * ff_cols, ff_cols)] = own[...]
    r.pos_pair[x] = r.positions[...].astype(wide)
    pl.semaphore_wait(barrier, len(greeted))

    got_z, got_x, got_y, got_c = {}, {}, {}, {}

    def place(part):
        return (x, y, c) if part == "block" else (d, x, y, c)

    def source(part):
        return getattr(r, part + "_all").at[place(part)]

    def own_to_x(part):
        got_x[part, 0] = mail.push(source(part), getattr(r, part + "_all").at[place(part)], x_peer)

    def own_to_y(part):
        got_y[part, 0] = [
            mail.push(source(part), getattr(r, part + "_all").at[place(part)], y_peer)
        ]

    relayed = depth >= 4
    relays = ((depth - 1, 2, 0), (1, depth - 3, depth - 1)) if relayed else ()
    z_order = sorted(range(1, depth), key=lambda offset: offset != 2)

    def blocks_to_z(key, block_of):
        for offset in range(1, depth):
            when = None
            if relayed and offset == 1:
                when = d < depth - 1
            if relayed and offset == depth - 1:
                when = d > 0
            number = len(mail.started)
            copy = mail.push(block_of(d), block_of(d), z_peer(offset), when)
            got_z[key, offset] = copy, number

    def blocks_to_x(key, block_of):
        for offset in z_order:
            got_z[key, offset][0].wait_recv()
            block = block_of(deep(depth - offset))
            if offset == 2:
                for other, relay, _ in relays:
                    to = {"dp": lax.rem(d + depth - 2 + other, depth)}
                    mail.push(block, block, to, d == relay, got_z[key, other][1])
            got_x[key, offset] = mail.push(block, block, x_peer)

    def block_of(part):
        return lambda slot: getattr(r, part + "_all").at[(slot,) + place(part)[1:]]

    def own_to_z(part):
        blocks_to_z(part, block_of(part))

    def to_x(part):
        blocks_to_x(part, block_of(part))

    def near_to_y(part):
        got_x[part, 0].wait_recv()
        at = (1 - x, y, c) if part == "block" else (d, 1 - x, y, c)
        block = getattr(r, part + "_all").at[at]
        got_y[part, 0].append(mail.push(block, block, y_peer))

    def to_y(part):
        for offset in range(1, depth):
            got_x[part, offset].wait_recv()
            block = getattr(r, part + "_all").at[deep(depth - offset), :, y, c]
            got_y[part, offset] = [mail.push(block, block, y_peer)]

    def to_c(part):
        for offset in range(1 if part == "block" else depth):
            for copy in got_y[part, offset]:
                copy.wait_recv()
            block = getattr(r, part + "_all")
            block = block if part == "block" else block.at[deep(depth - offset)]
            block = block.at[:, :, c]
            got_c[part, offset] = mail.push(block, block, c_peer)

    def arrived(part):
        for offset in range(1 if part == "block" else depth):
            got_c[part, offset].wait_recv()

    def ff_piece(slot, piece):
        return r.ff_all.at[slot, x, pl.ds(piece * ff_cols, ff_cols)]

    def ff_to_z(piece):
        blocks_to_z(("ff", piece), lambda slot: ff_piece(slot, piece))

    def ff_own_to_x():
        block = r.ff_all.at[d, x]
        got_x["ff", 0] = mail.push(block, block, x_peer)

    def ff_to_x(piece):
        blocks_to_x(("ff", piece), lambda slot: ff_piece(slot, piece))

    position_copy = mail.push(r.pos_pair.at[x], r.pos_pair.at[x], x_peer)
    for part in ("kv", "block", "q", "o"):
        own_to_x(part)
        own_to_y(part)
        if part != "block":
            own_to_z(part)

    def rope_tables():
        position_copy.wait_recv()
        for half in bits:
            r.pos_all[half * 4 : half * 4 + 4] = r.pos_pair[half]
        turned = r.pos_all[...].T
        ladder = lax.broadcasted_iota(jnp.int32, (1, half_width), 1).astype(wide)
        frequency = jnp.exp(ladder * (-2.0 / head_width) * math.log(rope_base))
        column = lax.broadcasted_iota(jnp.int32, turned.shape, 1)
        r.pos_own[...] = jnp.sum(jnp.where(column == me, turned, 0.0), axis=1, keepdims=True)
        for block in range(8):
            angle = turned[:, block : block + 1] * frequency
            r.cosine[block] = jnp.cos(angle)
            r.sine[block] = jnp.sin(angle)

    def shuffle():
        size = 2 * head_width
        there = lax.broadcasted_iota(jnp.int32, (size, size), 1).astype(wide)
        here = lax.broadcasted_iota(jnp.int32, (size, size), 0).astype(wide)

        def sorted_place(place):
            block = jnp.floor((place + 0.5) / (2 * key_cols))
            inside = place - block * (2 * key_cols)
            value = inside >= key_cols
            return block * key_cols + jnp.where(value, inside - key_cols + head_width, inside)

        r.unsort[...] = jnp.where(sorted_place(here) == there, 1.0, 0.0).astype(narrow)
        r.sort[...] = jnp.where(sorted_place(there) == here, 1.0, 0.0).astype(narrow)

    def attention_inputs():
        arrived("block")
        gain = r.norm_gains[0:1]
        for px in bits:
            for py in bits:
                for pc in bits:
                    values = r.block_all[px, py, pc].astype(wide)
                    r.attn_in[px * 4 + py * 2 + pc] = norm_rows(values, gain)[0].astype(narrow)

    def keys_and_values():
        arrived("kv")
        blocks = r.kv_all[...].reshape(2 * head_width, width)
        r.kv_sorted[...] = rows_dot(r.sort[...], blocks, 1, 0).astype(narrow)
        gain = r.qk_gains[1:2]
        for pair in range(4):
            two = pl.ds(2 * pair, 2)
            inputs = r.attn_in[two].reshape(2 * rows, width)
            raw = rows_dot(inputs, r.kv_sorted[...], 1, 1)
            key_raw = raw[:, :head_width]
            r.key_raw[two] = key_raw.reshape(2, rows, head_width)
            cosine = r.cosine[two].reshape(2 * rows, half_width)
            sine_part = r.sine[two].reshape(2 * rows, half_width)
            turned = rotate(norm_rows(key_raw, gain)[0], cosine, sine_part)
            r.keys[pl.ds(2 * pair * rows, 2 * rows)] = turned.astype(narrow)
            r.values[pl.ds(2 * pair * rows, 2 * rows)] = raw[:, head_width:].astype(narrow)

    shuffle()
    rope_tables()
    to_x("kv")
    near_to_y("kv")
    near_to_y("block")
    ff_to_z(0)
    to_x("q")
    near_to_y("q")
    to_y("kv")
    ff_to_z(1)
    ff_own_to_x()
    to_x("o")
    near_to_y("o")
    to_y("q")
    ff_to_z(2)
    to_c("block")
    attention_inputs()
    ff_to_x(0)
    to_c("kv")
    to_y("o")
    keys_and_values()
    ff_to_x(1)
    to_c("q")

    query_gain = r.qk_gains[0:1]
    arrived("q")
    weight = r.q_all[...].reshape(full, width)
    r.q_raw[...] = rows_dot(r.attn_in[me], weight, 1, 1)
    for head in range(heads):
        turned = rotate(
            norm_rows(r.q_raw[:, head * head_width : (head + 1) * head_width], query_gain)[0],
            r.cosine[me],
            r.sine[me],
        )
        r.q_rot[head] = (turned * score_scale).astype(narrow)
    to_c("o")
    ff_to_x(2)

    query_index = lax.broadcasted_iota(jnp.int32, (rows, all_rows), 0) + me * rows
    key_index = lax.broadcasted_iota(jnp.int32, (rows, all_rows), 1)
    lowest_key = query_index - r.pos_own[...].astype(jnp.int32)
    visible = (key_index <= query_index) & (key_index >= lowest_key)
    r.bias[...] = jnp.where(visible, 0.0, negative_fill)
    for head in range(heads):
        scores = rows_dot(r.q_rot[head], r.keys[...], 1, 1)
        scores = jnp.where(r.bias[...] < 0.0, negative_fill, scores)
        top = jnp.max(scores, axis=1, keepdims=True)
        raised = jnp.exp(scores - top)
        prob_rows = raised * (1.0 / jnp.sum(raised, axis=1, keepdims=True))
        r.probs[head] = prob_rows
        r.probs_narrow[head] = prob_rows.astype(narrow)
        exact = rows_dot(prob_rows.astype(narrow), r.values[...], 1, 0)
        r.exact[head] = exact
        r.attn_out[:, head * head_width : (head + 1) * head_width] = exact.astype(narrow)
    arrived("o")
    out_weight = r.o_all[...].reshape(full, width)
    r.branch[...] = rows_dot(r.attn_out[...], out_weight, 1, 0)
    def send_factor(name):
        copies = []
        for step in plane_steps:
            px, py, pc = (flip(here, bit) for here, bit in zip((x, y, c), step))
            copies.append(
                mail.push(getattr(r, name).at[:, px, py, pc], getattr(r, name + "_got").at[me], plane_peer(*step))
            )
        getattr(r, name + "_got")[me] = getattr(r, name)[:, x, y, c]
        return copies

    def send_group_factor():
        copies = []
        for dy, dc in chip_steps:
            source = r.out_turned.at[:, :, flip(y, dy), flip(c, dc)]
            copies.append(mail.push(source, r.out_turned_got.at[y, c], plane_peer(0, dy, dc)))
        r.out_turned_got[y, c] = r.out_turned[:, :, y, c]
        return copies

    def turned_blocks(name, values, columns):
        getattr(r, name)[...] = values.astype(wide).T.astype(narrow).reshape(depth, 2, 2, 2, columns, rows)

    input_wide = r.block_in[...].astype(wide)
    branch_normed = norm_rows(r.branch[...], r.norm_gains[1:2])[0]
    r.middle[...] = input_wide + branch_normed
    mlp_rows = norm_rows(r.middle[...], r.norm_gains[2:3])[0].astype(narrow)

    def share_rows(name, values):
        getattr(r, name)[y, c] = values
        block = getattr(r, name).at[y, c]
        return mail.push(block, block, c_peer), mail.push(block, block, y_peer)

    def far_rows(name, from_y):
        from_y.wait_recv()
        block = getattr(r, name).at[1 - y, c]
        return mail.push(block, block, c_peer)

    def fetch_ff():
        got_x["ff", 0].wait_recv()
        for piece in range(3):
            for offset in range(1, depth):
                got_x[("ff", piece), offset].wait_recv()

    def ff_part(index):
        piece = r.ff_all[:, :, pl.ds(index * ff_cols, ff_cols)]
        return piece.reshape(2 * depth * ff_cols, width)

    def group_sum(name, half, own_rows, waiting, early, between):
        part, near, far = getattr(r, name), getattr(r, name + "_near"), getattr(r, name + "_far")
        from_c, from_y = own_rows
        from_c.wait_recv()
        half(y)
        near_own = mail.push(part.at[y, 1 - c], near.at[0], c_peer)
        forwarded = from_y()
        waiting()
        forwarded.wait_recv()
        early()
        half(1 - y)
        near_far = mail.push(part.at[1 - y, 1 - c], near.at[1], c_peer)
        near_far.wait_recv()
        summed = part[1 - y, c].astype(wide) + near[1].astype(wide)
        getattr(r, name + "_sum")[...] = summed.astype(narrow)
        far_copy = mail.push(getattr(r, name + "_sum"), far, y_peer)
        between()
        near_own.wait_recv()
        own = part[y, c].astype(wide) + near[0].astype(wide)
        far_copy.wait_recv()
        return own + far[...].astype(wide)

    def forward_half(side):
        inputs = r.mlp_in[side].reshape(2 * rows, width)
        gate_pre = rows_dot(inputs, ff_part(0), 1, 1)
        up_pre = rows_dot(inputs, ff_part(1), 1, 1)
        r.gate_pre[side] = gate_pre
        r.up_pre[side] = up_pre
        hidden = (gelu_parts(gate_pre)[0] * up_pre).astype(narrow)
        r.hidden[side] = hidden
        part = rows_dot(hidden, ff_part(2), 1, 0).astype(narrow)
        r.down[side] = part.reshape(2, rows, width)

    def nothing():
        pass

    near_copy, y_copy = share_rows("mlp_in", mlp_rows)
    turned_blocks("out_turned", r.attn_out[...], query_cols)
    out_copies = send_group_factor()
    fetch_ff()
    r.down_raw[...] = group_sum(
        "down", forward_half, (near_copy, lambda: far_rows("mlp_in", y_copy)), nothing, nothing, nothing
    )
    down_raw = r.down_raw[...]
    down_normed, inverse_down = norm_rows(down_raw, r.norm_gains[3:4])
    r.block_out[...] = (r.middle[...] + down_normed).astype(narrow)
    cot_wide = r.cotangent[...].astype(wide)
    grad_down_raw, gain_three = norm_back(down_raw, inverse_down, r.norm_gains[3:4], cot_wide)
    r.gains[...] = jnp.zeros_like(r.gains)
    r.gains[3:4] = jnp.sum(gain_three, axis=0, keepdims=True)

    def backward_half(side):
        grad_hidden = rows_dot(r.grad_down[side].reshape(2 * rows, width), ff_part(2), 1, 1)
        gelu, slope = gelu_parts(r.gate_pre[side])
        grad_gate = (grad_hidden * r.up_pre[side] * slope).astype(narrow)
        grad_up = (grad_hidden * gelu).astype(narrow)
        r.grad_gate[side] = grad_gate
        r.grad_up[side] = grad_up
        part = rows_dot(grad_gate, ff_part(0), 1, 0) + rows_dot(grad_up, ff_part(1), 1, 0)
        r.mlp_back[side] = part.astype(narrow).reshape(2, rows, width)

    ff_width = 2 * depth * ff_cols

    factors = ((r.grad_gate, r.mlp_in), (r.grad_up, r.mlp_in), (r.hidden, r.grad_down))

    def side_terms(index, side):
        left, right = factors[index]
        return rows_dot(left[side], right[side].reshape(2 * rows, width), 0, 0)

    def near_terms():
        for index in range(3):
            r.ff_wide[index] = side_terms(index, y)

    def far_terms(index):
        terms = (r.ff_wide[index] + side_terms(index, 1 - y)).astype(narrow)
        r.ff_terms[:, :, pl.ds(index * ff_cols, ff_cols)] = terms.reshape(depth, 2, ff_cols, width)

    ff_across = {}

    both = 2 * ff_cols

    def ff_terms_to_x(offset):
        source = r.ff_terms.at[deep(offset), 1 - x, pl.ds(0, both)]
        ff_across[offset] = mail.push(source, r.ff_near.at[offset], x_peer)

    down_copies = []

    def down_terms():
        far_terms(2)
        for offset in range(1, depth):
            source = r.ff_terms.at[deep(offset), :, pl.ds(both, ff_cols)]
            down_copies.append(mail.push(source, r.down_got.at[offset], z_peer(offset)))

    def down_step():
        summed = r.ff_terms[d, :, pl.ds(both, ff_cols)].astype(wide)
        for copy in down_copies:
            copy.wait_recv()
        for offset in range(1, depth):
            summed += r.down_got[offset].astype(wide)
        r.down_wide[...] = summed
        r.down_sums[...] = summed.astype(narrow)
        return mail.push(r.down_sums.at[1 - x], r.down_near_sum, x_peer)

    def gate_terms():
        far_terms(0)
        far_terms(1)
        for offset in range(1, depth):
            ff_terms_to_x(offset)

    near_copy, y_copy = share_rows("grad_down", grad_down_raw.astype(narrow))
    grad_mlp_in = group_sum(
        "mlp_back",
        backward_half,
        (near_copy, lambda: far_rows("grad_down", y_copy)),
        near_terms,
        down_terms,
        gate_terms,
    )
    middle = r.middle[...]
    inverse_mid = norm_rows(middle, r.norm_gains[2:3])[1]
    grad_mid_part, gain_two = norm_back(middle, inverse_mid, r.norm_gains[2:3], grad_mlp_in)
    r.gains[2:3] = jnp.sum(gain_two, axis=0, keepdims=True)
    grad_middle = r.cotangent[...].astype(wide) + grad_mid_part
    r.grad_middle[...] = grad_middle
    branch = r.branch[...]
    inverse_branch = norm_rows(branch, r.norm_gains[1:2])[1]
    grad_branch_raw, gain_one = norm_back(branch, inverse_branch, r.norm_gains[1:2], grad_middle)
    r.gains[1:2] = jnp.sum(gain_one, axis=0, keepdims=True)
    grad_branch = grad_branch_raw.astype(narrow)
    branch_c, branch_y = share_rows("branch_all", grad_branch)

    head_grad = rows_dot(grad_branch, out_weight, 1, 1).astype(narrow)
    for head in range(heads):
        r.head_grad[head] = head_grad[:, head * head_width : (head + 1) * head_width]

    ff_deep = []

    def ff_step(offset):
        ff_across[offset].wait_recv()
        summed = r.ff_terms[deep(offset), x, pl.ds(0, both)].astype(wide) + r.ff_near[offset].astype(wide)
        if offset:
            r.ff_sum[offset] = summed.astype(narrow)
            ff_deep.append(mail.push(r.ff_sum.at[offset], r.ff_got.at[offset], z_peer(offset)))
        else:
            r.ff_own[...] = summed

    for head in range(heads):
        grad_rows = r.head_grad[head]
        delta = jnp.sum(grad_rows.astype(wide) * r.exact[head], axis=1, keepdims=True)
        grad_probs = rows_dot(grad_rows, r.values[...], 1, 1)
        r.grad_scores[head] = (r.probs[head] * (grad_probs - delta)).astype(narrow)
    ff_step(1)
    all_grads = r.head_grad[...].reshape(heads * rows, head_width)
    all_queries = r.q_rot[...].reshape(heads * rows, head_width)
    kv_near = []
    for pair in range(4):
        here = slice(2 * pair * rows, 2 * (pair + 1) * rows)
        px, py = pair // 2, pair % 2
        key_part = rows_dot(
            r.grad_scores[:, :, here].reshape(heads * rows, 2 * rows), all_queries, 0, 0
        )
        value_part = rows_dot(
            r.probs_narrow[:, :, here].reshape(heads * rows, 2 * rows), all_grads, 0, 0
        )
        r.kv_terms[px, py, :, :, :head_width] = key_part.astype(narrow).reshape(2, rows, head_width)
        r.kv_terms[px, py, :, :, head_width:] = value_part.astype(narrow).reshape(2, rows, head_width)
        kv_near.append(mail.push(r.kv_terms.at[px, py, 1 - c], r.kv_near.at[px, py], c_peer))
    ff_step(2)
    branch_far = far_rows("branch_all", branch_y)

    cosine, sine_part = r.cosine[me], r.sine[me]
    gain_query = jnp.zeros((1, head_width), wide)
    for head in range(heads):
        here = slice(head * head_width, (head + 1) * head_width)
        turned = rows_dot(r.grad_scores[head], r.keys[...], 1, 0) * score_scale
        upstream = rotate(turned, cosine, -sine_part)
        query_raw = r.q_raw[:, here]
        inverse = norm_rows(query_raw, query_gain)[1]
        grad_raw, gain_rows = norm_back(query_raw, inverse, query_gain, upstream)
        gain_query += jnp.sum(gain_rows, axis=0, keepdims=True)
        r.grad_query[:, here] = grad_raw.astype(narrow)
    r.gains[4:5, :head_width] = gain_query

    for px in bits:
        for py in bits:
            kv_near[2 * px + py].wait_recv()
            summed = r.kv_terms[px, py, c].astype(wide) + r.kv_near[px, py].astype(wide)
            r.kv_sums[px, py] = summed.astype(narrow)
    kv_copies = []
    for number, (dx, dy) in enumerate(chip_steps):
        kv_copies.append(
            mail.push(
                r.kv_sums.at[flip(x, dx), flip(y, dy)], r.kv_far.at[number], plane_peer(dx, dy, 0)
            )
        )
    turned_blocks("query_turned", r.grad_query[...], query_cols)
    query_copies = send_factor("query_turned")
    ff_step(3)
    down_copy = down_step()
    ff_terms_to_x(0)

    def deep_copies(name):
        return [
            mail.push(getattr(r, name + "_terms").at[deep(offset)], getattr(r, name + "_far").at[offset], z_peer(offset))
            for offset in range(1, depth)
        ]

    for copy in out_copies + [branch_c, branch_far]:
        copy.wait_recv()
    terms = jnp.zeros((2 * depth * query_cols, width), wide)
    for py in bits:
        for pc in bits:
            left = r.out_turned_got[py, pc].reshape(2 * depth * query_cols, rows)
            terms += rows_dot(left, r.branch_all[py, pc], 1, 0)
    r.out_both[...] = terms.astype(narrow).reshape(depth, 2, query_cols, width)
    out_near = mail.push(r.out_both.at[:, 1 - x], r.out_near, x_peer)
    query_part = rows_dot(r.grad_query[...], r.q_all[...].reshape(full, width), 1, 0)
    r.query_part[...] = query_part

    def weight_terms(name, copies, columns):
        for copy in copies:
            copy.wait_recv()
        terms = jnp.zeros((depth * columns, width), wide)
        for block in range(8):
            left = getattr(r, name + "_got")[block].reshape(depth * columns, rows)
            terms += rows_dot(left, r.attn_in[block], 1, 0)
        getattr(r, name + "_wide")[...] = terms.reshape(depth, columns, width)
        getattr(r, name + "_terms")[...] = terms.astype(narrow).reshape(depth, columns, width)
        return deep_copies(name)

    for offset in range(4, depth):
        ff_step(offset)
    for copy in kv_copies:
        copy.wait_recv()
    kv_sum = r.kv_sums[x, y].astype(wide)
    for number in range(len(chip_steps)):
        kv_sum += r.kv_far[number].astype(wide)
    key_gain = r.qk_gains[1:2]
    key_raw = r.key_raw[me]
    key_back = rotate(kv_sum[:, :head_width], cosine, -sine_part)
    inverse_key = norm_rows(key_raw, key_gain)[1]
    grad_key_raw, gain_key = norm_back(key_raw, inverse_key, key_gain, key_back)
    r.gains[5:6, :head_width] = jnp.sum(gain_key, axis=0, keepdims=True)
    r.grad_kv[:, :head_width] = grad_key_raw.astype(narrow)
    r.grad_kv[:, head_width:] = kv_sum[:, head_width:].astype(narrow)
    kv_turned = rows_dot(r.unsort[...], r.grad_kv[...], 1, 1).astype(narrow)
    r.kv_turned[...] = kv_turned.reshape(depth, 2, 2, 2, 2 * key_cols, rows)
    kv_factor_copies = send_factor("kv_turned")

    grad_attn_in = r.query_part[...] + rows_dot(r.grad_kv[...], r.kv_sorted[...], 1, 0)
    input_wide = r.block_in[...].astype(wide)
    inverse_in = norm_rows(input_wide, r.norm_gains[0:1])[1]
    grad_in_part, gain_zero = norm_back(input_wide, inverse_in, r.norm_gains[0:1], grad_attn_in)
    r.d_block_in[...] = (r.grad_middle[...] + grad_in_part).astype(narrow)
    r.gains[0:1] = jnp.sum(gain_zero, axis=0, keepdims=True)
    gain_copies = [
        mail.push(r.gains, r.gains_got.at[number], plane_peer(*step))
        for number, step in enumerate(plane_steps)
    ]

    query_deep = weight_terms("query_turned", query_copies, query_cols)
    out_near.wait_recv()
    summed = r.out_both[:, x].astype(wide) + r.out_near[...].astype(wide)
    r.out_turned_wide[...] = summed
    r.out_turned_terms[...] = summed.astype(narrow)
    out_deep = deep_copies("out_turned")
    kv_deep = weight_terms("kv_turned", kv_factor_copies, 2 * key_cols)
    gain_sum = r.gains[...]
    for number, copy in enumerate(gain_copies):
        copy.wait_recv()
        gain_sum += r.gains_got[number]
    r.gains_sum[...] = gain_sum
    gain_deep = [
        mail.push(r.gains_sum, r.gains_deep.at[offset], z_peer(offset)) for offset in range(1, depth)
    ]
    ff_step(0)

    def deep_sum(own, far, copies):
        for number, copy in enumerate(copies):
            copy.wait_recv()
            own += far[number + 1].astype(wide)
        return own

    r.grad_q_rows[...] = deep_sum(r.query_turned_wide[d], r.query_turned_far, query_deep)
    r.grad_o_rows[...] = deep_sum(r.out_turned_wide[d], r.out_turned_far, out_deep)
    r.grad_ff_rows[:both] = deep_sum(r.ff_own[...], r.ff_got, ff_deep)
    down_copy.wait_recv()
    r.grad_ff_rows[both:] = r.down_wide[x] + r.down_near_sum[...].astype(wide)
    r.grad_kv_rows[...] = deep_sum(r.kv_turned_wide[d], r.kv_turned_far, kv_deep)
    r.gains_out[...] = deep_sum(r.gains_sum[...], r.gains_deep, gain_deep)
    mail.settle()


def split_kernel(block_ref, back_ref, gains_ref, q_ref, o_ref, kv_ref, ff_ref, *outs):
    key_cols, ff_cols = outs[5].shape[0], outs[8].shape[0]
    outs[0][...] = block_ref[...]
    outs[1][...] = back_ref[...]
    norm_count = outs[2].shape[0]
    outs[2][...] = gains_ref[:norm_count]
    outs[3][...] = gains_ref[norm_count : norm_count + outs[3].shape[0], : outs[3].shape[1]]
    outs[4][...] = q_ref[...]
    outs[5][...] = kv_ref[:key_cols]
    outs[6][...] = kv_ref[key_cols:]
    outs[7][...] = o_ref[...]
    for piece in range(3):
        outs[8 + piece][...] = ff_ref[piece * ff_cols : (piece + 1) * ff_cols]


def fused_local(
    block_in,
    cotangent,
    positions,
    norm_gains,
    qk_gains,
    w_query,
    w_key,
    w_value,
    w_out,
    w_gate,
    w_up,
    w_down,
):
    narrow, wide = jnp.bfloat16, jnp.float32
    rows, width = block_in.shape
    head_width = qk_gains.shape[1]
    depth = lax.axis_size("dp")
    query_cols, key_cols, ff_cols = w_query.shape[1], w_key.shape[1], w_gate.shape[1]
    full = query_cols * lax.axis_size(every_axis)
    heads = full // head_width
    plane = lax.axis_size(sequence_axes)
    length = plane * rows
    ff_width = 2 * depth * ff_cols
    operands = dict(
        block_in=block_in,
        cotangent=cotangent,
        positions=positions.reshape(-1, rows),
        norm_gains=norm_gains,
        qk_gains=qk_gains,
        q_rows=w_query.T,
        o_rows=w_out,
        key_rows=w_key.T,
        value_rows=w_value.T,
        gate_rows=w_gate.T,
        up_rows=w_up.T,
        down_rows=w_down,
    )
    results = dict(
        block_out=((rows, width), narrow),
        d_block_in=((rows, width), narrow),
        gains_out=((8, width), wide),
        grad_q_rows=((query_cols, width), wide),
        grad_o_rows=((query_cols, width), wide),
        grad_kv_rows=((2 * key_cols, width), wide),
        grad_ff_rows=((3 * ff_cols, width), wide),
    )
    cube = (depth, 2, 2, 2)
    scratch = dict(
        block_all=((2, 2, 2, rows, width), narrow),
        kv_all=(cube + (2 * key_cols, width), narrow),
        q_all=(cube + (query_cols, width), narrow),
        o_all=(cube + (query_cols, width), narrow),
        ff_all=((depth, 2, 3 * ff_cols, width), narrow),
        pos_pair=((2, plane // 2, rows), wide),
        pos_all=((plane, rows), wide),
        pos_own=((rows, 1), wide),
        cosine=((plane, rows, head_width // 2), wide),
        sine=((plane, rows, head_width // 2), wide),
        sort=((2 * head_width, 2 * head_width), narrow),
        unsort=((2 * head_width, 2 * head_width), narrow),
        attn_in=((plane, rows, width), narrow),
        kv_sorted=((2 * head_width, width), narrow),
        key_raw=((plane, rows, head_width), wide),
        keys=((length, head_width), narrow),
        values=((length, head_width), narrow),
        q_raw=((rows, full), wide),
        q_rot=((heads, rows, head_width), narrow),
        bias=((rows, length), wide),
        probs=((heads, rows, length), wide),
        probs_narrow=((heads, rows, length), narrow),
        exact=((heads, rows, head_width), wide),
        attn_out=((rows, full), narrow),
        branch=((rows, width), wide),
        middle=((rows, width), wide),
        mlp_in=((2, 2, rows, width), narrow),
        gate_pre=((2, 2 * rows, ff_width), wide),
        up_pre=((2, 2 * rows, ff_width), wide),
        hidden=((2, 2 * rows, ff_width), narrow),
        down_raw=((rows, width), wide),
        grad_down=((2, 2, rows, width), narrow),
        grad_gate=((2, 2 * rows, ff_width), narrow),
        grad_up=((2, 2 * rows, ff_width), narrow),
        grad_middle=((rows, width), wide),
        branch_all=((2, 2, rows, width), narrow),
        out_both=((depth, 2, query_cols, width), narrow),
        out_near=((depth, query_cols, width), narrow),
        ff_wide=((3, ff_width, width), wide),
        head_grad=((heads, rows, head_width), narrow),
        grad_scores=((heads, rows, length), narrow),
        grad_query=((rows, full), narrow),
        query_part=((rows, width), wide),
        grad_kv=((rows, 2 * head_width), narrow),
        kv_terms=((2, 2, 2, rows, 2 * head_width), narrow),
        kv_near=((2, 2, rows, 2 * head_width), narrow),
        kv_sums=((2, 2, rows, 2 * head_width), narrow),
        kv_far=((3, rows, 2 * head_width), narrow),
        ff_terms=((depth, 2, 3 * ff_cols, width), narrow),
        ff_near=((depth, 2 * ff_cols, width), narrow),
        ff_sum=((depth, 2 * ff_cols, width), narrow),
        ff_got=((depth, 2 * ff_cols, width), narrow),
        ff_own=((2 * ff_cols, width), wide),
        down_got=((depth, 2, ff_cols, width), narrow),
        down_wide=((2, ff_cols, width), wide),
        down_sums=((2, ff_cols, width), narrow),
        down_near_sum=((ff_cols, width), narrow),
        gains=((8, width), wide),
        gains_got=((plane - 1, 8, width), wide),
        gains_sum=((8, width), wide),
        gains_deep=((depth, 8, width), wide),
    )
    for name in ("down", "mlp_back"):
        scratch[name] = ((2, 2, rows, width), narrow)
        scratch[name + "_near"] = ((2, rows, width), narrow)
        scratch[name + "_sum"] = ((rows, width), narrow)
        scratch[name + "_far"] = ((rows, width), narrow)
    for name, columns in (("out_turned", query_cols), ("query_turned", query_cols), ("kv_turned", 2 * key_cols)):
        scratch[name] = (cube + (columns, rows), narrow)
        scratch[name + "_got"] = ((plane, depth, columns, rows), narrow)
        scratch[name + "_wide"] = ((depth, columns, width), wide)
        scratch[name + "_terms"] = ((depth, columns, width), narrow)
        scratch[name + "_far"] = ((depth, columns, width), narrow)
    scratch["out_turned_got"] = ((2, 2, depth, 2, query_cols, rows), narrow)
    names = list(operands) + list(results) + list(scratch) + ["send_sems", "recv_sems"]
    in_vmem = pl.BlockSpec(memory_space=pltpu.VMEM)
    outs = pl.pallas_call(
        lambda *refs: fused_kernel(names, *refs),
        out_shape=[jax.ShapeDtypeStruct(*result) for result in results.values()],
        in_specs=[in_vmem] * len(operands),
        out_specs=[in_vmem] * len(results),
        scratch_shapes=[pltpu.VMEM(*one) for one in scratch.values()]
        + [pltpu.SemaphoreType.DMA((copy_limit,))] * 2,
        compiler_params=pltpu.CompilerParams(
            collective_id=11, has_side_effects=True, vmem_limit_bytes=56 * 1024 * 1024
        ),
        name="layer",
    )(*operands.values())
    parts = [
        ((rows, width), narrow),
        ((rows, width), narrow),
        (norm_gains.shape, wide),
        (qk_gains.shape, wide),
        ((query_cols, width), wide),
        ((key_cols, width), wide),
        ((key_cols, width), wide),
        ((query_cols, width), wide),
        ((ff_cols, width), wide),
        ((ff_cols, width), wide),
        ((ff_cols, width), wide),
    ]
    parts = pl.pallas_call(
        split_kernel,
        out_shape=[jax.ShapeDtypeStruct(*part) for part in parts],
        in_specs=[in_vmem] * len(results),
        out_specs=[in_vmem] * len(parts),
        name="split",
    )(*outs)
    turned = (4, 5, 6, 8, 9)
    return tuple(part.T if index in turned else part for index, part in enumerate(parts))


def fits_fused(block_in, w_query, w_key, w_gate):
    tiles = (w_query.shape[1], 2 * w_key.shape[1], w_gate.shape[1])
    return (
        lax.axis_size("ctx") == 2
        and lax.axis_size("head") == 4
        and block_in.shape[0] % 128 == 0
        and all(columns % 16 == 0 for columns in tiles)
    )


def either_local(*args):
    if fits_fused(args[0], args[5], args[6], args[9]):
        return fused_local(*args)
    return local(*args)


def solution(mesh):
    in_specs = (
        P(every_axis, None),
        P(every_axis, None),
        P(weight_axes),
        P(),
        P(),
        P(None, every_axis),
        P(None, every_axis),
        P(None, every_axis),
        P(every_axis, None),
        P(None, every_axis),
        P(None, every_axis),
        P(every_axis, None),
    )
    out_specs = (
        P(every_axis, None),
        P(every_axis, None),
        P(),
        P(),
        P(None, every_axis),
        P(None, every_axis),
        P(None, every_axis),
        P(every_axis, None),
        P(None, every_axis),
        P(None, every_axis),
        P(every_axis, None),
    )
    return jax.shard_map(either_local, mesh=mesh, in_specs=in_specs, out_specs=out_specs, check_vma=False)
```

```python
import math
import types

import jax
import jax.numpy as jnp
from jax import lax
from jax.experimental import pallas as pl
from jax.experimental.pallas import tpu as pltpu
from jax.sharding import PartitionSpec as P

epsilon = 1e-06
rope_base = 1000000.0
score_scale = 0.0625
negative_fill = -1e30


def norm_rows(values, gain_vec):
    inverse = lax.rsqrt(jnp.mean(values * values, axis=-1, keepdims=True) + epsilon)
    return (values * inverse * gain_vec, inverse)


def norm_back(values, inverse, gain_vec, upstream):
    scaled = upstream * gain_vec
    inner_mean = jnp.mean(scaled * values, axis=-1, keepdims=True)
    return (
        inverse * scaled - values * (inverse * inverse * inverse) * inner_mean,
        upstream * values * inverse,
    )


def rope_angles(positions, full_width):
    ladder = jnp.arange(full_width // 2, dtype=jnp.float32)
    frequency = jnp.exp(ladder * (-2.0 / full_width) * math.log(rope_base))
    angles = positions.astype(jnp.float32)[:, None] * frequency[None, :]
    return (jnp.cos(angles), jnp.sin(angles))


def rotate(values, cosine, sine_part):
    middle = values.shape[-1] // 2
    first_half = values[..., :middle]
    second = values[..., middle:]
    return jnp.concatenate(
        [first_half * cosine - second * sine_part, second * cosine + first_half * sine_part],
        axis=-1,
    )


def gelu_product(gate_pre, up_pre):
    return jax.nn.gelu(gate_pre, approximate=True) * up_pre


every_axis = ("dp", "ctx", "head")
sequence_axes = ("ctx", "head")
weight_axes = ("dp", "ctx")


def place_in(axes):
    place = 0
    for name in axes:
        place = place * lax.axis_size(name) + lax.axis_index(name)
    return place


def coordinates(axes, place):
    found = {}
    for name in reversed(axes):
        size = lax.axis_size(name)
        found[name] = lax.rem(place, size)
        place = place // size
    return found


def each_peer(count, step):
    if count <= 8:
        for offset in range(1, count):
            step(offset)
    else:

        def looped(offset, carry):
            step(offset)
            return carry

        lax.fori_loop(1, count, looped, 0)


def exchange_kernel(kinds, greet, counts, *refs):
    total = len(kinds)
    sources, targets, sems = refs[:total], refs[total : 2 * total], refs[2 * total :]
    barrier = pltpu.get_barrier_semaphore()
    waits = 0
    for axes, count in greet:
        me = place_in(axes)

        def greet_peer(offset, axes=axes, count=count, me=me):
            pl.semaphore_signal(
                barrier,
                inc=1,
                device_id=coordinates(axes, lax.rem(me + offset, count)),
                device_id_type=pl.DeviceIdType.MESH,
            )

        each_peer(count, greet_peer)
        waits += count - 1
    locals_started = []
    for part, (kind, axes) in enumerate(kinds):
        me = place_in(axes)
        source = {"scatter": me, "relative": 0}.get(kind)
        source = sources[part] if source is None else sources[part].at[source]
        copy = pltpu.make_async_copy(source, targets[part].at[me], sems[3 * part + 2].at[0])
        copy.start()
        locals_started.append(copy)
    pl.semaphore_wait(barrier, waits)

    def descriptor(part, offset, backward):
        kind, axes = kinds[part]
        count = counts[part]
        me = place_in(axes)
        to = lax.rem(me + offset, count)
        origin = lax.rem(me + count - offset, count) if backward else me
        source = {"scatter": to, "relative": lax.rem(count - offset, count)}.get(kind)
        source = sources[part] if source is None else sources[part].at[source]
        return pltpu.make_async_remote_copy(
            src_ref=source,
            dst_ref=targets[part].at[origin],
            send_sem=sems[3 * part].at[offset],
            recv_sem=sems[3 * part + 1].at[origin],
            device_id=coordinates(axes, to),
            device_id_type=pl.DeviceIdType.MESH,
        )

    for part in range(total):
        each_peer(counts[part], lambda offset: descriptor(part, offset, False).start())
    for copy in locals_started:
        copy.wait()
    for part in range(total):
        each_peer(counts[part], lambda offset: descriptor(part, offset, True).wait_recv())
    for part in range(total):
        each_peer(counts[part], lambda offset: descriptor(part, offset, False).wait_send())


def exchange(call_id, name, parts, greet_axes=None):
    kinds = tuple((kind, axes) for kind, axes, _ in parts)
    arrays = [array for _, _, array in parts]
    counts = tuple(lax.axis_size(axes) for _, axes in kinds)
    if greet_axes is None:
        greet_axes = (kinds[0][1],)
    greet = tuple((axes, lax.axis_size(axes)) for axes in greet_axes)
    shapes = [
        jax.ShapeDtypeStruct(
            (count,) + array.shape if kind == "gather" else array.shape, array.dtype
        )
        for (kind, _, array), count in zip(parts, counts)
    ]
    scratch = []
    for count in counts:
        scratch += [
            pltpu.SemaphoreType.DMA((count,)),
            pltpu.SemaphoreType.DMA((count,)),
            pltpu.SemaphoreType.DMA((1,)),
        ]
    in_vmem = pl.BlockSpec(memory_space=pltpu.VMEM)
    return pl.pallas_call(
        lambda *refs: exchange_kernel(kinds, greet, counts, *refs),
        out_shape=shapes,
        in_specs=[in_vmem] * len(arrays),
        out_specs=[in_vmem] * len(arrays),
        scratch_shapes=scratch,
        compiler_params=pltpu.CompilerParams(collective_id=call_id, has_side_effects=True),
        name=name,
    )(*arrays)


def digit_place(digit):
    if digit == "head_slow":
        return lax.axis_index("head") // fast_size()
    if digit == "head_fast":
        return lax.rem(lax.axis_index("head"), fast_size())
    return lax.axis_index(digit)


def fast_size():
    return 2 if lax.axis_size("head") % 2 == 0 else 1


def digit_size(digit):
    if digit == "head_slow":
        return lax.axis_size("head") // fast_size()
    if digit == "head_fast":
        return fast_size()
    return lax.axis_size(digit)


def digit_device(digit, value):
    if digit == "head_slow":
        return {"head": value * fast_size() + digit_place("head_fast")}
    if digit == "head_fast":
        return {"head": digit_place("head_slow") * fast_size() + value}
    return {digit: value}


def staged_kernel(plans, greeted, *refs):
    total = len(plans)
    sources, targets, sems = refs[:total], refs[total : 2 * total], list(refs[2 * total :])
    barrier = pltpu.get_barrier_semaphore()
    waits = 0
    for digit in greeted:
        count, me = digit_size(digit), digit_place(digit)
        for offset in range(1, count):
            pl.semaphore_signal(
                barrier,
                inc=1,
                device_id=digit_device(digit, lax.rem(me + offset, count)),
                device_id_type=pl.DeviceIdType.MESH,
            )
            waits += 1
    local_sems = sems[:total]
    rest = sems[total:]
    pairs = []
    for plan in plans:
        pairs.append([(rest.pop(0), rest.pop(0)) for _ in plan])
    own = []
    for part, plan in enumerate(plans):
        here = tuple(digit_place(digit) for digit in reversed(plan))
        copy = pltpu.make_async_copy(sources[part], targets[part].at[here], local_sems[part].at[0])
        copy.start()
        own.append(copy)
    pl.semaphore_wait(barrier, waits)

    def descriptors(part, turn, backward):
        plan = plans[part]
        digit = plan[turn]
        count, me = digit_size(digit), digit_place(digit)
        outer = tuple(digit_place(name) for name in reversed(plan[turn + 1 :]))
        found = []
        for offset in range(1, count):
            to = lax.rem(me + offset, count)
            origin = lax.rem(me + count - offset, count) if backward else me
            source = sources[part] if turn == 0 else targets[part].at[outer + (me,)]
            found.append(
                pltpu.make_async_remote_copy(
                    src_ref=source,
                    dst_ref=targets[part].at[outer + (origin,)],
                    send_sem=pairs[part][turn][0].at[offset],
                    recv_sem=pairs[part][turn][1].at[origin],
                    device_id=digit_device(digit, to),
                    device_id_type=pl.DeviceIdType.MESH,
                )
            )
        return found

    most = max(len(plan) for plan in plans)
    for turn in range(most + 1):
        for part, plan in enumerate(plans):
            if 0 < turn <= len(plan):
                for copy in descriptors(part, turn - 1, True):
                    copy.wait_recv()
            if turn == 1:
                own[part].wait()
            if turn < len(plan):
                for copy in descriptors(part, turn, False):
                    copy.start()
    for part, plan in enumerate(plans):
        for turn in range(len(plan)):
            for copy in descriptors(part, turn, False):
                copy.wait_send()


def staged_gather(call_id, name, parts):
    plans = [plan for plan, _ in parts]
    arrays = [array for _, array in parts]
    greeted = []
    for plan in plans:
        greeted += [digit for digit in plan if digit not in greeted]
    shapes = [
        jax.ShapeDtypeStruct(
            tuple(digit_size(digit) for digit in reversed(plan)) + array.shape, array.dtype
        )
        for plan, array in parts
    ]
    scratch = [pltpu.SemaphoreType.DMA((1,)) for _ in parts]
    for plan in plans:
        for digit in plan:
            scratch += [pltpu.SemaphoreType.DMA((digit_size(digit),))] * 2
    in_vmem = pl.BlockSpec(memory_space=pltpu.VMEM)
    return pl.pallas_call(
        lambda *refs: staged_kernel(plans, greeted, *refs),
        out_shape=shapes,
        in_specs=[in_vmem] * len(arrays),
        out_specs=[in_vmem] * len(arrays),
        scratch_shapes=scratch,
        compiler_params=pltpu.CompilerParams(collective_id=call_id, has_side_effects=True),
        name=name,
    )(*arrays)


def gather_rows(call_id, name, rows):
    (blocks,) = exchange(call_id, name, [("gather", ("head",), rows)])
    return blocks.reshape(-1, rows.shape[1])


def shifted(array, axis, offset):
    count = lax.axis_size(axis)
    return lax.ppermute(array, axis, [(here, (here + offset) % count) for here in range(count)])


def gelu_parts(value):
    root = math.sqrt(2.0 / math.pi)
    square = value * value
    tanh_part = jnp.tanh(root * (value + 0.044715 * value * square))
    gelu = 0.5 * value * (1.0 + tanh_part)
    slope = 0.5 * (1.0 + tanh_part) + 0.5 * value * (1.0 - tanh_part * tanh_part) * root * (
        1.0 + 3.0 * 0.044715 * square
    )
    return gelu, slope


def mlp_forward_kernel(rows_ref, gate_ref, up_ref, down_ref, gate_pre_ref, up_pre_ref, hidden_ref, part_ref):
    rows = rows_ref[...]
    gate_pre = rows_dot(rows, gate_ref[...], 1, 1)
    up_pre = rows_dot(rows, up_ref[...], 1, 1)
    gate_pre_ref[...] = gate_pre
    up_pre_ref[...] = up_pre
    hidden = (gelu_parts(gate_pre)[0] * up_pre).astype(jnp.bfloat16)
    hidden_ref[...] = hidden
    part_ref[...] = rows_dot(hidden, down_ref[...], 1, 0).astype(jnp.bfloat16)


def mlp_backward_kernel(
    rows_ref, gate_ref, up_ref, down_ref, gate_pre_ref, up_pre_ref, grad_gate_ref, grad_up_ref, part_ref
):
    grad_hidden = rows_dot(rows_ref[...], down_ref[...], 1, 1)
    gelu, slope = gelu_parts(gate_pre_ref[...])
    grad_gate = (grad_hidden * up_pre_ref[...] * slope).astype(jnp.bfloat16)
    grad_up = (grad_hidden * gelu).astype(jnp.bfloat16)
    grad_gate_ref[...] = grad_gate
    grad_up_ref[...] = grad_up
    part_ref[...] = (
        rows_dot(grad_gate, gate_ref[...], 1, 0) + rows_dot(grad_up, up_ref[...], 1, 0)
    ).astype(jnp.bfloat16)


def rows_dot(left, right, left_dim, right_dim):
    return lax.dot_general(
        left, right, (((left_dim,), (right_dim,)), ((), ())), preferred_element_type=jnp.float32
    )


def add_up(blocks):
    return jnp.sum(blocks.astype(jnp.float32), axis=0)


def local(
    block_in,
    cotangent,
    positions,
    norm_gains,
    qk_gains,
    w_query,
    w_key,
    w_value,
    w_out,
    w_gate,
    w_up,
    w_down,
):
    tok_rows, model_width = block_in.shape
    head_count = lax.axis_size("head")
    head_width = qk_gains.shape[1]
    ctx_slot = lax.axis_index("ctx")
    query_rows = head_count * tok_rows
    group_count = lax.axis_size(weight_axes)
    every_count = lax.axis_size(every_axis)
    length_all = lax.axis_size(sequence_axes) * tok_rows
    query_cols = w_query.shape[1]
    key_cols = w_key.shape[1]
    ff_cols = w_gate.shape[1]
    narrow = jnp.bfloat16

    ff_rows = jnp.concatenate([w_gate.T, w_up.T, w_down], axis=0)
    dp_count, ctx_count = lax.axis_size("dp"), lax.axis_size("ctx")

    to_heads = [
        (head * group_count + index, index * head_count + head)
        for head in range(head_count)
        for index in range(group_count)
    ]
    to_owners = [(there, here) for here, there in to_heads]
    head_rows = lax.ppermute(
        jnp.concatenate([w_query.T, w_out], axis=0), every_axis, to_heads
    )
    key_value_rows = jnp.concatenate([w_key.T, w_value.T], axis=0)
    block_all, key_value_all, head_all, position_all = staged_gather(
        1,
        "first_gather",
        [
            (("ctx", "head_slow", "head_fast"), block_in),
            (("dp", "ctx", "head_slow", "head_fast"), key_value_rows),
            (("dp", "ctx"), head_rows),
            (("ctx",), positions.reshape(-1, 128)),
        ],
    )
    block_all, ff_rows = lax.optimization_barrier((block_all, ff_rows))
    near_blocks = [ff_rows] + [shifted(ff_rows, "dp", offset) for offset in range(1, dp_count)]
    ff_across = [shifted(ff_rows, "ctx", offset) for offset in range(1, ctx_count)]
    block_all = block_all.transpose(2, 1, 0, 3, 4)
    key_value_all = key_value_all.transpose(3, 2, 1, 0, 4, 5).reshape(
        every_count, 2 * key_cols, model_width
    )
    head_all = head_all.transpose(1, 0, 2, 3).reshape(group_count, 2 * query_cols, model_width)
    query_weight = head_all[:, :query_cols].reshape(head_width, model_width)
    out_weight = head_all[:, query_cols:].reshape(head_width, model_width)
    key_weight = key_value_all[:, :key_cols].reshape(head_width, model_width)
    value_weight = key_value_all[:, key_cols:].reshape(head_width, model_width)

    input_all = block_all.reshape(length_all, model_width).astype(jnp.float32)
    attn_in_all = norm_rows(input_all, norm_gains[0])[0].astype(narrow)
    first_query = ctx_slot * query_rows
    attn_in = lax.dynamic_slice_in_dim(attn_in_all, first_query, query_rows)
    query_raw = rows_dot(attn_in, query_weight, 1, 1)
    key_raw = rows_dot(attn_in_all, key_weight, 1, 1)
    all_values = rows_dot(attn_in_all, value_weight, 1, 1).astype(narrow)
    query_normed, inverse_query = norm_rows(query_raw, qk_gains[0])
    key_normed, inverse_key = norm_rows(key_raw, qk_gains[1])
    cosine, sine_part = rope_angles(position_all.reshape(length_all), head_width)
    cosine_own = lax.dynamic_slice_in_dim(cosine, first_query, query_rows)
    sine_own = lax.dynamic_slice_in_dim(sine_part, first_query, query_rows)
    head_query = (rotate(query_normed, cosine_own, sine_own) * score_scale).astype(narrow)
    all_keys = rotate(key_normed, cosine, sine_part).astype(narrow)

    query_index = first_query + jnp.arange(query_rows, dtype=jnp.int32)
    lowest_key = query_index - positions
    key_index = jnp.arange(length_all, dtype=jnp.int32)
    visible = (key_index[None, :] <= query_index[:, None]) & (
        key_index[None, :] >= lowest_key[:, None]
    )
    scores = jnp.where(visible, rows_dot(head_query, all_keys, 1, 1), negative_fill)
    top = jnp.max(scores, axis=1, keepdims=True)
    log_total = top + jnp.log(jnp.sum(jnp.exp(scores - top), axis=1, keepdims=True))
    probs_wide = jnp.exp(scores - log_total)
    prob_rows = probs_wide.astype(narrow)
    attn_exact = rows_dot(prob_rows, all_values, 1, 0)
    attn_out = attn_exact.astype(narrow)
    branch_part = rows_dot(attn_out, out_weight, 1, 0).astype(narrow)
    (branch_blocks,) = exchange(
        2,
        "branch_scatter",
        [("scatter", ("head",), branch_part.reshape(head_count, tok_rows, model_width))],
    )
    branch = add_up(branch_blocks)
    input_wide = block_in.astype(jnp.float32)
    inverse_in = norm_rows(input_wide, norm_gains[0])[1]
    branch_normed, inverse_branch = norm_rows(branch, norm_gains[1])
    middle = input_wide + branch_normed
    mlp_norm, inverse_mid = norm_rows(middle, norm_gains[2])
    mlp_norm, near_blocks, ff_across = lax.optimization_barrier((mlp_norm, near_blocks, ff_across))
    ff_slots = list(near_blocks)
    for offset in range(1, ctx_count):
        ff_slots += [ff_across[offset - 1]]
        ff_slots += [shifted(block, "ctx", offset) for block in near_blocks[1:]]
    mlp_in = gather_rows(3, "mlp_gather", mlp_norm.astype(narrow))

    ff_width = group_count * ff_cols
    gate_weight = jnp.concatenate([block[:ff_cols] for block in ff_slots], axis=0)
    up_weight = jnp.concatenate([block[ff_cols : 2 * ff_cols] for block in ff_slots], axis=0)
    down_weight = jnp.concatenate([block[2 * ff_cols :] for block in ff_slots], axis=0)
    wide_ff = jax.ShapeDtypeStruct((query_rows, ff_width), jnp.float32)
    narrow_ff = jax.ShapeDtypeStruct((query_rows, ff_width), narrow)
    narrow_rows = jax.ShapeDtypeStruct((query_rows, model_width), narrow)
    gate_pre, up_pre, hidden, down_part = pl.pallas_call(
        mlp_forward_kernel,
        out_shape=[wide_ff, wide_ff, narrow_ff, narrow_rows],
        name="mlp_forward",
    )(mlp_in, gate_weight, up_weight, down_weight)
    (down_blocks,) = exchange(
        4,
        "down_scatter",
        [("scatter", ("head",), down_part.reshape(head_count, tok_rows, model_width))],
    )
    down_raw = add_up(down_blocks)
    down_normed, inverse_down = norm_rows(down_raw, norm_gains[3])
    block_out = (middle + down_normed).astype(narrow)
    cot_wide = cotangent.astype(jnp.float32)
    grad_down_raw, gain_three = norm_back(down_raw, inverse_down, norm_gains[3], cot_wide)
    grad_down_in = gather_rows(5, "grad_down_gather", grad_down_raw.astype(narrow))
    grad_gate_in, grad_up_in, grad_mlp_part = pl.pallas_call(
        mlp_backward_kernel,
        out_shape=[narrow_ff, narrow_ff, narrow_rows],
        name="mlp_backward",
    )(grad_down_in, gate_weight, up_weight, down_weight, gate_pre, up_pre)
    slots = (ctx_count, dp_count, ff_cols, model_width)
    ff_terms = jnp.concatenate(
        [
            rows_dot(grad_gate_in, mlp_in, 0, 0).astype(narrow).reshape(slots),
            rows_dot(grad_up_in, mlp_in, 0, 0).astype(narrow).reshape(slots),
            rows_dot(hidden, grad_down_in, 0, 0).astype(narrow).reshape(slots),
        ],
        axis=2,
    )
    half = dp_count // 2
    grad_mlp_blocks, ff_early = exchange(
        6,
        "grad_mlp_scatter",
        [
            (
                "scatter",
                ("head",),
                grad_mlp_part.reshape(head_count, tok_rows, model_width),
            ),
            ("relative", ("ctx",), ff_terms[:, :half]),
        ],
        (("head",), ("ctx",)),
    )
    grad_mlp_in = add_up(grad_mlp_blocks)
    grad_mid_part, gain_two = norm_back(middle, inverse_mid, norm_gains[2], grad_mlp_in)
    grad_middle = cot_wide + grad_mid_part
    grad_branch_raw, gain_one = norm_back(branch, inverse_branch, norm_gains[1], grad_middle)
    grad_branch_blocks, ff_late = exchange(
        7,
        "grad_branch_gather",
        [
            ("gather", ("head",), grad_branch_raw.astype(narrow)),
            ("relative", ("ctx",), ff_terms[:, half:]),
        ],
        (("head",), ("ctx",)),
    )
    grad_branch = grad_branch_blocks.reshape(query_rows, model_width)
    ff_sums = jnp.concatenate([add_up(ff_early), add_up(ff_late)], axis=0).astype(narrow)
    head_grad = rows_dot(grad_branch, out_weight, 1, 1).astype(narrow)
    row_delta = jnp.sum(head_grad.astype(jnp.float32) * attn_exact, axis=1, keepdims=True)
    grad_probs = rows_dot(head_grad, all_values, 1, 1)
    grad_scores = (probs_wide * (grad_probs - row_delta)).astype(narrow)
    value_sums = rows_dot(prob_rows, head_grad, 0, 0)
    key_sums = rows_dot(grad_scores, head_query, 0, 0)
    grad_rot_query = rows_dot(grad_scores, all_keys, 1, 0)
    query_back = rotate(grad_rot_query * score_scale, cosine_own, -sine_own)
    grad_query_raw, gain_query = norm_back(query_raw, inverse_query, qk_gains[0], query_back)
    key_back = rotate(key_sums, cosine, -sine_part)
    grad_key_raw, gain_key = norm_back(key_raw, inverse_key, qk_gains[1], key_back)
    grad_query_in = grad_query_raw.astype(narrow)
    grad_key_in = grad_key_raw.astype(narrow)
    grad_value_in = value_sums.astype(narrow)
    grad_attn_part = rows_dot(grad_key_in, key_weight, 1, 0) + rows_dot(
        grad_value_in, value_weight, 1, 0
    )
    own_part = lax.dynamic_slice_in_dim(grad_attn_part, first_query, query_rows) + rows_dot(
        grad_query_in, query_weight, 1, 0
    )
    grad_attn_part = lax.dynamic_update_slice_in_dim(grad_attn_part, own_part, first_query, 0)
    head_terms = jnp.concatenate(
        [
            rows_dot(grad_query_in, attn_in, 0, 0).reshape(group_count, query_cols, model_width),
            rows_dot(attn_out, grad_branch, 0, 0).reshape(group_count, query_cols, model_width),
        ],
        axis=1,
    ).astype(narrow)
    planes = (dp_count, every_count // dp_count, key_cols, model_width)
    key_value_terms = jnp.concatenate(
        [
            rows_dot(grad_key_in, attn_in_all, 0, 0).reshape(planes),
            rows_dot(grad_value_in, attn_in_all, 0, 0).reshape(planes),
        ],
        axis=2,
    ).astype(narrow).transpose(1, 0, 2, 3)
    head_terms = head_terms.reshape(dp_count, ctx_count, 2 * query_cols, model_width)
    grad_attn_blocks, head_blocks, key_value_blocks, ff_blocks = exchange(
        8,
        "last_scatter",
        [
            (
                "scatter",
                sequence_axes,
                grad_attn_part.astype(narrow).reshape(-1, tok_rows, model_width),
            ),
            ("scatter", ("ctx",), head_terms.transpose(1, 0, 2, 3)),
            ("scatter", sequence_axes, key_value_terms),
            ("relative", ("dp",), ff_sums),
        ],
        (sequence_axes, ("dp",)),
    )
    ff_own = add_up(ff_blocks)
    grad_attn_in = add_up(grad_attn_blocks)
    grad_in_part, gain_zero = norm_back(input_wide, inverse_in, norm_gains[0], grad_attn_in)
    d_block_in = (grad_middle + grad_in_part).astype(narrow)

    pad = ((0, 0), (0, model_width - head_width))
    gain_terms = jnp.concatenate(
        [
            jnp.sum(gain_zero, axis=0, keepdims=True),
            jnp.sum(gain_one, axis=0, keepdims=True),
            jnp.sum(gain_two, axis=0, keepdims=True),
            jnp.sum(gain_three, axis=0, keepdims=True),
            jnp.pad(jnp.sum(gain_query, axis=0, keepdims=True), pad),
            jnp.pad(jnp.sum(gain_key, axis=0, keepdims=True), pad),
            jnp.zeros((2, model_width), jnp.float32),
        ],
        axis=0,
    )
    gain_blocks, head_blocks, key_value_blocks = exchange(
        9,
        "depth_exchange",
        [
            ("gather", ("dp",), gain_terms),
            ("scatter", ("dp",), add_up(head_blocks).astype(narrow)),
            ("scatter", ("dp",), add_up(key_value_blocks).astype(narrow)),
        ],
    )
    head_own = lax.ppermute(add_up(head_blocks).astype(narrow), every_axis, to_owners).astype(
        jnp.float32
    )
    (gain_blocks,) = exchange(10, "gain_gather", [("gather", sequence_axes, add_up(gain_blocks))])
    gains = add_up(gain_blocks)
    key_value_own = add_up(key_value_blocks)
    return (
        block_out,
        d_block_in,
        gains[:4],
        gains[4:6, :head_width],
        head_own[:query_cols].T,
        key_value_own[:key_cols].T,
        key_value_own[key_cols:].T,
        head_own[query_cols:],
        ff_own[:ff_cols].T,
        ff_own[ff_cols : 2 * ff_cols].T,
        ff_own[2 * ff_cols :],
    )


bits = (0, 1)


class Mail:
    def __init__(self, send_sems, recv_sems):
        self.send_sems, self.recv_sems = send_sems, recv_sems
        self.started = []

    def push(self, source, target, to, when=None, arrives_as=None):
        number = len(self.started)
        copy = pltpu.make_async_remote_copy(
            src_ref=source,
            dst_ref=target,
            send_sem=self.send_sems.at[number],
            recv_sem=self.recv_sems.at[number if arrives_as is None else arrives_as],
            device_id=to,
            device_id_type=pl.DeviceIdType.MESH,
        )
        if when is None:
            copy.start()
        else:
            pl.when(when)(copy.start)
        self.started.append((copy, when))
        return copy

    def settle(self):
        for copy, when in self.started:
            if when is None:
                copy.wait_send()
            else:
                pl.when(when)(copy.wait_send)


copy_limit = 176


def fused_kernel(names, *refs):
    r = types.SimpleNamespace(**dict(zip(names, refs)))
    narrow, wide = jnp.bfloat16, jnp.float32
    d, x, h = lax.axis_index("dp"), lax.axis_index("ctx"), lax.axis_index("head")
    depth = lax.axis_size("dp")
    y, c = h // 2, lax.rem(h, 2)
    me = x * 4 + h
    mail = Mail(r.send_sems, r.recv_sems)
    rows, width = r.block_in.shape
    head_width = r.qk_gains.shape[1]
    half_width = head_width // 2
    heads, query_cols = r.q_raw.shape[1] // head_width, r.q_rows.shape[0]
    key_cols = r.key_rows.shape[0]
    ff_cols = r.gate_rows.shape[0]
    all_rows = 8 * rows
    full = heads * head_width

    def deep(offset):
        return lax.rem(d + offset, depth)

    def z_peer(offset):
        return {"dp": deep(offset)}

    x_peer = {"ctx": 1 - x}
    y_peer = {"head": (1 - y) * 2 + c}
    c_peer = {"head": y * 2 + 1 - c}

    def flip(place, bit):
        return 1 - place if bit else place

    def plane_peer(dx, dy, dc):
        return {"ctx": flip(x, dx), "head": flip(y, dy) * 2 + flip(c, dc)}

    plane_steps = [(dx, dy, dc) for dx in bits for dy in bits for dc in bits][1:]
    chip_steps = [(0, 1), (1, 0), (1, 1)]

    barrier = pltpu.get_barrier_semaphore()
    greeted = [z_peer(offset) for offset in range(1, depth)] + [plane_peer(*s) for s in plane_steps]
    for peer in greeted:
        pl.semaphore_signal(barrier, inc=1, device_id=peer, device_id_type=pl.DeviceIdType.MESH)
    r.block_all[x, y, c] = r.block_in[...]
    key_value = [r.key_rows[...].astype(wide), r.value_rows[...].astype(wide)]
    r.kv_all[d, x, y, c] = jnp.concatenate(key_value, axis=0).astype(narrow)
    r.q_all[d, x, y, c] = r.q_rows[...]
    r.o_all[d, x, y, c] = r.o_rows[...]
    for piece, own in enumerate((r.gate_rows, r.up_rows, r.down_rows)):
        r.ff_all[d, x, pl.ds(piece * ff_cols, ff_cols)] = own[...]
    r.pos_pair[x] = r.positions[...].astype(wide)
    pl.semaphore_wait(barrier, len(greeted))

    got_z, got_x, got_y, got_c = {}, {}, {}, {}

    def place(part):
        return (x, y, c) if part == "block" else (d, x, y, c)

    def source(part):
        return getattr(r, part + "_all").at[place(part)]

    def own_to_x(part):
        got_x[part, 0] = mail.push(source(part), getattr(r, part + "_all").at[place(part)], x_peer)

    def own_to_y(part):
        got_y[part, 0] = [
            mail.push(source(part), getattr(r, part + "_all").at[place(part)], y_peer)
        ]

    relayed = depth >= 4
    relays = ((depth - 1, 2, 0), (1, depth - 3, depth - 1)) if relayed else ()
    z_order = sorted(range(1, depth), key=lambda offset: offset != 2)

    def blocks_to_z(key, block_of):
        for offset in range(1, depth):
            when = None
            if relayed and offset == 1:
                when = d < depth - 1
            if relayed and offset == depth - 1:
                when = d > 0
            number = len(mail.started)
            copy = mail.push(block_of(d), block_of(d), z_peer(offset), when)
            got_z[key, offset] = copy, number

    def blocks_relay(key, block_of):
        if relayed:
            got_z[key, 2][0].wait_recv()
            block = block_of(deep(depth - 2))
            for other, relay, _ in relays:
                to = {"dp": lax.rem(d + depth - 2 + other, depth)}
                mail.push(block, block, to, d == relay, got_z[key, other][1])

    def blocks_to_x(key, block_of):
        for offset in z_order:
            if not relayed or offset != 2:
                got_z[key, offset][0].wait_recv()
            block = block_of(deep(depth - offset))
            got_x[key, offset] = mail.push(block, block, x_peer)

    def relay(part):
        blocks_relay(part, block_of(part))

    def block_of(part):
        return lambda slot: getattr(r, part + "_all").at[(slot,) + place(part)[1:]]

    def own_to_z(part):
        blocks_to_z(part, block_of(part))

    def to_x(part):
        blocks_to_x(part, block_of(part))

    def near_to_y(part):
        got_x[part, 0].wait_recv()
        at = (1 - x, y, c) if part == "block" else (d, 1 - x, y, c)
        block = getattr(r, part + "_all").at[at]
        got_y[part, 0].append(mail.push(block, block, y_peer))

    def to_y(part):
        for offset in range(1, depth):
            got_x[part, offset].wait_recv()
            block = getattr(r, part + "_all").at[deep(depth - offset), :, y, c]
            got_y[part, offset] = [mail.push(block, block, y_peer)]

    def to_c(part):
        for offset in range(1 if part == "block" else depth):
            for copy in got_y[part, offset]:
                copy.wait_recv()
            block = getattr(r, part + "_all")
            block = block if part == "block" else block.at[deep(depth - offset)]
            block = block.at[:, :, c]
            got_c[part, offset] = mail.push(block, block, c_peer)

    def arrived(part):
        for offset in range(1 if part == "block" else depth):
            got_c[part, offset].wait_recv()

    def ff_piece(slot, piece):
        return r.ff_all.at[slot, x, pl.ds(piece * ff_cols, ff_cols)]

    def ff_to_z(piece):
        blocks_to_z(("ff", piece), lambda slot: ff_piece(slot, piece))

    def ff_relay(piece):
        blocks_relay(("ff", piece), lambda slot: ff_piece(slot, piece))

    def ff_own_to_x():
        block = r.ff_all.at[d, x]
        got_x["ff", 0] = mail.push(block, block, x_peer)

    def ff_to_x(piece):
        blocks_to_x(("ff", piece), lambda slot: ff_piece(slot, piece))

    position_copy = mail.push(r.pos_pair.at[x], r.pos_pair.at[x], x_peer)
    for part in ("kv", "block", "q", "o"):
        own_to_x(part)
        own_to_y(part)
        if part != "block":
            own_to_z(part)

    def rope_tables():
        position_copy.wait_recv()
        for half in bits:
            r.pos_all[half * 4 : half * 4 + 4] = r.pos_pair[half]
        turned = r.pos_all[...].T
        ladder = lax.broadcasted_iota(jnp.int32, (1, half_width), 1).astype(wide)
        frequency = jnp.exp(ladder * (-2.0 / head_width) * math.log(rope_base))
        column = lax.broadcasted_iota(jnp.int32, turned.shape, 1)
        r.pos_own[...] = jnp.sum(jnp.where(column == me, turned, 0.0), axis=1, keepdims=True)
        for block in range(8):
            angle = turned[:, block : block + 1] * frequency
            r.cosine[block] = jnp.cos(angle)
            r.sine[block] = jnp.sin(angle)

    def shuffle():
        size = 2 * head_width
        there = lax.broadcasted_iota(jnp.int32, (size, size), 1).astype(wide)
        here = lax.broadcasted_iota(jnp.int32, (size, size), 0).astype(wide)

        def sorted_place(place):
            block = jnp.floor((place + 0.5) / (2 * key_cols))
            inside = place - block * (2 * key_cols)
            value = inside >= key_cols
            return block * key_cols + jnp.where(value, inside - key_cols + head_width, inside)

        r.unsort[...] = jnp.where(sorted_place(here) == there, 1.0, 0.0).astype(narrow)
        r.sort[...] = jnp.where(sorted_place(there) == here, 1.0, 0.0).astype(narrow)

    def attention_inputs():
        arrived("block")
        gain = r.norm_gains[0:1]
        for px in bits:
            for py in bits:
                for pc in bits:
                    values = r.block_all[px, py, pc].astype(wide)
                    r.attn_in[px * 4 + py * 2 + pc] = norm_rows(values, gain)[0].astype(narrow)

    def keys_and_values():
        arrived("kv")
        blocks = r.kv_all[...].reshape(2 * head_width, width)
        r.kv_sorted[...] = rows_dot(r.sort[...], blocks, 1, 0).astype(narrow)
        gain = r.qk_gains[1:2]
        for pair in range(4):
            two = pl.ds(2 * pair, 2)
            inputs = r.attn_in[two].reshape(2 * rows, width)
            raw = rows_dot(inputs, r.kv_sorted[...], 1, 1)
            key_raw = raw[:, :head_width]
            r.key_raw[two] = key_raw.reshape(2, rows, head_width)
            cosine = r.cosine[two].reshape(2 * rows, half_width)
            sine_part = r.sine[two].reshape(2 * rows, half_width)
            turned = rotate(norm_rows(key_raw, gain)[0], cosine, sine_part)
            r.keys[pl.ds(2 * pair * rows, 2 * rows)] = turned.astype(narrow)
            r.values[pl.ds(2 * pair * rows, 2 * rows)] = raw[:, head_width:].astype(narrow)

    shuffle()
    relay("kv")
    rope_tables()
    relay("q")
    to_x("kv")
    relay("o")
    near_to_y("kv")
    near_to_y("block")
    ff_to_z(0)
    to_x("q")
    near_to_y("q")
    to_y("kv")
    ff_to_z(1)
    ff_own_to_x()
    to_x("o")
    near_to_y("o")
    ff_relay(0)
    to_y("q")
    ff_to_z(2)
    to_c("block")
    attention_inputs()
    ff_relay(1)
    ff_to_x(0)
    to_c("kv")
    to_y("o")
    keys_and_values()
    ff_relay(2)
    ff_to_x(1)
    to_c("q")

    query_gain = r.qk_gains[0:1]
    arrived("q")
    weight = r.q_all[...].reshape(full, width)
    r.q_raw[...] = rows_dot(r.attn_in[me], weight, 1, 1)
    for head in range(heads):
        turned = rotate(
            norm_rows(r.q_raw[:, head * head_width : (head + 1) * head_width], query_gain)[0],
            r.cosine[me],
            r.sine[me],
        )
        r.q_rot[head] = (turned * score_scale).astype(narrow)
    ff_to_x(2)
    to_c("o")

    query_index = lax.broadcasted_iota(jnp.int32, (rows, all_rows), 0) + me * rows
    key_index = lax.broadcasted_iota(jnp.int32, (rows, all_rows), 1)
    lowest_key = query_index - r.pos_own[...].astype(jnp.int32)
    visible = (key_index <= query_index) & (key_index >= lowest_key)
    r.bias[...] = jnp.where(visible, 0.0, negative_fill)
    for head in range(heads):
        scores = rows_dot(r.q_rot[head], r.keys[...], 1, 1)
        scores = jnp.where(r.bias[...] < 0.0, negative_fill, scores)
        top = jnp.max(scores, axis=1, keepdims=True)
        raised = jnp.exp(scores - top)
        prob_rows = raised * (1.0 / jnp.sum(raised, axis=1, keepdims=True))
        r.probs[head] = prob_rows
        r.probs_narrow[head] = prob_rows.astype(narrow)
        exact = rows_dot(prob_rows.astype(narrow), r.values[...], 1, 0)
        r.exact[head] = exact
        r.attn_out[:, head * head_width : (head + 1) * head_width] = exact.astype(narrow)
    arrived("o")
    out_weight = r.o_all[...].reshape(full, width)
    r.branch[...] = rows_dot(r.attn_out[...], out_weight, 1, 0)
    def send_factor(name):
        copies = []
        for step in plane_steps:
            px, py, pc = (flip(here, bit) for here, bit in zip((x, y, c), step))
            copies.append(
                mail.push(getattr(r, name).at[:, px, py, pc], getattr(r, name + "_got").at[me], plane_peer(*step))
            )
        getattr(r, name + "_got")[me] = getattr(r, name)[:, x, y, c]
        return copies

    def send_group_factor():
        copies = []
        for dy, dc in chip_steps:
            source = r.out_turned.at[:, :, flip(y, dy), flip(c, dc)]
            copies.append(mail.push(source, r.out_turned_got.at[y, c], plane_peer(0, dy, dc)))
        r.out_turned_got[y, c] = r.out_turned[:, :, y, c]
        return copies

    def turned_blocks(name, values, columns):
        getattr(r, name)[...] = values.astype(wide).T.astype(narrow).reshape(depth, 2, 2, 2, columns, rows)

    input_wide = r.block_in[...].astype(wide)
    branch_normed = norm_rows(r.branch[...], r.norm_gains[1:2])[0]
    r.middle[...] = input_wide + branch_normed
    mlp_rows = norm_rows(r.middle[...], r.norm_gains[2:3])[0].astype(narrow)

    def share_rows(name, values):
        getattr(r, name)[y, c] = values
        block = getattr(r, name).at[y, c]
        return mail.push(block, block, c_peer), mail.push(block, block, y_peer)

    def far_rows(name, from_y):
        from_y.wait_recv()
        block = getattr(r, name).at[1 - y, c]
        return mail.push(block, block, c_peer)

    def fetch_ff():
        got_x["ff", 0].wait_recv()
        for piece in range(3):
            for offset in range(1, depth):
                got_x[("ff", piece), offset].wait_recv()

    def ff_part(index):
        piece = r.ff_all[:, :, pl.ds(index * ff_cols, ff_cols)]
        return piece.reshape(2 * depth * ff_cols, width)

    def group_sum(name, half, own_rows, waiting, early, between):
        part, near, far = getattr(r, name), getattr(r, name + "_near"), getattr(r, name + "_far")
        from_c, from_y = own_rows
        from_c.wait_recv()
        half(y)
        near_own = mail.push(part.at[y, 1 - c], near.at[0], c_peer)
        forwarded = from_y()
        waiting()
        forwarded.wait_recv()
        early()
        half(1 - y)
        near_far = mail.push(part.at[1 - y, 1 - c], near.at[1], c_peer)
        near_far.wait_recv()
        summed = part[1 - y, c].astype(wide) + near[1].astype(wide)
        getattr(r, name + "_sum")[...] = summed.astype(narrow)
        far_copy = mail.push(getattr(r, name + "_sum"), far, y_peer)
        between()
        near_own.wait_recv()
        own = part[y, c].astype(wide) + near[0].astype(wide)
        far_copy.wait_recv()
        return own + far[...].astype(wide)

    def forward_half(side):
        inputs = r.mlp_in[side].reshape(2 * rows, width)
        gate_pre = rows_dot(inputs, ff_part(0), 1, 1)
        up_pre = rows_dot(inputs, ff_part(1), 1, 1)
        r.gate_pre[side] = gate_pre
        r.up_pre[side] = up_pre
        hidden = (gelu_parts(gate_pre)[0] * up_pre).astype(narrow)
        r.hidden[side] = hidden
        part = rows_dot(hidden, ff_part(2), 1, 0).astype(narrow)
        r.down[side] = part.reshape(2, rows, width)

    def nothing():
        pass

    near_copy, y_copy = share_rows("mlp_in", mlp_rows)
    turned_blocks("out_turned", r.attn_out[...], query_cols)
    out_copies = send_group_factor()
    fetch_ff()
    r.down_raw[...] = group_sum(
        "down", forward_half, (near_copy, lambda: far_rows("mlp_in", y_copy)), nothing, nothing, nothing
    )
    down_raw = r.down_raw[...]
    down_normed, inverse_down = norm_rows(down_raw, r.norm_gains[3:4])
    r.block_out[...] = (r.middle[...] + down_normed).astype(narrow)
    cot_wide = r.cotangent[...].astype(wide)
    grad_down_raw, gain_three = norm_back(down_raw, inverse_down, r.norm_gains[3:4], cot_wide)
    r.gains[...] = jnp.zeros_like(r.gains)
    r.gains[3:4] = jnp.sum(gain_three, axis=0, keepdims=True)

    def backward_half(side):
        grad_hidden = rows_dot(r.grad_down[side].reshape(2 * rows, width), ff_part(2), 1, 1)
        gelu, slope = gelu_parts(r.gate_pre[side])
        grad_gate = (grad_hidden * r.up_pre[side] * slope).astype(narrow)
        grad_up = (grad_hidden * gelu).astype(narrow)
        r.grad_gate[side] = grad_gate
        r.grad_up[side] = grad_up
        part = rows_dot(grad_gate, ff_part(0), 1, 0) + rows_dot(grad_up, ff_part(1), 1, 0)
        r.mlp_back[side] = part.astype(narrow).reshape(2, rows, width)

    ff_width = 2 * depth * ff_cols

    factors = ((r.grad_gate, r.mlp_in), (r.grad_up, r.mlp_in), (r.hidden, r.grad_down))

    def side_terms(index, side):
        left, right = factors[index]
        return rows_dot(left[side], right[side].reshape(2 * rows, width), 0, 0)

    def near_terms():
        for index in range(3):
            r.ff_wide[index] = side_terms(index, y)

    def far_terms(index):
        terms = (r.ff_wide[index] + side_terms(index, 1 - y)).astype(narrow)
        r.ff_terms[:, :, pl.ds(index * ff_cols, ff_cols)] = terms.reshape(depth, 2, ff_cols, width)

    ff_across = {}

    both = 2 * ff_cols

    def ff_terms_to_x(offset):
        source = r.ff_terms.at[deep(offset), 1 - x, pl.ds(0, both)]
        ff_across[offset] = mail.push(source, r.ff_near.at[offset], x_peer)

    down_copies = []

    def down_terms():
        far_terms(2)
        for offset in range(1, depth):
            source = r.ff_terms.at[deep(offset), :, pl.ds(both, ff_cols)]
            down_copies.append(mail.push(source, r.down_got.at[offset], z_peer(offset)))

    def down_step():
        summed = r.ff_terms[d, :, pl.ds(both, ff_cols)].astype(wide)
        for copy in down_copies:
            copy.wait_recv()
        for offset in range(1, depth):
            summed += r.down_got[offset].astype(wide)
        r.down_wide[...] = summed
        r.down_sums[...] = summed.astype(narrow)
        return mail.push(r.down_sums.at[1 - x], r.down_near_sum, x_peer)

    def gate_terms():
        far_terms(0)
        far_terms(1)
        for offset in range(1, depth):
            ff_terms_to_x(offset)

    near_copy, y_copy = share_rows("grad_down", grad_down_raw.astype(narrow))
    grad_mlp_in = group_sum(
        "mlp_back",
        backward_half,
        (near_copy, lambda: far_rows("grad_down", y_copy)),
        near_terms,
        down_terms,
        gate_terms,
    )
    middle = r.middle[...]
    inverse_mid = norm_rows(middle, r.norm_gains[2:3])[1]
    grad_mid_part, gain_two = norm_back(middle, inverse_mid, r.norm_gains[2:3], grad_mlp_in)
    r.gains[2:3] = jnp.sum(gain_two, axis=0, keepdims=True)
    grad_middle = r.cotangent[...].astype(wide) + grad_mid_part
    r.grad_middle[...] = grad_middle
    branch = r.branch[...]
    inverse_branch = norm_rows(branch, r.norm_gains[1:2])[1]
    grad_branch_raw, gain_one = norm_back(branch, inverse_branch, r.norm_gains[1:2], grad_middle)
    r.gains[1:2] = jnp.sum(gain_one, axis=0, keepdims=True)
    grad_branch = grad_branch_raw.astype(narrow)
    branch_c, branch_y = share_rows("branch_all", grad_branch)

    head_grad = rows_dot(grad_branch, out_weight, 1, 1).astype(narrow)
    for head in range(heads):
        r.head_grad[head] = head_grad[:, head * head_width : (head + 1) * head_width]

    ff_deep = []

    def ff_step(offset):
        ff_across[offset].wait_recv()
        summed = r.ff_terms[deep(offset), x, pl.ds(0, both)].astype(wide) + r.ff_near[offset].astype(wide)
        if offset:
            r.ff_sum[offset] = summed.astype(narrow)
            ff_deep.append(mail.push(r.ff_sum.at[offset], r.ff_got.at[offset], z_peer(offset)))
        else:
            r.ff_own[...] = summed

    for head in range(heads):
        grad_rows = r.head_grad[head]
        delta = jnp.sum(grad_rows.astype(wide) * r.exact[head], axis=1, keepdims=True)
        grad_probs = rows_dot(grad_rows, r.values[...], 1, 1)
        r.grad_scores[head] = (r.probs[head] * (grad_probs - delta)).astype(narrow)
    ff_step(1)
    all_grads = r.head_grad[...].reshape(heads * rows, head_width)
    all_queries = r.q_rot[...].reshape(heads * rows, head_width)
    kv_near = []
    for pair in range(4):
        here = slice(2 * pair * rows, 2 * (pair + 1) * rows)
        px, py = pair // 2, pair % 2
        key_part = rows_dot(
            r.grad_scores[:, :, here].reshape(heads * rows, 2 * rows), all_queries, 0, 0
        )
        value_part = rows_dot(
            r.probs_narrow[:, :, here].reshape(heads * rows, 2 * rows), all_grads, 0, 0
        )
        r.kv_terms[px, py, :, :, :head_width] = key_part.astype(narrow).reshape(2, rows, head_width)
        r.kv_terms[px, py, :, :, head_width:] = value_part.astype(narrow).reshape(2, rows, head_width)
        kv_near.append(mail.push(r.kv_terms.at[px, py, 1 - c], r.kv_near.at[px, py], c_peer))
    ff_step(2)
    branch_far = far_rows("branch_all", branch_y)

    cosine, sine_part = r.cosine[me], r.sine[me]
    gain_query = jnp.zeros((1, head_width), wide)
    for head in range(heads):
        here = slice(head * head_width, (head + 1) * head_width)
        turned = rows_dot(r.grad_scores[head], r.keys[...], 1, 0) * score_scale
        upstream = rotate(turned, cosine, -sine_part)
        query_raw = r.q_raw[:, here]
        inverse = norm_rows(query_raw, query_gain)[1]
        grad_raw, gain_rows = norm_back(query_raw, inverse, query_gain, upstream)
        gain_query += jnp.sum(gain_rows, axis=0, keepdims=True)
        r.grad_query[:, here] = grad_raw.astype(narrow)
    r.gains[4:5, :head_width] = gain_query

    for px in bits:
        for py in bits:
            kv_near[2 * px + py].wait_recv()
            summed = r.kv_terms[px, py, c].astype(wide) + r.kv_near[px, py].astype(wide)
            r.kv_sums[px, py] = summed.astype(narrow)
    kv_copies = []
    for number, (dx, dy) in enumerate(chip_steps):
        kv_copies.append(
            mail.push(
                r.kv_sums.at[flip(x, dx), flip(y, dy)], r.kv_far.at[number], plane_peer(dx, dy, 0)
            )
        )
    turned_blocks("query_turned", r.grad_query[...], query_cols)
    query_copies = send_factor("query_turned")
    ff_step(3)

    def deep_copies(name):
        return [
            mail.push(getattr(r, name + "_terms").at[deep(offset)], getattr(r, name + "_far").at[offset], z_peer(offset))
            for offset in range(1, depth)
        ]

    for copy in out_copies + [branch_c, branch_far]:
        copy.wait_recv()
    terms = jnp.zeros((2 * depth * query_cols, width), wide)
    for py in bits:
        for pc in bits:
            left = r.out_turned_got[py, pc].reshape(2 * depth * query_cols, rows)
            terms += rows_dot(left, r.branch_all[py, pc], 1, 0)
    r.out_both[...] = terms.astype(narrow).reshape(depth, 2, query_cols, width)
    out_near = mail.push(r.out_both.at[:, 1 - x], r.out_near, x_peer)
    query_part = rows_dot(r.grad_query[...], r.q_all[...].reshape(full, width), 1, 0)
    r.query_part[...] = query_part

    def weight_terms(name, copies, columns):
        for copy in copies:
            copy.wait_recv()
        terms = jnp.zeros((depth * columns, width), wide)
        for block in range(8):
            left = getattr(r, name + "_got")[block].reshape(depth * columns, rows)
            terms += rows_dot(left, r.attn_in[block], 1, 0)
        getattr(r, name + "_wide")[...] = terms.reshape(depth, columns, width)
        getattr(r, name + "_terms")[...] = terms.astype(narrow).reshape(depth, columns, width)
        return deep_copies(name)

    for offset in range(4, depth):
        ff_step(offset)
    for copy in kv_copies:
        copy.wait_recv()
    kv_sum = r.kv_sums[x, y].astype(wide)
    for number in range(len(chip_steps)):
        kv_sum += r.kv_far[number].astype(wide)
    key_gain = r.qk_gains[1:2]
    key_raw = r.key_raw[me]
    key_back = rotate(kv_sum[:, :head_width], cosine, -sine_part)
    inverse_key = norm_rows(key_raw, key_gain)[1]
    grad_key_raw, gain_key = norm_back(key_raw, inverse_key, key_gain, key_back)
    r.gains[5:6, :head_width] = jnp.sum(gain_key, axis=0, keepdims=True)
    r.grad_kv[:, :head_width] = grad_key_raw.astype(narrow)
    r.grad_kv[:, head_width:] = kv_sum[:, head_width:].astype(narrow)
    kv_turned = rows_dot(r.unsort[...], r.grad_kv[...], 1, 1).astype(narrow)
    r.kv_turned[...] = kv_turned.reshape(depth, 2, 2, 2, 2 * key_cols, rows)
    kv_factor_copies = send_factor("kv_turned")

    grad_attn_in = r.query_part[...] + rows_dot(r.grad_kv[...], r.kv_sorted[...], 1, 0)
    input_wide = r.block_in[...].astype(wide)
    inverse_in = norm_rows(input_wide, r.norm_gains[0:1])[1]
    grad_in_part, gain_zero = norm_back(input_wide, inverse_in, r.norm_gains[0:1], grad_attn_in)
    r.d_block_in[...] = (r.grad_middle[...] + grad_in_part).astype(narrow)
    r.gains[0:1] = jnp.sum(gain_zero, axis=0, keepdims=True)
    gain_copies = [
        mail.push(r.gains, r.gains_got.at[number], plane_peer(*step))
        for number, step in enumerate(plane_steps)
    ]

    query_deep = weight_terms("query_turned", query_copies, query_cols)
    down_copy = down_step()
    ff_terms_to_x(0)
    out_near.wait_recv()
    summed = r.out_both[:, x].astype(wide) + r.out_near[...].astype(wide)
    r.out_turned_wide[...] = summed
    r.out_turned_terms[...] = summed.astype(narrow)
    out_deep = deep_copies("out_turned")
    kv_deep = weight_terms("kv_turned", kv_factor_copies, 2 * key_cols)
    gain_sum = r.gains[...]
    for number, copy in enumerate(gain_copies):
        copy.wait_recv()
        gain_sum += r.gains_got[number]
    r.gains_sum[...] = gain_sum
    gain_deep = [
        mail.push(r.gains_sum, r.gains_deep.at[offset], z_peer(offset)) for offset in range(1, depth)
    ]
    ff_step(0)

    def deep_sum(own, far, copies):
        for number, copy in enumerate(copies):
            copy.wait_recv()
            own += far[number + 1].astype(wide)
        return own

    r.grad_q_rows[...] = deep_sum(r.query_turned_wide[d], r.query_turned_far, query_deep)
    r.grad_o_rows[...] = deep_sum(r.out_turned_wide[d], r.out_turned_far, out_deep)
    r.grad_ff_rows[:both] = deep_sum(r.ff_own[...], r.ff_got, ff_deep)
    down_copy.wait_recv()
    r.grad_ff_rows[both:] = r.down_wide[x] + r.down_near_sum[...].astype(wide)
    r.grad_kv_rows[...] = deep_sum(r.kv_turned_wide[d], r.kv_turned_far, kv_deep)
    r.gains_out[...] = deep_sum(r.gains_sum[...], r.gains_deep, gain_deep)
    mail.settle()


def split_kernel(block_ref, back_ref, gains_ref, q_ref, o_ref, kv_ref, ff_ref, *outs):
    key_cols, ff_cols = outs[5].shape[0], outs[8].shape[0]
    outs[0][...] = block_ref[...]
    outs[1][...] = back_ref[...]
    norm_count = outs[2].shape[0]
    outs[2][...] = gains_ref[:norm_count]
    outs[3][...] = gains_ref[norm_count : norm_count + outs[3].shape[0], : outs[3].shape[1]]
    outs[4][...] = q_ref[...]
    outs[5][...] = kv_ref[:key_cols]
    outs[6][...] = kv_ref[key_cols:]
    outs[7][...] = o_ref[...]
    for piece in range(3):
        outs[8 + piece][...] = ff_ref[piece * ff_cols : (piece + 1) * ff_cols]


def fused_local(
    block_in,
    cotangent,
    positions,
    norm_gains,
    qk_gains,
    w_query,
    w_key,
    w_value,
    w_out,
    w_gate,
    w_up,
    w_down,
):
    narrow, wide = jnp.bfloat16, jnp.float32
    rows, width = block_in.shape
    head_width = qk_gains.shape[1]
    depth = lax.axis_size("dp")
    query_cols, key_cols, ff_cols = w_query.shape[1], w_key.shape[1], w_gate.shape[1]
    full = query_cols * lax.axis_size(every_axis)
    heads = full // head_width
    plane = lax.axis_size(sequence_axes)
    length = plane * rows
    ff_width = 2 * depth * ff_cols
    operands = dict(
        block_in=block_in,
        cotangent=cotangent,
        positions=positions.reshape(-1, rows),
        norm_gains=norm_gains,
        qk_gains=qk_gains,
        q_rows=w_query.T,
        o_rows=w_out,
        key_rows=w_key.T,
        value_rows=w_value.T,
        gate_rows=w_gate.T,
        up_rows=w_up.T,
        down_rows=w_down,
    )
    results = dict(
        block_out=((rows, width), narrow),
        d_block_in=((rows, width), narrow),
        gains_out=((8, width), wide),
        grad_q_rows=((query_cols, width), wide),
        grad_o_rows=((query_cols, width), wide),
        grad_kv_rows=((2 * key_cols, width), wide),
        grad_ff_rows=((3 * ff_cols, width), wide),
    )
    cube = (depth, 2, 2, 2)
    scratch = dict(
        block_all=((2, 2, 2, rows, width), narrow),
        kv_all=(cube + (2 * key_cols, width), narrow),
        q_all=(cube + (query_cols, width), narrow),
        o_all=(cube + (query_cols, width), narrow),
        ff_all=((depth, 2, 3 * ff_cols, width), narrow),
        pos_pair=((2, plane // 2, rows), wide),
        pos_all=((plane, rows), wide),
        pos_own=((rows, 1), wide),
        cosine=((plane, rows, head_width // 2), wide),
        sine=((plane, rows, head_width // 2), wide),
        sort=((2 * head_width, 2 * head_width), narrow),
        unsort=((2 * head_width, 2 * head_width), narrow),
        attn_in=((plane, rows, width), narrow),
        kv_sorted=((2 * head_width, width), narrow),
        key_raw=((plane, rows, head_width), wide),
        keys=((length, head_width), narrow),
        values=((length, head_width), narrow),
        q_raw=((rows, full), wide),
        q_rot=((heads, rows, head_width), narrow),
        bias=((rows, length), wide),
        probs=((heads, rows, length), wide),
        probs_narrow=((heads, rows, length), narrow),
        exact=((heads, rows, head_width), wide),
        attn_out=((rows, full), narrow),
        branch=((rows, width), wide),
        middle=((rows, width), wide),
        mlp_in=((2, 2, rows, width), narrow),
        gate_pre=((2, 2 * rows, ff_width), wide),
        up_pre=((2, 2 * rows, ff_width), wide),
        hidden=((2, 2 * rows, ff_width), narrow),
        down_raw=((rows, width), wide),
        grad_down=((2, 2, rows, width), narrow),
        grad_gate=((2, 2 * rows, ff_width), narrow),
        grad_up=((2, 2 * rows, ff_width), narrow),
        grad_middle=((rows, width), wide),
        branch_all=((2, 2, rows, width), narrow),
        out_both=((depth, 2, query_cols, width), narrow),
        out_near=((depth, query_cols, width), narrow),
        ff_wide=((3, ff_width, width), wide),
        head_grad=((heads, rows, head_width), narrow),
        grad_scores=((heads, rows, length), narrow),
        grad_query=((rows, full), narrow),
        query_part=((rows, width), wide),
        grad_kv=((rows, 2 * head_width), narrow),
        kv_terms=((2, 2, 2, rows, 2 * head_width), narrow),
        kv_near=((2, 2, rows, 2 * head_width), narrow),
        kv_sums=((2, 2, rows, 2 * head_width), narrow),
        kv_far=((3, rows, 2 * head_width), narrow),
        ff_terms=((depth, 2, 3 * ff_cols, width), narrow),
        ff_near=((depth, 2 * ff_cols, width), narrow),
        ff_sum=((depth, 2 * ff_cols, width), narrow),
        ff_got=((depth, 2 * ff_cols, width), narrow),
        ff_own=((2 * ff_cols, width), wide),
        down_got=((depth, 2, ff_cols, width), narrow),
        down_wide=((2, ff_cols, width), wide),
        down_sums=((2, ff_cols, width), narrow),
        down_near_sum=((ff_cols, width), narrow),
        gains=((8, width), wide),
        gains_got=((plane - 1, 8, width), wide),
        gains_sum=((8, width), wide),
        gains_deep=((depth, 8, width), wide),
    )
    for name in ("down", "mlp_back"):
        scratch[name] = ((2, 2, rows, width), narrow)
        scratch[name + "_near"] = ((2, rows, width), narrow)
        scratch[name + "_sum"] = ((rows, width), narrow)
        scratch[name + "_far"] = ((rows, width), narrow)
    for name, columns in (("out_turned", query_cols), ("query_turned", query_cols), ("kv_turned", 2 * key_cols)):
        scratch[name] = (cube + (columns, rows), narrow)
        scratch[name + "_got"] = ((plane, depth, columns, rows), narrow)
        scratch[name + "_wide"] = ((depth, columns, width), wide)
        scratch[name + "_terms"] = ((depth, columns, width), narrow)
        scratch[name + "_far"] = ((depth, columns, width), narrow)
    scratch["out_turned_got"] = ((2, 2, depth, 2, query_cols, rows), narrow)
    names = list(operands) + list(results) + list(scratch) + ["send_sems", "recv_sems"]
    in_vmem = pl.BlockSpec(memory_space=pltpu.VMEM)
    outs = pl.pallas_call(
        lambda *refs: fused_kernel(names, *refs),
        out_shape=[jax.ShapeDtypeStruct(*result) for result in results.values()],
        in_specs=[in_vmem] * len(operands),
        out_specs=[in_vmem] * len(results),
        scratch_shapes=[pltpu.VMEM(*one) for one in scratch.values()]
        + [pltpu.SemaphoreType.DMA((copy_limit,))] * 2,
        compiler_params=pltpu.CompilerParams(
            collective_id=11, has_side_effects=True, vmem_limit_bytes=56 * 1024 * 1024
        ),
        name="layer",
    )(*operands.values())
    parts = [
        ((rows, width), narrow),
        ((rows, width), narrow),
        (norm_gains.shape, wide),
        (qk_gains.shape, wide),
        ((query_cols, width), wide),
        ((key_cols, width), wide),
        ((key_cols, width), wide),
        ((query_cols, width), wide),
        ((ff_cols, width), wide),
        ((ff_cols, width), wide),
        ((ff_cols, width), wide),
    ]
    parts = pl.pallas_call(
        split_kernel,
        out_shape=[jax.ShapeDtypeStruct(*part) for part in parts],
        in_specs=[in_vmem] * len(results),
        out_specs=[in_vmem] * len(parts),
        name="split",
    )(*outs)
    turned = (4, 5, 6, 8, 9)
    return tuple(part.T if index in turned else part for index, part in enumerate(parts))


def fits_fused(block_in, w_query, w_key, w_gate):
    tiles = (w_query.shape[1], 2 * w_key.shape[1], w_gate.shape[1])
    return (
        lax.axis_size("ctx") == 2
        and lax.axis_size("head") == 4
        and block_in.shape[0] % 128 == 0
        and all(columns % 16 == 0 for columns in tiles)
    )


def either_local(*args):
    if fits_fused(args[0], args[5], args[6], args[9]):
        return fused_local(*args)
    return local(*args)


def solution(mesh):
    in_specs = (
        P(every_axis, None),
        P(every_axis, None),
        P(weight_axes),
        P(),
        P(),
        P(None, every_axis),
        P(None, every_axis),
        P(None, every_axis),
        P(every_axis, None),
        P(None, every_axis),
        P(None, every_axis),
        P(every_axis, None),
    )
    out_specs = (
        P(every_axis, None),
        P(every_axis, None),
        P(),
        P(),
        P(None, every_axis),
        P(None, every_axis),
        P(None, every_axis),
        P(every_axis, None),
        P(None, every_axis),
        P(None, every_axis),
        P(every_axis, None),
    )
    return jax.shard_map(either_local, mesh=mesh, in_specs=in_specs, out_specs=out_specs, check_vma=False)
```

```python
import math
import types

import jax
import jax.numpy as jnp
from jax import lax
from jax.experimental import pallas as pl
from jax.experimental.pallas import tpu as pltpu
from jax.sharding import PartitionSpec as P

epsilon = 1e-06
rope_base = 1000000.0
score_scale = 0.0625
negative_fill = -1e30


def norm_rows(values, gain_vec):
    inverse = lax.rsqrt(jnp.mean(values * values, axis=-1, keepdims=True) + epsilon)
    return (values * inverse * gain_vec, inverse)


def norm_back(values, inverse, gain_vec, upstream):
    scaled = upstream * gain_vec
    inner_mean = jnp.mean(scaled * values, axis=-1, keepdims=True)
    return (
        inverse * scaled - values * (inverse * inverse * inverse) * inner_mean,
        upstream * values * inverse,
    )


def rope_angles(positions, full_width):
    ladder = jnp.arange(full_width // 2, dtype=jnp.float32)
    frequency = jnp.exp(ladder * (-2.0 / full_width) * math.log(rope_base))
    angles = positions.astype(jnp.float32)[:, None] * frequency[None, :]
    return (jnp.cos(angles), jnp.sin(angles))


def rotate(values, cosine, sine_part):
    middle = values.shape[-1] // 2
    first_half = values[..., :middle]
    second = values[..., middle:]
    return jnp.concatenate(
        [first_half * cosine - second * sine_part, second * cosine + first_half * sine_part],
        axis=-1,
    )


def gelu_product(gate_pre, up_pre):
    return jax.nn.gelu(gate_pre, approximate=True) * up_pre


every_axis = ("dp", "ctx", "head")
sequence_axes = ("ctx", "head")
weight_axes = ("dp", "ctx")


def place_in(axes):
    place = 0
    for name in axes:
        place = place * lax.axis_size(name) + lax.axis_index(name)
    return place


def coordinates(axes, place):
    found = {}
    for name in reversed(axes):
        size = lax.axis_size(name)
        found[name] = lax.rem(place, size)
        place = place // size
    return found


def each_peer(count, step):
    if count <= 8:
        for offset in range(1, count):
            step(offset)
    else:

        def looped(offset, carry):
            step(offset)
            return carry

        lax.fori_loop(1, count, looped, 0)


def exchange_kernel(kinds, greet, counts, *refs):
    total = len(kinds)
    sources, targets, sems = refs[:total], refs[total : 2 * total], refs[2 * total :]
    barrier = pltpu.get_barrier_semaphore()
    waits = 0
    for axes, count in greet:
        me = place_in(axes)

        def greet_peer(offset, axes=axes, count=count, me=me):
            pl.semaphore_signal(
                barrier,
                inc=1,
                device_id=coordinates(axes, lax.rem(me + offset, count)),
                device_id_type=pl.DeviceIdType.MESH,
            )

        each_peer(count, greet_peer)
        waits += count - 1
    locals_started = []
    for part, (kind, axes) in enumerate(kinds):
        me = place_in(axes)
        source = {"scatter": me, "relative": 0}.get(kind)
        source = sources[part] if source is None else sources[part].at[source]
        copy = pltpu.make_async_copy(source, targets[part].at[me], sems[3 * part + 2].at[0])
        copy.start()
        locals_started.append(copy)
    pl.semaphore_wait(barrier, waits)

    def descriptor(part, offset, backward):
        kind, axes = kinds[part]
        count = counts[part]
        me = place_in(axes)
        to = lax.rem(me + offset, count)
        origin = lax.rem(me + count - offset, count) if backward else me
        source = {"scatter": to, "relative": lax.rem(count - offset, count)}.get(kind)
        source = sources[part] if source is None else sources[part].at[source]
        return pltpu.make_async_remote_copy(
            src_ref=source,
            dst_ref=targets[part].at[origin],
            send_sem=sems[3 * part].at[offset],
            recv_sem=sems[3 * part + 1].at[origin],
            device_id=coordinates(axes, to),
            device_id_type=pl.DeviceIdType.MESH,
        )

    for part in range(total):
        each_peer(counts[part], lambda offset: descriptor(part, offset, False).start())
    for copy in locals_started:
        copy.wait()
    for part in range(total):
        each_peer(counts[part], lambda offset: descriptor(part, offset, True).wait_recv())
    for part in range(total):
        each_peer(counts[part], lambda offset: descriptor(part, offset, False).wait_send())


def exchange(call_id, name, parts, greet_axes=None):
    kinds = tuple((kind, axes) for kind, axes, _ in parts)
    arrays = [array for _, _, array in parts]
    counts = tuple(lax.axis_size(axes) for _, axes in kinds)
    if greet_axes is None:
        greet_axes = (kinds[0][1],)
    greet = tuple((axes, lax.axis_size(axes)) for axes in greet_axes)
    shapes = [
        jax.ShapeDtypeStruct(
            (count,) + array.shape if kind == "gather" else array.shape, array.dtype
        )
        for (kind, _, array), count in zip(parts, counts)
    ]
    scratch = []
    for count in counts:
        scratch += [
            pltpu.SemaphoreType.DMA((count,)),
            pltpu.SemaphoreType.DMA((count,)),
            pltpu.SemaphoreType.DMA((1,)),
        ]
    in_vmem = pl.BlockSpec(memory_space=pltpu.VMEM)
    return pl.pallas_call(
        lambda *refs: exchange_kernel(kinds, greet, counts, *refs),
        out_shape=shapes,
        in_specs=[in_vmem] * len(arrays),
        out_specs=[in_vmem] * len(arrays),
        scratch_shapes=scratch,
        compiler_params=pltpu.CompilerParams(collective_id=call_id, has_side_effects=True),
        name=name,
    )(*arrays)


def digit_place(digit):
    if digit == "head_slow":
        return lax.axis_index("head") // fast_size()
    if digit == "head_fast":
        return lax.rem(lax.axis_index("head"), fast_size())
    return lax.axis_index(digit)


def fast_size():
    return 2 if lax.axis_size("head") % 2 == 0 else 1


def digit_size(digit):
    if digit == "head_slow":
        return lax.axis_size("head") // fast_size()
    if digit == "head_fast":
        return fast_size()
    return lax.axis_size(digit)


def digit_device(digit, value):
    if digit == "head_slow":
        return {"head": value * fast_size() + digit_place("head_fast")}
    if digit == "head_fast":
        return {"head": digit_place("head_slow") * fast_size() + value}
    return {digit: value}


def staged_kernel(plans, greeted, *refs):
    total = len(plans)
    sources, targets, sems = refs[:total], refs[total : 2 * total], list(refs[2 * total :])
    barrier = pltpu.get_barrier_semaphore()
    waits = 0
    for digit in greeted:
        count, me = digit_size(digit), digit_place(digit)
        for offset in range(1, count):
            pl.semaphore_signal(
                barrier,
                inc=1,
                device_id=digit_device(digit, lax.rem(me + offset, count)),
                device_id_type=pl.DeviceIdType.MESH,
            )
            waits += 1
    local_sems = sems[:total]
    rest = sems[total:]
    pairs = []
    for plan in plans:
        pairs.append([(rest.pop(0), rest.pop(0)) for _ in plan])
    own = []
    for part, plan in enumerate(plans):
        here = tuple(digit_place(digit) for digit in reversed(plan))
        copy = pltpu.make_async_copy(sources[part], targets[part].at[here], local_sems[part].at[0])
        copy.start()
        own.append(copy)
    pl.semaphore_wait(barrier, waits)

    def descriptors(part, turn, backward):
        plan = plans[part]
        digit = plan[turn]
        count, me = digit_size(digit), digit_place(digit)
        outer = tuple(digit_place(name) for name in reversed(plan[turn + 1 :]))
        found = []
        for offset in range(1, count):
            to = lax.rem(me + offset, count)
            origin = lax.rem(me + count - offset, count) if backward else me
            source = sources[part] if turn == 0 else targets[part].at[outer + (me,)]
            found.append(
                pltpu.make_async_remote_copy(
                    src_ref=source,
                    dst_ref=targets[part].at[outer + (origin,)],
                    send_sem=pairs[part][turn][0].at[offset],
                    recv_sem=pairs[part][turn][1].at[origin],
                    device_id=digit_device(digit, to),
                    device_id_type=pl.DeviceIdType.MESH,
                )
            )
        return found

    most = max(len(plan) for plan in plans)
    for turn in range(most + 1):
        for part, plan in enumerate(plans):
            if 0 < turn <= len(plan):
                for copy in descriptors(part, turn - 1, True):
                    copy.wait_recv()
            if turn == 1:
                own[part].wait()
            if turn < len(plan):
                for copy in descriptors(part, turn, False):
                    copy.start()
    for part, plan in enumerate(plans):
        for turn in range(len(plan)):
            for copy in descriptors(part, turn, False):
                copy.wait_send()


def staged_gather(call_id, name, parts):
    plans = [plan for plan, _ in parts]
    arrays = [array for _, array in parts]
    greeted = []
    for plan in plans:
        greeted += [digit for digit in plan if digit not in greeted]
    shapes = [
        jax.ShapeDtypeStruct(
            tuple(digit_size(digit) for digit in reversed(plan)) + array.shape, array.dtype
        )
        for plan, array in parts
    ]
    scratch = [pltpu.SemaphoreType.DMA((1,)) for _ in parts]
    for plan in plans:
        for digit in plan:
            scratch += [pltpu.SemaphoreType.DMA((digit_size(digit),))] * 2
    in_vmem = pl.BlockSpec(memory_space=pltpu.VMEM)
    return pl.pallas_call(
        lambda *refs: staged_kernel(plans, greeted, *refs),
        out_shape=shapes,
        in_specs=[in_vmem] * len(arrays),
        out_specs=[in_vmem] * len(arrays),
        scratch_shapes=scratch,
        compiler_params=pltpu.CompilerParams(collective_id=call_id, has_side_effects=True),
        name=name,
    )(*arrays)


def gather_rows(call_id, name, rows):
    (blocks,) = exchange(call_id, name, [("gather", ("head",), rows)])
    return blocks.reshape(-1, rows.shape[1])


def shifted(array, axis, offset):
    count = lax.axis_size(axis)
    return lax.ppermute(array, axis, [(here, (here + offset) % count) for here in range(count)])


def gelu_parts(value):
    root = math.sqrt(2.0 / math.pi)
    square = value * value
    tanh_part = jnp.tanh(root * (value + 0.044715 * value * square))
    gelu = 0.5 * value * (1.0 + tanh_part)
    slope = 0.5 * (1.0 + tanh_part) + 0.5 * value * (1.0 - tanh_part * tanh_part) * root * (
        1.0 + 3.0 * 0.044715 * square
    )
    return gelu, slope


def mlp_forward_kernel(rows_ref, gate_ref, up_ref, down_ref, gate_pre_ref, up_pre_ref, hidden_ref, part_ref):
    rows = rows_ref[...]
    gate_pre = rows_dot(rows, gate_ref[...], 1, 1)
    up_pre = rows_dot(rows, up_ref[...], 1, 1)
    gate_pre_ref[...] = gate_pre
    up_pre_ref[...] = up_pre
    hidden = (gelu_parts(gate_pre)[0] * up_pre).astype(jnp.bfloat16)
    hidden_ref[...] = hidden
    part_ref[...] = rows_dot(hidden, down_ref[...], 1, 0).astype(jnp.bfloat16)


def mlp_backward_kernel(
    rows_ref, gate_ref, up_ref, down_ref, gate_pre_ref, up_pre_ref, grad_gate_ref, grad_up_ref, part_ref
):
    grad_hidden = rows_dot(rows_ref[...], down_ref[...], 1, 1)
    gelu, slope = gelu_parts(gate_pre_ref[...])
    grad_gate = (grad_hidden * up_pre_ref[...] * slope).astype(jnp.bfloat16)
    grad_up = (grad_hidden * gelu).astype(jnp.bfloat16)
    grad_gate_ref[...] = grad_gate
    grad_up_ref[...] = grad_up
    part_ref[...] = (
        rows_dot(grad_gate, gate_ref[...], 1, 0) + rows_dot(grad_up, up_ref[...], 1, 0)
    ).astype(jnp.bfloat16)


def rows_dot(left, right, left_dim, right_dim):
    return lax.dot_general(
        left, right, (((left_dim,), (right_dim,)), ((), ())), preferred_element_type=jnp.float32
    )


def add_up(blocks):
    return jnp.sum(blocks.astype(jnp.float32), axis=0)


def local(
    block_in,
    cotangent,
    positions,
    norm_gains,
    qk_gains,
    w_query,
    w_key,
    w_value,
    w_out,
    w_gate,
    w_up,
    w_down,
):
    tok_rows, model_width = block_in.shape
    head_count = lax.axis_size("head")
    head_width = qk_gains.shape[1]
    ctx_slot = lax.axis_index("ctx")
    query_rows = head_count * tok_rows
    group_count = lax.axis_size(weight_axes)
    every_count = lax.axis_size(every_axis)
    length_all = lax.axis_size(sequence_axes) * tok_rows
    query_cols = w_query.shape[1]
    key_cols = w_key.shape[1]
    ff_cols = w_gate.shape[1]
    narrow = jnp.bfloat16

    ff_rows = jnp.concatenate([w_gate.T, w_up.T, w_down], axis=0)
    dp_count, ctx_count = lax.axis_size("dp"), lax.axis_size("ctx")

    to_heads = [
        (head * group_count + index, index * head_count + head)
        for head in range(head_count)
        for index in range(group_count)
    ]
    to_owners = [(there, here) for here, there in to_heads]
    head_rows = lax.ppermute(
        jnp.concatenate([w_query.T, w_out], axis=0), every_axis, to_heads
    )
    key_value_rows = jnp.concatenate([w_key.T, w_value.T], axis=0)
    block_all, key_value_all, head_all, position_all = staged_gather(
        1,
        "first_gather",
        [
            (("ctx", "head_slow", "head_fast"), block_in),
            (("dp", "ctx", "head_slow", "head_fast"), key_value_rows),
            (("dp", "ctx"), head_rows),
            (("ctx",), positions.reshape(-1, 128)),
        ],
    )
    block_all, ff_rows = lax.optimization_barrier((block_all, ff_rows))
    near_blocks = [ff_rows] + [shifted(ff_rows, "dp", offset) for offset in range(1, dp_count)]
    ff_across = [shifted(ff_rows, "ctx", offset) for offset in range(1, ctx_count)]
    block_all = block_all.transpose(2, 1, 0, 3, 4)
    key_value_all = key_value_all.transpose(3, 2, 1, 0, 4, 5).reshape(
        every_count, 2 * key_cols, model_width
    )
    head_all = head_all.transpose(1, 0, 2, 3).reshape(group_count, 2 * query_cols, model_width)
    query_weight = head_all[:, :query_cols].reshape(head_width, model_width)
    out_weight = head_all[:, query_cols:].reshape(head_width, model_width)
    key_weight = key_value_all[:, :key_cols].reshape(head_width, model_width)
    value_weight = key_value_all[:, key_cols:].reshape(head_width, model_width)

    input_all = block_all.reshape(length_all, model_width).astype(jnp.float32)
    attn_in_all = norm_rows(input_all, norm_gains[0])[0].astype(narrow)
    first_query = ctx_slot * query_rows
    attn_in = lax.dynamic_slice_in_dim(attn_in_all, first_query, query_rows)
    query_raw = rows_dot(attn_in, query_weight, 1, 1)
    key_raw = rows_dot(attn_in_all, key_weight, 1, 1)
    all_values = rows_dot(attn_in_all, value_weight, 1, 1).astype(narrow)
    query_normed, inverse_query = norm_rows(query_raw, qk_gains[0])
    key_normed, inverse_key = norm_rows(key_raw, qk_gains[1])
    cosine, sine_part = rope_angles(position_all.reshape(length_all), head_width)
    cosine_own = lax.dynamic_slice_in_dim(cosine, first_query, query_rows)
    sine_own = lax.dynamic_slice_in_dim(sine_part, first_query, query_rows)
    head_query = (rotate(query_normed, cosine_own, sine_own) * score_scale).astype(narrow)
    all_keys = rotate(key_normed, cosine, sine_part).astype(narrow)

    query_index = first_query + jnp.arange(query_rows, dtype=jnp.int32)
    lowest_key = query_index - positions
    key_index = jnp.arange(length_all, dtype=jnp.int32)
    visible = (key_index[None, :] <= query_index[:, None]) & (
        key_index[None, :] >= lowest_key[:, None]
    )
    scores = jnp.where(visible, rows_dot(head_query, all_keys, 1, 1), negative_fill)
    top = jnp.max(scores, axis=1, keepdims=True)
    log_total = top + jnp.log(jnp.sum(jnp.exp(scores - top), axis=1, keepdims=True))
    probs_wide = jnp.exp(scores - log_total)
    prob_rows = probs_wide.astype(narrow)
    attn_exact = rows_dot(prob_rows, all_values, 1, 0)
    attn_out = attn_exact.astype(narrow)
    branch_part = rows_dot(attn_out, out_weight, 1, 0).astype(narrow)
    (branch_blocks,) = exchange(
        2,
        "branch_scatter",
        [("scatter", ("head",), branch_part.reshape(head_count, tok_rows, model_width))],
    )
    branch = add_up(branch_blocks)
    input_wide = block_in.astype(jnp.float32)
    inverse_in = norm_rows(input_wide, norm_gains[0])[1]
    branch_normed, inverse_branch = norm_rows(branch, norm_gains[1])
    middle = input_wide + branch_normed
    mlp_norm, inverse_mid = norm_rows(middle, norm_gains[2])
    mlp_norm, near_blocks, ff_across = lax.optimization_barrier((mlp_norm, near_blocks, ff_across))
    ff_slots = list(near_blocks)
    for offset in range(1, ctx_count):
        ff_slots += [ff_across[offset - 1]]
        ff_slots += [shifted(block, "ctx", offset) for block in near_blocks[1:]]
    mlp_in = gather_rows(3, "mlp_gather", mlp_norm.astype(narrow))

    ff_width = group_count * ff_cols
    gate_weight = jnp.concatenate([block[:ff_cols] for block in ff_slots], axis=0)
    up_weight = jnp.concatenate([block[ff_cols : 2 * ff_cols] for block in ff_slots], axis=0)
    down_weight = jnp.concatenate([block[2 * ff_cols :] for block in ff_slots], axis=0)
    wide_ff = jax.ShapeDtypeStruct((query_rows, ff_width), jnp.float32)
    narrow_ff = jax.ShapeDtypeStruct((query_rows, ff_width), narrow)
    narrow_rows = jax.ShapeDtypeStruct((query_rows, model_width), narrow)
    gate_pre, up_pre, hidden, down_part = pl.pallas_call(
        mlp_forward_kernel,
        out_shape=[wide_ff, wide_ff, narrow_ff, narrow_rows],
        name="mlp_forward",
    )(mlp_in, gate_weight, up_weight, down_weight)
    (down_blocks,) = exchange(
        4,
        "down_scatter",
        [("scatter", ("head",), down_part.reshape(head_count, tok_rows, model_width))],
    )
    down_raw = add_up(down_blocks)
    down_normed, inverse_down = norm_rows(down_raw, norm_gains[3])
    block_out = (middle + down_normed).astype(narrow)
    cot_wide = cotangent.astype(jnp.float32)
    grad_down_raw, gain_three = norm_back(down_raw, inverse_down, norm_gains[3], cot_wide)
    grad_down_in = gather_rows(5, "grad_down_gather", grad_down_raw.astype(narrow))
    grad_gate_in, grad_up_in, grad_mlp_part = pl.pallas_call(
        mlp_backward_kernel,
        out_shape=[narrow_ff, narrow_ff, narrow_rows],
        name="mlp_backward",
    )(grad_down_in, gate_weight, up_weight, down_weight, gate_pre, up_pre)
    slots = (ctx_count, dp_count, ff_cols, model_width)
    ff_terms = jnp.concatenate(
        [
            rows_dot(grad_gate_in, mlp_in, 0, 0).astype(narrow).reshape(slots),
            rows_dot(grad_up_in, mlp_in, 0, 0).astype(narrow).reshape(slots),
            rows_dot(hidden, grad_down_in, 0, 0).astype(narrow).reshape(slots),
        ],
        axis=2,
    )
    half = dp_count // 2
    grad_mlp_blocks, ff_early = exchange(
        6,
        "grad_mlp_scatter",
        [
            (
                "scatter",
                ("head",),
                grad_mlp_part.reshape(head_count, tok_rows, model_width),
            ),
            ("relative", ("ctx",), ff_terms[:, :half]),
        ],
        (("head",), ("ctx",)),
    )
    grad_mlp_in = add_up(grad_mlp_blocks)
    grad_mid_part, gain_two = norm_back(middle, inverse_mid, norm_gains[2], grad_mlp_in)
    grad_middle = cot_wide + grad_mid_part
    grad_branch_raw, gain_one = norm_back(branch, inverse_branch, norm_gains[1], grad_middle)
    grad_branch_blocks, ff_late = exchange(
        7,
        "grad_branch_gather",
        [
            ("gather", ("head",), grad_branch_raw.astype(narrow)),
            ("relative", ("ctx",), ff_terms[:, half:]),
        ],
        (("head",), ("ctx",)),
    )
    grad_branch = grad_branch_blocks.reshape(query_rows, model_width)
    ff_sums = jnp.concatenate([add_up(ff_early), add_up(ff_late)], axis=0).astype(narrow)
    head_grad = rows_dot(grad_branch, out_weight, 1, 1).astype(narrow)
    row_delta = jnp.sum(head_grad.astype(jnp.float32) * attn_exact, axis=1, keepdims=True)
    grad_probs = rows_dot(head_grad, all_values, 1, 1)
    grad_scores = (probs_wide * (grad_probs - row_delta)).astype(narrow)
    value_sums = rows_dot(prob_rows, head_grad, 0, 0)
    key_sums = rows_dot(grad_scores, head_query, 0, 0)
    grad_rot_query = rows_dot(grad_scores, all_keys, 1, 0)
    query_back = rotate(grad_rot_query * score_scale, cosine_own, -sine_own)
    grad_query_raw, gain_query = norm_back(query_raw, inverse_query, qk_gains[0], query_back)
    key_back = rotate(key_sums, cosine, -sine_part)
    grad_key_raw, gain_key = norm_back(key_raw, inverse_key, qk_gains[1], key_back)
    grad_query_in = grad_query_raw.astype(narrow)
    grad_key_in = grad_key_raw.astype(narrow)
    grad_value_in = value_sums.astype(narrow)
    grad_attn_part = rows_dot(grad_key_in, key_weight, 1, 0) + rows_dot(
        grad_value_in, value_weight, 1, 0
    )
    own_part = lax.dynamic_slice_in_dim(grad_attn_part, first_query, query_rows) + rows_dot(
        grad_query_in, query_weight, 1, 0
    )
    grad_attn_part = lax.dynamic_update_slice_in_dim(grad_attn_part, own_part, first_query, 0)
    head_terms = jnp.concatenate(
        [
            rows_dot(grad_query_in, attn_in, 0, 0).reshape(group_count, query_cols, model_width),
            rows_dot(attn_out, grad_branch, 0, 0).reshape(group_count, query_cols, model_width),
        ],
        axis=1,
    ).astype(narrow)
    planes = (dp_count, every_count // dp_count, key_cols, model_width)
    key_value_terms = jnp.concatenate(
        [
            rows_dot(grad_key_in, attn_in_all, 0, 0).reshape(planes),
            rows_dot(grad_value_in, attn_in_all, 0, 0).reshape(planes),
        ],
        axis=2,
    ).astype(narrow).transpose(1, 0, 2, 3)
    head_terms = head_terms.reshape(dp_count, ctx_count, 2 * query_cols, model_width)
    grad_attn_blocks, head_blocks, key_value_blocks, ff_blocks = exchange(
        8,
        "last_scatter",
        [
            (
                "scatter",
                sequence_axes,
                grad_attn_part.astype(narrow).reshape(-1, tok_rows, model_width),
            ),
            ("scatter", ("ctx",), head_terms.transpose(1, 0, 2, 3)),
            ("scatter", sequence_axes, key_value_terms),
            ("relative", ("dp",), ff_sums),
        ],
        (sequence_axes, ("dp",)),
    )
    ff_own = add_up(ff_blocks)
    grad_attn_in = add_up(grad_attn_blocks)
    grad_in_part, gain_zero = norm_back(input_wide, inverse_in, norm_gains[0], grad_attn_in)
    d_block_in = (grad_middle + grad_in_part).astype(narrow)

    pad = ((0, 0), (0, model_width - head_width))
    gain_terms = jnp.concatenate(
        [
            jnp.sum(gain_zero, axis=0, keepdims=True),
            jnp.sum(gain_one, axis=0, keepdims=True),
            jnp.sum(gain_two, axis=0, keepdims=True),
            jnp.sum(gain_three, axis=0, keepdims=True),
            jnp.pad(jnp.sum(gain_query, axis=0, keepdims=True), pad),
            jnp.pad(jnp.sum(gain_key, axis=0, keepdims=True), pad),
            jnp.zeros((2, model_width), jnp.float32),
        ],
        axis=0,
    )
    gain_blocks, head_blocks, key_value_blocks = exchange(
        9,
        "depth_exchange",
        [
            ("gather", ("dp",), gain_terms),
            ("scatter", ("dp",), add_up(head_blocks).astype(narrow)),
            ("scatter", ("dp",), add_up(key_value_blocks).astype(narrow)),
        ],
    )
    head_own = lax.ppermute(add_up(head_blocks).astype(narrow), every_axis, to_owners).astype(
        jnp.float32
    )
    (gain_blocks,) = exchange(10, "gain_gather", [("gather", sequence_axes, add_up(gain_blocks))])
    gains = add_up(gain_blocks)
    key_value_own = add_up(key_value_blocks)
    return (
        block_out,
        d_block_in,
        gains[:4],
        gains[4:6, :head_width],
        head_own[:query_cols].T,
        key_value_own[:key_cols].T,
        key_value_own[key_cols:].T,
        head_own[query_cols:],
        ff_own[:ff_cols].T,
        ff_own[ff_cols : 2 * ff_cols].T,
        ff_own[2 * ff_cols :],
    )


bits = (0, 1)


class Mail:
    def __init__(self, send_sems, recv_sems):
        self.send_sems, self.recv_sems = send_sems, recv_sems
        self.started = []

    def push(self, source, target, to, when=None, arrives_as=None):
        number = len(self.started)
        copy = pltpu.make_async_remote_copy(
            src_ref=source,
            dst_ref=target,
            send_sem=self.send_sems.at[number],
            recv_sem=self.recv_sems.at[number if arrives_as is None else arrives_as],
            device_id=to,
            device_id_type=pl.DeviceIdType.MESH,
        )
        if when is None:
            copy.start()
        else:
            pl.when(when)(copy.start)
        self.started.append((copy, when))
        return copy

    def settle(self):
        for copy, when in self.started:
            if when is None:
                copy.wait_send()
            else:
                pl.when(when)(copy.wait_send)


copy_limit = 176


def fused_kernel(names, *refs):
    r = types.SimpleNamespace(**dict(zip(names, refs)))
    narrow, wide = jnp.bfloat16, jnp.float32
    d, x, h = lax.axis_index("dp"), lax.axis_index("ctx"), lax.axis_index("head")
    depth = lax.axis_size("dp")
    y, c = h // 2, lax.rem(h, 2)
    me = x * 4 + h
    mail = Mail(r.send_sems, r.recv_sems)
    rows, width = r.block_in.shape
    head_width = r.qk_gains.shape[1]
    half_width = head_width // 2
    heads, query_cols = r.q_raw.shape[1] // head_width, r.q_rows.shape[0]
    key_cols = r.key_rows.shape[0]
    ff_cols = r.gate_rows.shape[0]
    all_rows = 8 * rows
    full = heads * head_width

    def deep(offset):
        return lax.rem(d + offset, depth)

    def z_peer(offset):
        return {"dp": deep(offset)}

    x_peer = {"ctx": 1 - x}
    y_peer = {"head": (1 - y) * 2 + c}
    c_peer = {"head": y * 2 + 1 - c}

    def flip(place, bit):
        return 1 - place if bit else place

    def plane_peer(dx, dy, dc):
        return {"ctx": flip(x, dx), "head": flip(y, dy) * 2 + flip(c, dc)}

    plane_steps = [(dx, dy, dc) for dx in bits for dy in bits for dc in bits][1:]
    chip_steps = [(1, 1), (1, 0), (0, 1)]

    barrier = pltpu.get_barrier_semaphore()
    greeted = [z_peer(offset) for offset in range(1, depth)] + [plane_peer(*s) for s in plane_steps]
    for peer in greeted:
        pl.semaphore_signal(barrier, inc=1, device_id=peer, device_id_type=pl.DeviceIdType.MESH)
    r.block_all[x, y, c] = r.block_in[...]
    key_value = [r.key_rows[...].astype(wide), r.value_rows[...].astype(wide)]
    r.kv_all[d, x, y, c] = jnp.concatenate(key_value, axis=0).astype(narrow)
    r.q_all[d, x, y, c] = r.q_rows[...]
    r.o_all[d, x, y, c] = r.o_rows[...]
    for piece, own in enumerate((r.gate_rows, r.up_rows, r.down_rows)):
        r.ff_all[d, x, pl.ds(piece * ff_cols, ff_cols)] = own[...]
    r.pos_pair[x] = r.positions[...].astype(wide)
    pl.semaphore_wait(barrier, len(greeted))

    got_z, got_x, got_y, got_c = {}, {}, {}, {}

    def place(part):
        return (x, y, c) if part == "block" else (d, x, y, c)

    def source(part):
        return getattr(r, part + "_all").at[place(part)]

    def own_to_x(part):
        got_x[part, 0] = mail.push(source(part), getattr(r, part + "_all").at[place(part)], x_peer)

    def own_to_y(part):
        got_y[part, 0] = [
            mail.push(source(part), getattr(r, part + "_all").at[place(part)], y_peer)
        ]

    relayed = depth >= 4
    relays = ((depth - 1, 2, 0), (1, depth - 3, depth - 1)) if relayed else ()
    z_order = sorted(range(1, depth), key=lambda offset: offset != 2)

    def blocks_to_z(key, block_of):
        for offset in range(1, depth):
            when = None
            if relayed and offset == 1:
                when = d < depth - 1
            if relayed and offset == depth - 1:
                when = d > 0
            number = len(mail.started)
            copy = mail.push(block_of(d), block_of(d), z_peer(offset), when)
            got_z[key, offset] = copy, number

    def blocks_relay(key, block_of):
        if relayed:
            got_z[key, 2][0].wait_recv()
            block = block_of(deep(depth - 2))
            for other, relay, _ in relays:
                to = {"dp": lax.rem(d + depth - 2 + other, depth)}
                mail.push(block, block, to, d == relay, got_z[key, other][1])

    def blocks_to_x(key, block_of):
        for offset in z_order:
            if not relayed or offset != 2:
                got_z[key, offset][0].wait_recv()
            block = block_of(deep(depth - offset))
            got_x[key, offset] = mail.push(block, block, x_peer)

    def relay(part):
        blocks_relay(part, block_of(part))

    def block_of(part):
        return lambda slot: getattr(r, part + "_all").at[(slot,) + place(part)[1:]]

    def own_to_z(part):
        blocks_to_z(part, block_of(part))

    def to_x(part):
        blocks_to_x(part, block_of(part))

    def near_to_y(part):
        got_x[part, 0].wait_recv()
        at = (1 - x, y, c) if part == "block" else (d, 1 - x, y, c)
        block = getattr(r, part + "_all").at[at]
        got_y[part, 0].append(mail.push(block, block, y_peer))

    def to_y(part):
        for offset in range(1, depth):
            got_x[part, offset].wait_recv()
            block = getattr(r, part + "_all").at[deep(depth - offset), :, y, c]
            got_y[part, offset] = [mail.push(block, block, y_peer)]

    def to_c(part):
        for offset in range(1 if part == "block" else depth):
            for copy in got_y[part, offset]:
                copy.wait_recv()
            block = getattr(r, part + "_all")
            block = block if part == "block" else block.at[deep(depth - offset)]
            block = block.at[:, :, c]
            got_c[part, offset] = mail.push(block, block, c_peer)

    def arrived(part):
        for offset in range(1 if part == "block" else depth):
            got_c[part, offset].wait_recv()

    def ff_piece(slot, piece):
        return r.ff_all.at[slot, x, pl.ds(piece * ff_cols, ff_cols)]

    def ff_to_z(piece):
        blocks_to_z(("ff", piece), lambda slot: ff_piece(slot, piece))

    def ff_relay(piece):
        blocks_relay(("ff", piece), lambda slot: ff_piece(slot, piece))

    def ff_own_to_x():
        block = r.ff_all.at[d, x]
        got_x["ff", 0] = mail.push(block, block, x_peer)

    def ff_to_x(piece):
        blocks_to_x(("ff", piece), lambda slot: ff_piece(slot, piece))

    position_copy = mail.push(r.pos_pair.at[x], r.pos_pair.at[x], x_peer)
    for part in ("kv", "block", "q", "o"):
        own_to_x(part)
        own_to_y(part)
        if part != "block":
            own_to_z(part)

    def rope_tables():
        position_copy.wait_recv()
        for half in bits:
            r.pos_all[half * 4 : half * 4 + 4] = r.pos_pair[half]
        turned = r.pos_all[...].T
        ladder = lax.broadcasted_iota(jnp.int32, (1, half_width), 1).astype(wide)
        frequency = jnp.exp(ladder * (-2.0 / head_width) * math.log(rope_base))
        column = lax.broadcasted_iota(jnp.int32, turned.shape, 1)
        r.pos_own[...] = jnp.sum(jnp.where(column == me, turned, 0.0), axis=1, keepdims=True)
        for block in range(8):
            angle = turned[:, block : block + 1] * frequency
            r.cosine[block] = jnp.cos(angle)
            r.sine[block] = jnp.sin(angle)

    def shuffle():
        size = 2 * head_width
        there = lax.broadcasted_iota(jnp.int32, (size, size), 1).astype(wide)
        here = lax.broadcasted_iota(jnp.int32, (size, size), 0).astype(wide)

        def sorted_place(place):
            block = jnp.floor((place + 0.5) / (2 * key_cols))
            inside = place - block * (2 * key_cols)
            value = inside >= key_cols
            return block * key_cols + jnp.where(value, inside - key_cols + head_width, inside)

        r.unsort[...] = jnp.where(sorted_place(here) == there, 1.0, 0.0).astype(narrow)
        r.sort[...] = jnp.where(sorted_place(there) == here, 1.0, 0.0).astype(narrow)

    def attention_inputs():
        arrived("block")
        gain = r.norm_gains[0:1]
        for px in bits:
            for py in bits:
                for pc in bits:
                    values = r.block_all[px, py, pc].astype(wide)
                    r.attn_in[px * 4 + py * 2 + pc] = norm_rows(values, gain)[0].astype(narrow)

    def keys_and_values():
        arrived("kv")
        blocks = r.kv_all[...].reshape(2 * head_width, width)
        r.kv_sorted[...] = rows_dot(r.sort[...], blocks, 1, 0).astype(narrow)
        gain = r.qk_gains[1:2]
        for pair in range(4):
            two = pl.ds(2 * pair, 2)
            inputs = r.attn_in[two].reshape(2 * rows, width)
            raw = rows_dot(inputs, r.kv_sorted[...], 1, 1)
            key_raw = raw[:, :head_width]
            r.key_raw[two] = key_raw.reshape(2, rows, head_width)
            cosine = r.cosine[two].reshape(2 * rows, half_width)
            sine_part = r.sine[two].reshape(2 * rows, half_width)
            turned = rotate(norm_rows(key_raw, gain)[0], cosine, sine_part)
            r.keys[pl.ds(2 * pair * rows, 2 * rows)] = turned.astype(narrow)
            r.values[pl.ds(2 * pair * rows, 2 * rows)] = raw[:, head_width:].astype(narrow)

    shuffle()
    relay("kv")
    relay("q")
    to_x("kv")
    relay("o")
    near_to_y("kv")
    near_to_y("block")
    ff_to_z(0)
    to_x("q")
    near_to_y("q")
    rope_tables()
    to_y("kv")
    ff_to_z(1)
    ff_own_to_x()
    to_x("o")
    near_to_y("o")
    ff_relay(0)
    to_y("q")
    ff_to_z(2)
    to_c("block")
    attention_inputs()
    ff_relay(1)
    ff_to_x(0)
    to_c("kv")
    to_y("o")
    keys_and_values()
    ff_relay(2)
    ff_to_x(1)
    to_c("q")

    query_gain = r.qk_gains[0:1]
    arrived("q")
    weight = r.q_all[...].reshape(full, width)
    r.q_raw[...] = rows_dot(r.attn_in[me], weight, 1, 1)
    for head in range(heads):
        turned = rotate(
            norm_rows(r.q_raw[:, head * head_width : (head + 1) * head_width], query_gain)[0],
            r.cosine[me],
            r.sine[me],
        )
        r.q_rot[head] = (turned * score_scale).astype(narrow)
    ff_to_x(2)
    to_c("o")

    query_index = lax.broadcasted_iota(jnp.int32, (rows, all_rows), 0) + me * rows
    key_index = lax.broadcasted_iota(jnp.int32, (rows, all_rows), 1)
    lowest_key = query_index - r.pos_own[...].astype(jnp.int32)
    visible = (key_index <= query_index) & (key_index >= lowest_key)
    r.bias[...] = jnp.where(visible, 0.0, negative_fill)
    for head in range(heads):
        scores = rows_dot(r.q_rot[head], r.keys[...], 1, 1)
        scores = jnp.where(r.bias[...] < 0.0, negative_fill, scores)
        top = jnp.max(scores, axis=1, keepdims=True)
        raised = jnp.exp(scores - top)
        prob_rows = raised * (1.0 / jnp.sum(raised, axis=1, keepdims=True))
        r.probs[head] = prob_rows
        r.probs_narrow[head] = prob_rows.astype(narrow)
        exact = rows_dot(prob_rows.astype(narrow), r.values[...], 1, 0)
        r.exact[head] = exact
        r.attn_out[:, head * head_width : (head + 1) * head_width] = exact.astype(narrow)
    arrived("o")
    out_weight = r.o_all[...].reshape(full, width)
    r.branch[...] = rows_dot(r.attn_out[...], out_weight, 1, 0)
    def send_factor(name):
        copies = []
        for step in plane_steps:
            px, py, pc = (flip(here, bit) for here, bit in zip((x, y, c), step))
            copies.append(
                mail.push(getattr(r, name).at[:, px, py, pc], getattr(r, name + "_got").at[me], plane_peer(*step))
            )
        getattr(r, name + "_got")[me] = getattr(r, name)[:, x, y, c]
        return copies

    def send_group_factor():
        copies = []
        for dy, dc in chip_steps:
            source = r.out_turned.at[:, :, flip(y, dy), flip(c, dc)]
            copies.append(mail.push(source, r.out_turned_got.at[y, c], plane_peer(0, dy, dc)))
        r.out_turned_got[y, c] = r.out_turned[:, :, y, c]
        return copies

    def turned_blocks(name, values, columns):
        getattr(r, name)[...] = values.astype(wide).T.astype(narrow).reshape(depth, 2, 2, 2, columns, rows)

    input_wide = r.block_in[...].astype(wide)
    branch_normed = norm_rows(r.branch[...], r.norm_gains[1:2])[0]
    r.middle[...] = input_wide + branch_normed
    mlp_rows = norm_rows(r.middle[...], r.norm_gains[2:3])[0].astype(narrow)

    def share_rows(name, values):
        getattr(r, name)[y, c] = values
        block = getattr(r, name).at[y, c]
        return mail.push(block, block, c_peer), mail.push(block, block, y_peer)

    def far_rows(name, from_y):
        from_y.wait_recv()
        block = getattr(r, name).at[1 - y, c]
        return mail.push(block, block, c_peer)

    def fetch_ff():
        got_x["ff", 0].wait_recv()
        for piece in range(3):
            for offset in range(1, depth):
                got_x[("ff", piece), offset].wait_recv()

    def ff_part(index):
        piece = r.ff_all[:, :, pl.ds(index * ff_cols, ff_cols)]
        return piece.reshape(2 * depth * ff_cols, width)

    def group_sum(name, half, own_rows, waiting, early, between):
        part, near, far = getattr(r, name), getattr(r, name + "_near"), getattr(r, name + "_far")
        from_c, from_y = own_rows
        from_c.wait_recv()
        half(y)
        near_own = mail.push(part.at[y, 1 - c], near.at[0], c_peer)
        forwarded = from_y()
        waiting()
        forwarded.wait_recv()
        early()
        half(1 - y)
        near_far = mail.push(part.at[1 - y, 1 - c], near.at[1], c_peer)
        near_far.wait_recv()
        summed = part[1 - y, c].astype(wide) + near[1].astype(wide)
        getattr(r, name + "_sum")[...] = summed.astype(narrow)
        far_copy = mail.push(getattr(r, name + "_sum"), far, y_peer)
        between()
        near_own.wait_recv()
        own = part[y, c].astype(wide) + near[0].astype(wide)
        far_copy.wait_recv()
        return own + far[...].astype(wide)

    def forward_half(side):
        inputs = r.mlp_in[side].reshape(2 * rows, width)
        gate_pre = rows_dot(inputs, ff_part(0), 1, 1)
        up_pre = rows_dot(inputs, ff_part(1), 1, 1)
        r.gate_pre[side] = gate_pre
        r.up_pre[side] = up_pre
        hidden = (gelu_parts(gate_pre)[0] * up_pre).astype(narrow)
        r.hidden[side] = hidden
        part = rows_dot(hidden, ff_part(2), 1, 0).astype(narrow)
        r.down[side] = part.reshape(2, rows, width)

    def nothing():
        pass

    near_copy, y_copy = share_rows("mlp_in", mlp_rows)
    turned_blocks("out_turned", r.attn_out[...], query_cols)
    out_copies = send_group_factor()
    fetch_ff()
    r.down_raw[...] = group_sum(
        "down", forward_half, (near_copy, lambda: far_rows("mlp_in", y_copy)), nothing, nothing, nothing
    )
    down_raw = r.down_raw[...]
    down_normed, inverse_down = norm_rows(down_raw, r.norm_gains[3:4])
    r.block_out[...] = (r.middle[...] + down_normed).astype(narrow)
    cot_wide = r.cotangent[...].astype(wide)
    grad_down_raw, gain_three = norm_back(down_raw, inverse_down, r.norm_gains[3:4], cot_wide)
    r.gains[...] = jnp.zeros_like(r.gains)
    r.gains[3:4] = jnp.sum(gain_three, axis=0, keepdims=True)

    def backward_half(side):
        grad_hidden = rows_dot(r.grad_down[side].reshape(2 * rows, width), ff_part(2), 1, 1)
        gelu, slope = gelu_parts(r.gate_pre[side])
        grad_gate = (grad_hidden * r.up_pre[side] * slope).astype(narrow)
        grad_up = (grad_hidden * gelu).astype(narrow)
        r.grad_gate[side] = grad_gate
        r.grad_up[side] = grad_up
        part = rows_dot(grad_gate, ff_part(0), 1, 0) + rows_dot(grad_up, ff_part(1), 1, 0)
        r.mlp_back[side] = part.astype(narrow).reshape(2, rows, width)

    ff_width = 2 * depth * ff_cols

    factors = ((r.grad_gate, r.mlp_in), (r.grad_up, r.mlp_in), (r.hidden, r.grad_down))

    def side_terms(index, side):
        left, right = factors[index]
        return rows_dot(left[side], right[side].reshape(2 * rows, width), 0, 0)

    def near_terms():
        for index in range(3):
            r.ff_wide[index] = side_terms(index, y)

    def far_terms(index):
        terms = (r.ff_wide[index] + side_terms(index, 1 - y)).astype(narrow)
        r.ff_terms[:, :, pl.ds(index * ff_cols, ff_cols)] = terms.reshape(depth, 2, ff_cols, width)

    ff_across = {}

    both = 2 * ff_cols

    def ff_terms_to_x(offset):
        source = r.ff_terms.at[deep(offset), 1 - x, pl.ds(0, both)]
        ff_across[offset] = mail.push(source, r.ff_near.at[offset], x_peer)

    down_copies = []

    def down_terms():
        far_terms(2)
        for offset in range(1, depth):
            source = r.ff_terms.at[deep(offset), :, pl.ds(both, ff_cols)]
            down_copies.append(mail.push(source, r.down_got.at[offset], z_peer(offset)))

    def down_step():
        summed = r.ff_terms[d, :, pl.ds(both, ff_cols)].astype(wide)
        for copy in down_copies:
            copy.wait_recv()
        for offset in range(1, depth):
            summed += r.down_got[offset].astype(wide)
        r.down_wide[...] = summed
        r.down_sums[...] = summed.astype(narrow)
        return mail.push(r.down_sums.at[1 - x], r.down_near_sum, x_peer)

    def gate_terms():
        far_terms(0)
        far_terms(1)
        for offset in range(1, depth):
            ff_terms_to_x(offset)

    near_copy, y_copy = share_rows("grad_down", grad_down_raw.astype(narrow))
    grad_mlp_in = group_sum(
        "mlp_back",
        backward_half,
        (near_copy, lambda: far_rows("grad_down", y_copy)),
        near_terms,
        down_terms,
        gate_terms,
    )
    middle = r.middle[...]
    inverse_mid = norm_rows(middle, r.norm_gains[2:3])[1]
    grad_mid_part, gain_two = norm_back(middle, inverse_mid, r.norm_gains[2:3], grad_mlp_in)
    r.gains[2:3] = jnp.sum(gain_two, axis=0, keepdims=True)
    grad_middle = r.cotangent[...].astype(wide) + grad_mid_part
    r.grad_middle[...] = grad_middle
    branch = r.branch[...]
    inverse_branch = norm_rows(branch, r.norm_gains[1:2])[1]
    grad_branch_raw, gain_one = norm_back(branch, inverse_branch, r.norm_gains[1:2], grad_middle)
    r.gains[1:2] = jnp.sum(gain_one, axis=0, keepdims=True)
    grad_branch = grad_branch_raw.astype(narrow)
    branch_c, branch_y = share_rows("branch_all", grad_branch)

    head_grad = rows_dot(grad_branch, out_weight, 1, 1).astype(narrow)
    for head in range(heads):
        r.head_grad[head] = head_grad[:, head * head_width : (head + 1) * head_width]

    ff_deep = []

    def ff_step(offset):
        ff_across[offset].wait_recv()
        summed = r.ff_terms[deep(offset), x, pl.ds(0, both)].astype(wide) + r.ff_near[offset].astype(wide)
        if offset:
            r.ff_sum[offset] = summed.astype(narrow)
            ff_deep.append(mail.push(r.ff_sum.at[offset], r.ff_got.at[offset], z_peer(offset)))
        else:
            r.ff_own[...] = summed

    for head in range(heads):
        grad_rows = r.head_grad[head]
        delta = jnp.sum(grad_rows.astype(wide) * r.exact[head], axis=1, keepdims=True)
        grad_probs = rows_dot(grad_rows, r.values[...], 1, 1)
        r.grad_scores[head] = (r.probs[head] * (grad_probs - delta)).astype(narrow)
    ff_step(1)
    all_grads = r.head_grad[...].reshape(heads * rows, head_width)
    all_queries = r.q_rot[...].reshape(heads * rows, head_width)
    kv_near = []
    for pair in range(4):
        here = slice(2 * pair * rows, 2 * (pair + 1) * rows)
        px, py = pair // 2, pair % 2
        key_part = rows_dot(
            r.grad_scores[:, :, here].reshape(heads * rows, 2 * rows), all_queries, 0, 0
        )
        value_part = rows_dot(
            r.probs_narrow[:, :, here].reshape(heads * rows, 2 * rows), all_grads, 0, 0
        )
        r.kv_terms[px, py, :, :, :head_width] = key_part.astype(narrow).reshape(2, rows, head_width)
        r.kv_terms[px, py, :, :, head_width:] = value_part.astype(narrow).reshape(2, rows, head_width)
        kv_near.append(mail.push(r.kv_terms.at[px, py, 1 - c], r.kv_near.at[px, py], c_peer))
    ff_step(2)
    branch_far = far_rows("branch_all", branch_y)

    cosine, sine_part = r.cosine[me], r.sine[me]
    gain_query = jnp.zeros((1, head_width), wide)
    for head in range(heads):
        here = slice(head * head_width, (head + 1) * head_width)
        turned = rows_dot(r.grad_scores[head], r.keys[...], 1, 0) * score_scale
        upstream = rotate(turned, cosine, -sine_part)
        query_raw = r.q_raw[:, here]
        inverse = norm_rows(query_raw, query_gain)[1]
        grad_raw, gain_rows = norm_back(query_raw, inverse, query_gain, upstream)
        gain_query += jnp.sum(gain_rows, axis=0, keepdims=True)
        r.grad_query[:, here] = grad_raw.astype(narrow)
    r.gains[4:5, :head_width] = gain_query

    for px in bits:
        for py in bits:
            kv_near[2 * px + py].wait_recv()
            summed = r.kv_terms[px, py, c].astype(wide) + r.kv_near[px, py].astype(wide)
            r.kv_sums[px, py] = summed.astype(narrow)
    kv_copies = []
    for number, (dx, dy) in enumerate(chip_steps):
        kv_copies.append(
            mail.push(
                r.kv_sums.at[flip(x, dx), flip(y, dy)], r.kv_far.at[number], plane_peer(dx, dy, 0)
            )
        )
    turned_blocks("query_turned", r.grad_query[...], query_cols)
    query_copies = send_factor("query_turned")
    ff_step(3)

    def deep_copies(name):
        return [
            mail.push(getattr(r, name + "_terms").at[deep(offset)], getattr(r, name + "_far").at[offset], z_peer(offset))
            for offset in range(1, depth)
        ]

    for copy in out_copies + [branch_c, branch_far]:
        copy.wait_recv()
    terms = jnp.zeros((2 * depth * query_cols, width), wide)
    for py in bits:
        for pc in bits:
            left = r.out_turned_got[py, pc].reshape(2 * depth * query_cols, rows)
            terms += rows_dot(left, r.branch_all[py, pc], 1, 0)
    r.out_both[...] = terms.astype(narrow).reshape(depth, 2, query_cols, width)
    out_near = mail.push(r.out_both.at[:, 1 - x], r.out_near, x_peer)
    query_part = rows_dot(r.grad_query[...], r.q_all[...].reshape(full, width), 1, 0)
    r.query_part[...] = query_part

    def weight_terms(name, copies, columns):
        for copy in copies:
            copy.wait_recv()
        terms = jnp.zeros((depth * columns, width), wide)
        for block in range(8):
            left = getattr(r, name + "_got")[block].reshape(depth * columns, rows)
            terms += rows_dot(left, r.attn_in[block], 1, 0)
        getattr(r, name + "_wide")[...] = terms.reshape(depth, columns, width)
        getattr(r, name + "_terms")[...] = terms.astype(narrow).reshape(depth, columns, width)
        return deep_copies(name)

    for offset in range(4, depth):
        ff_step(offset)
    for copy in kv_copies:
        copy.wait_recv()
    kv_sum = r.kv_sums[x, y].astype(wide)
    for number in range(len(chip_steps)):
        kv_sum += r.kv_far[number].astype(wide)
    key_gain = r.qk_gains[1:2]
    key_raw = r.key_raw[me]
    key_back = rotate(kv_sum[:, :head_width], cosine, -sine_part)
    inverse_key = norm_rows(key_raw, key_gain)[1]
    grad_key_raw, gain_key = norm_back(key_raw, inverse_key, key_gain, key_back)
    r.gains[5:6, :head_width] = jnp.sum(gain_key, axis=0, keepdims=True)
    r.grad_kv[:, :head_width] = grad_key_raw.astype(narrow)
    r.grad_kv[:, head_width:] = kv_sum[:, head_width:].astype(narrow)
    kv_turned = rows_dot(r.unsort[...], r.grad_kv[...], 1, 1).astype(narrow)
    r.kv_turned[...] = kv_turned.reshape(depth, 2, 2, 2, 2 * key_cols, rows)
    kv_factor_copies = send_factor("kv_turned")

    grad_attn_in = r.query_part[...] + rows_dot(r.grad_kv[...], r.kv_sorted[...], 1, 0)
    input_wide = r.block_in[...].astype(wide)
    inverse_in = norm_rows(input_wide, r.norm_gains[0:1])[1]
    grad_in_part, gain_zero = norm_back(input_wide, inverse_in, r.norm_gains[0:1], grad_attn_in)
    r.d_block_in[...] = (r.grad_middle[...] + grad_in_part).astype(narrow)
    r.gains[0:1] = jnp.sum(gain_zero, axis=0, keepdims=True)
    gain_copies = [
        mail.push(r.gains, r.gains_got.at[number], plane_peer(*step))
        for number, step in enumerate(plane_steps)
    ]

    query_deep = weight_terms("query_turned", query_copies, query_cols)
    down_copy = down_step()
    ff_terms_to_x(0)
    out_near.wait_recv()
    summed = r.out_both[:, x].astype(wide) + r.out_near[...].astype(wide)
    r.out_turned_wide[...] = summed
    r.out_turned_terms[...] = summed.astype(narrow)
    out_deep = deep_copies("out_turned")
    kv_deep = weight_terms("kv_turned", kv_factor_copies, 2 * key_cols)
    gain_sum = r.gains[...]
    for number, copy in enumerate(gain_copies):
        copy.wait_recv()
        gain_sum += r.gains_got[number]
    r.gains_sum[...] = gain_sum
    gain_deep = [
        mail.push(r.gains_sum, r.gains_deep.at[offset], z_peer(offset)) for offset in range(1, depth)
    ]
    ff_step(0)

    def deep_sum(own, far, copies):
        for number, copy in enumerate(copies):
            copy.wait_recv()
            own += far[number + 1].astype(wide)
        return own

    r.grad_q_rows[...] = deep_sum(r.query_turned_wide[d], r.query_turned_far, query_deep)
    r.grad_o_rows[...] = deep_sum(r.out_turned_wide[d], r.out_turned_far, out_deep)
    r.grad_ff_rows[:both] = deep_sum(r.ff_own[...], r.ff_got, ff_deep)
    down_copy.wait_recv()
    r.grad_ff_rows[both:] = r.down_wide[x] + r.down_near_sum[...].astype(wide)
    r.grad_kv_rows[...] = deep_sum(r.kv_turned_wide[d], r.kv_turned_far, kv_deep)
    r.gains_out[...] = deep_sum(r.gains_sum[...], r.gains_deep, gain_deep)
    mail.settle()


def split_kernel(block_ref, back_ref, gains_ref, q_ref, o_ref, kv_ref, ff_ref, *outs):
    key_cols, ff_cols = outs[5].shape[0], outs[8].shape[0]
    outs[0][...] = block_ref[...]
    outs[1][...] = back_ref[...]
    norm_count = outs[2].shape[0]
    outs[2][...] = gains_ref[:norm_count]
    outs[3][...] = gains_ref[norm_count : norm_count + outs[3].shape[0], : outs[3].shape[1]]
    outs[4][...] = q_ref[...]
    outs[5][...] = kv_ref[:key_cols]
    outs[6][...] = kv_ref[key_cols:]
    outs[7][...] = o_ref[...]
    for piece in range(3):
        outs[8 + piece][...] = ff_ref[piece * ff_cols : (piece + 1) * ff_cols]


def fused_local(
    block_in,
    cotangent,
    positions,
    norm_gains,
    qk_gains,
    w_query,
    w_key,
    w_value,
    w_out,
    w_gate,
    w_up,
    w_down,
):
    narrow, wide = jnp.bfloat16, jnp.float32
    rows, width = block_in.shape
    head_width = qk_gains.shape[1]
    depth = lax.axis_size("dp")
    query_cols, key_cols, ff_cols = w_query.shape[1], w_key.shape[1], w_gate.shape[1]
    full = query_cols * lax.axis_size(every_axis)
    heads = full // head_width
    plane = lax.axis_size(sequence_axes)
    length = plane * rows
    ff_width = 2 * depth * ff_cols
    operands = dict(
        block_in=block_in,
        cotangent=cotangent,
        positions=positions.reshape(-1, rows),
        norm_gains=norm_gains,
        qk_gains=qk_gains,
        q_rows=w_query.T,
        o_rows=w_out,
        key_rows=w_key.T,
        value_rows=w_value.T,
        gate_rows=w_gate.T,
        up_rows=w_up.T,
        down_rows=w_down,
    )
    results = dict(
        block_out=((rows, width), narrow),
        d_block_in=((rows, width), narrow),
        gains_out=((8, width), wide),
        grad_q_rows=((query_cols, width), wide),
        grad_o_rows=((query_cols, width), wide),
        grad_kv_rows=((2 * key_cols, width), wide),
        grad_ff_rows=((3 * ff_cols, width), wide),
    )
    cube = (depth, 2, 2, 2)
    scratch = dict(
        block_all=((2, 2, 2, rows, width), narrow),
        kv_all=(cube + (2 * key_cols, width), narrow),
        q_all=(cube + (query_cols, width), narrow),
        o_all=(cube + (query_cols, width), narrow),
        ff_all=((depth, 2, 3 * ff_cols, width), narrow),
        pos_pair=((2, plane // 2, rows), wide),
        pos_all=((plane, rows), wide),
        pos_own=((rows, 1), wide),
        cosine=((plane, rows, head_width // 2), wide),
        sine=((plane, rows, head_width // 2), wide),
        sort=((2 * head_width, 2 * head_width), narrow),
        unsort=((2 * head_width, 2 * head_width), narrow),
        attn_in=((plane, rows, width), narrow),
        kv_sorted=((2 * head_width, width), narrow),
        key_raw=((plane, rows, head_width), wide),
        keys=((length, head_width), narrow),
        values=((length, head_width), narrow),
        q_raw=((rows, full), wide),
        q_rot=((heads, rows, head_width), narrow),
        bias=((rows, length), wide),
        probs=((heads, rows, length), wide),
        probs_narrow=((heads, rows, length), narrow),
        exact=((heads, rows, head_width), wide),
        attn_out=((rows, full), narrow),
        branch=((rows, width), wide),
        middle=((rows, width), wide),
        mlp_in=((2, 2, rows, width), narrow),
        gate_pre=((2, 2 * rows, ff_width), wide),
        up_pre=((2, 2 * rows, ff_width), wide),
        hidden=((2, 2 * rows, ff_width), narrow),
        down_raw=((rows, width), wide),
        grad_down=((2, 2, rows, width), narrow),
        grad_gate=((2, 2 * rows, ff_width), narrow),
        grad_up=((2, 2 * rows, ff_width), narrow),
        grad_middle=((rows, width), wide),
        branch_all=((2, 2, rows, width), narrow),
        out_both=((depth, 2, query_cols, width), narrow),
        out_near=((depth, query_cols, width), narrow),
        ff_wide=((3, ff_width, width), wide),
        head_grad=((heads, rows, head_width), narrow),
        grad_scores=((heads, rows, length), narrow),
        grad_query=((rows, full), narrow),
        query_part=((rows, width), wide),
        grad_kv=((rows, 2 * head_width), narrow),
        kv_terms=((2, 2, 2, rows, 2 * head_width), narrow),
        kv_near=((2, 2, rows, 2 * head_width), narrow),
        kv_sums=((2, 2, rows, 2 * head_width), narrow),
        kv_far=((3, rows, 2 * head_width), narrow),
        ff_terms=((depth, 2, 3 * ff_cols, width), narrow),
        ff_near=((depth, 2 * ff_cols, width), narrow),
        ff_sum=((depth, 2 * ff_cols, width), narrow),
        ff_got=((depth, 2 * ff_cols, width), narrow),
        ff_own=((2 * ff_cols, width), wide),
        down_got=((depth, 2, ff_cols, width), narrow),
        down_wide=((2, ff_cols, width), wide),
        down_sums=((2, ff_cols, width), narrow),
        down_near_sum=((ff_cols, width), narrow),
        gains=((8, width), wide),
        gains_got=((plane - 1, 8, width), wide),
        gains_sum=((8, width), wide),
        gains_deep=((depth, 8, width), wide),
    )
    for name in ("down", "mlp_back"):
        scratch[name] = ((2, 2, rows, width), narrow)
        scratch[name + "_near"] = ((2, rows, width), narrow)
        scratch[name + "_sum"] = ((rows, width), narrow)
        scratch[name + "_far"] = ((rows, width), narrow)
    for name, columns in (("out_turned", query_cols), ("query_turned", query_cols), ("kv_turned", 2 * key_cols)):
        scratch[name] = (cube + (columns, rows), narrow)
        scratch[name + "_got"] = ((plane, depth, columns, rows), narrow)
        scratch[name + "_wide"] = ((depth, columns, width), wide)
        scratch[name + "_terms"] = ((depth, columns, width), narrow)
        scratch[name + "_far"] = ((depth, columns, width), narrow)
    scratch["out_turned_got"] = ((2, 2, depth, 2, query_cols, rows), narrow)
    names = list(operands) + list(results) + list(scratch) + ["send_sems", "recv_sems"]
    in_vmem = pl.BlockSpec(memory_space=pltpu.VMEM)
    outs = pl.pallas_call(
        lambda *refs: fused_kernel(names, *refs),
        out_shape=[jax.ShapeDtypeStruct(*result) for result in results.values()],
        in_specs=[in_vmem] * len(operands),
        out_specs=[in_vmem] * len(results),
        scratch_shapes=[pltpu.VMEM(*one) for one in scratch.values()]
        + [pltpu.SemaphoreType.DMA((copy_limit,))] * 2,
        compiler_params=pltpu.CompilerParams(
            collective_id=11, has_side_effects=True, vmem_limit_bytes=56 * 1024 * 1024
        ),
        name="layer",
    )(*operands.values())
    parts = [
        ((rows, width), narrow),
        ((rows, width), narrow),
        (norm_gains.shape, wide),
        (qk_gains.shape, wide),
        ((query_cols, width), wide),
        ((key_cols, width), wide),
        ((key_cols, width), wide),
        ((query_cols, width), wide),
        ((ff_cols, width), wide),
        ((ff_cols, width), wide),
        ((ff_cols, width), wide),
    ]
    parts = pl.pallas_call(
        split_kernel,
        out_shape=[jax.ShapeDtypeStruct(*part) for part in parts],
        in_specs=[in_vmem] * len(results),
        out_specs=[in_vmem] * len(parts),
        name="split",
    )(*outs)
    turned = (4, 5, 6, 8, 9)
    return tuple(part.T if index in turned else part for index, part in enumerate(parts))


def fits_fused(block_in, w_query, w_key, w_gate):
    tiles = (w_query.shape[1], 2 * w_key.shape[1], w_gate.shape[1])
    return (
        lax.axis_size("ctx") == 2
        and lax.axis_size("head") == 4
        and block_in.shape[0] % 128 == 0
        and all(columns % 16 == 0 for columns in tiles)
    )


def either_local(*args):
    if fits_fused(args[0], args[5], args[6], args[9]):
        return fused_local(*args)
    return local(*args)


def solution(mesh):
    in_specs = (
        P(every_axis, None),
        P(every_axis, None),
        P(weight_axes),
        P(),
        P(),
        P(None, every_axis),
        P(None, every_axis),
        P(None, every_axis),
        P(every_axis, None),
        P(None, every_axis),
        P(None, every_axis),
        P(every_axis, None),
    )
    out_specs = (
        P(every_axis, None),
        P(every_axis, None),
        P(),
        P(),
        P(None, every_axis),
        P(None, every_axis),
        P(None, every_axis),
        P(every_axis, None),
        P(None, every_axis),
        P(None, every_axis),
        P(every_axis, None),
    )
    return jax.shard_map(either_local, mesh=mesh, in_specs=in_specs, out_specs=out_specs, check_vma=False)
```
